32 devices in a mesh: groups: 2 (over y), pulse: 4 (over z), range: 2 (over x), sub: 2 (over core).
Axes of the slice: x: 2, y: 2, z: 4, core: 2. Of those that a mesh axis runs over, the one named last changes fastest.
Arguments:
- raw_echo: bfloat16 [2, 128, 16384], P(None, ('groups', 'pulse', 'sub'), 'range'), parts along dimension 1, may hold values from -6 to 6
- range_taps: bfloat16 [32, 512, 128], P('pulse'), may hold values from -0.25 to 0.25
- azim_taps: bfloat16 [128, 2048], P(('groups', 'pulse', 'sub')), parts along dimension 0, may hold values from -1 to 1
- tile_col: int32 [128, 1], P(('groups', 'pulse', 'sub')), parts along dimension 0, may hold values from 0 to 1; in each aligned block of 4 rows (0 to 3, 4 to 7, ...) at most 2 rows name the same one
Outputs:
- image: float32 [2, 8192, 4096], P(None, ('groups', 'pulse', 'range', 'sub')), parts along dimension 1
The draws below stay inside these ranges and needn't reach their ends.
There are 2 independent parts, one for each index of `groups`. The reference program is written for one: setup_inputs(seed, part) draws one part's arguments, and reference() takes and returns one part's arrays. A program takes and returns all parts, laid end to end along the dimension named above; an argument that names none is the same for every part. Nothing has to cross between parts.
Inputs may be any that keep to these rules, and one draw needn't show every extreme that they name: `tile_col`: in each aligned block of 4 pulses no tile column is named by more than 2 pulses.
All inputs are finite; a program needn't handle non-finite values.
Results may differ from the reference program's by a relative error of at most 0.008.
Values may be sent and summed in bfloat16 or wider, within the bound.
No kernel may reach another device: no remote copies, remote signals or barrier semaphores. Data moves between devices by JAX's collectives and lax.ppermute only.
A program may use at most 64 MiB of HBM per device.

```python
import math
import jax
import jax.numpy as jnp
import numpy as np
from jax import lax

S = 16384
G = 4096
KB = 128
PULSE_DEV = 4
CAP = 2
PULSES = 64
PULSE_SHARD = 8
TILE_COLS = 2
TW = 2048
RBIN = 512
N_PULSE = 4
N_RANGE = 2
N_SUB = 2


def levels(own_key, dims, pieces, smallest, largest):
    loudness, own = 1.0, jax.random.fold_in(own_key, 6)
    for dim, shards_of in pieces:
        steps = jnp.exp(jax.random.uniform(jax.random.fold_in(own, dim), (shards_of,), jnp.float32, smallest / len(pieces), largest / len(pieces)))
        loudness = loudness * jnp.repeat(steps, dims[dim] // shards_of).reshape([-1 if axis == dim else 1 for axis in range(len(dims))])
    return loudness


def deal_out(rng, own, number, rows, amount, top, most, slope):
    order = jax.random.permutation(rng, amount)
    heavy_load, common = shares(amount, rows * top, most, slope, True), shares(amount, rows * top, most, slope, False)
    places = jnp.arange(amount)

    def named(sizes, turn):
        used = int((sizes > 0).sum())
        fixed = max(1, used // 4)
        shifted = fixed + (places - fixed + turn * (used - fixed)) % max(1, amount - fixed)
        return jnp.zeros((amount,), jnp.int32).at[order[jnp.where(places < fixed, places, shifted)]].set(jnp.asarray(sizes, jnp.int32))

    sizes = jnp.where(number % 4 == 0, named(heavy_load, number // 4), named(common, number - number // 4 - 1))
    mixed = jax.random.permutation(jax.random.fold_in(own, 3), amount)
    giver, sink = mixed[0:amount // 2 * 2:2], mixed[1:amount // 2 * 2:2]
    margin = jnp.minimum(sizes[giver] - 1, most - sizes[sink]) // 2
    margin = jnp.where((giver == order[0]) | (sink == order[0]) | (sizes[sink] == 0), 0, jnp.maximum(margin, 0))
    shifted = jax.random.randint(jax.random.fold_in(own, 4), (amount // 2,), 0, 1 << 20) % (margin + 1)
    sizes = sizes.at[giver].add(-shifted).at[sink].add(shifted)
    items = jnp.searchsorted(jnp.cumsum(sizes), jnp.arange(rows * top), side="right").astype(jnp.int32)
    grid = items.reshape(top, rows).T
    grid = grid[jax.random.permutation(jax.random.fold_in(own, 1), rows)]
    turn = jax.random.randint(jax.random.fold_in(own, 2), (rows, 1), 0, top)
    return jnp.take_along_axis(grid, (jnp.arange(top)[None, :] + turn) % top, axis=1)


def shares(count, total, most, lean, full):
    loads = [(1 << 20) // math.isqrt(standing ** lean) + 1 for standing in range(1, count + 1)]
    largest = most if full else min(most, max(-(-total // count), total * loads[0] // sum(loads)))
    least = 1 if total - largest >= count - 1 else 0
    holding, spare = [largest] + [least] * (count - 1), total - largest - least * (count - 1)
    while spare > 0:
        candidates = [i for i in range(1, count) if holding[i] < largest] or [i for i in range(1, count) if holding[i] < most]
        pool, budget = sum([loads[i] for i in candidates]), spare
        for i in candidates:
            more = min(most - holding[i], max(1, budget * loads[i] // pool), spare)
            holding[i] = holding[i] + more
            spare = spare - more
    return np.array(holding)


def noise(rng, extent, spread, most, split=(), kind=jnp.bfloat16):
    drawn = jax.random.normal(rng, extent, jnp.float32) * spread
    if len(split) > 0:
        drawn = levels(rng, extent, split, -0.22, 0.18) * drawn
    return jnp.clip(drawn, min=-most, max=most).astype(kind)


def setup_inputs(seed: int = 0, part: int = 0) -> dict:
    key_list = jax.random.split(jax.random.key(seed), 5)
    part_keys = jax.random.split(jax.random.fold_in(key_list[4], part), 5)
    raw_echo = noise(part_keys[0], (2, PULSES, S), 1.0, 6.0, ((1, 8), (2, 2)))
    range_taps = noise(key_list[1], (G // KB, RBIN, KB), RBIN ** -0.5, 0.25, ((0, 4),))
    azim_taps = noise(part_keys[2], (PULSES, TW), (PULSES // TILE_COLS) ** -0.5, 1.0, ((0, 8),))
    tile_col_keys = jax.random.split(jax.random.fold_in(part_keys[3], 1), PULSES // PULSE_DEV)
    tile_col_turns = jax.random.permutation(jax.random.fold_in(part_keys[3], 3), PULSES // PULSE_DEV)
    tile_col = jax.vmap(lambda own, number: deal_out(jax.random.fold_in(part_keys[3], 2), own, number, PULSE_DEV, TILE_COLS, 1, CAP, 2))(tile_col_keys, tile_col_turns).reshape((PULSES, 1))
    return {"raw_echo": raw_echo, "range_taps": range_taps, "azim_taps": azim_taps, "tile_col": tile_col}


def reference(raw_echo, range_taps, azim_taps, tile_col):
    samples = raw_echo.astype(jnp.float32)
    transformed = jnp.fft.fft(samples[0] + 1j * samples[1], norm="ortho")
    spectrum = jnp.stack([jnp.real(transformed), jnp.imag(transformed)]).astype(jnp.bfloat16)
    blocked = spectrum.reshape(2, PULSES, G // KB, RBIN).astype(jnp.float32)
    highest = lax.Precision.HIGHEST
    ky_rows = jnp.einsum("xpbr,brj->xpbj", blocked, range_taps.astype(jnp.float32), precision=highest)
    ky_rows = ky_rows.reshape(2, PULSES, G).astype(jnp.bfloat16)
    by_half = ky_rows.reshape(2, N_PULSE, N_SUB, PULSE_SHARD, G)
    taps_half = azim_taps.reshape(N_PULSE, N_SUB, PULSE_SHARD, TW)
    cols_half = tile_col[:, 0].reshape(N_PULSE, N_SUB, PULSE_SHARD)
    most_rows = N_PULSE * N_RANGE * CAP
    kspace = jnp.zeros((2, G, G), jnp.float32)
    for half_index in range(N_SUB):
        half_lines = by_half[:, :, half_index].reshape(2, N_PULSE * PULSE_SHARD, G)
        half_taps = taps_half[:, half_index].reshape(N_PULSE * PULSE_SHARD, TW)
        half_cols = cols_half[:, half_index].reshape(N_PULSE * PULSE_SHARD)

        def one_tile(column):
            ranked = jnp.argsort(jnp.where(half_cols == column, 0, 1), stable=True)[:most_rows]
            chosen_lines = half_lines[:, ranked].astype(jnp.float32)
            inside = half_cols[ranked] == column
            chosen_taps = jnp.where(inside[:, None], half_taps[ranked].astype(jnp.float32), jnp.zeros((), jnp.float32))
            return jnp.einsum("xpj,pi->xji", chosen_lines, chosen_taps, precision=highest)

        tiles = lax.map(one_tile, jnp.arange(N_RANGE, dtype=jnp.int32))
        partial_value = jnp.transpose(tiles, (1, 2, 0, 3)).reshape(2, G, G)
        rounded = lax.optimization_barrier(partial_value.astype(jnp.bfloat16))
        kspace = kspace + rounded.astype(jnp.float32)
    pictured = jnp.fft.ifft2(kspace[0] + 1j * kspace[1], norm="ortho")
    return jnp.stack([jnp.real(pictured), jnp.imag(pictured)]).astype(jnp.float32)
```

```python
import functools
import math

import jax
import jax.numpy as jnp
import numpy as np
from jax import lax
from jax.experimental import pallas as pl
from jax.experimental.pallas import tpu as pltpu
from jax.sharding import PartitionSpec as P

LANES = 128
F32 = jnp.float32
BF16 = jnp.bfloat16
VMEM = pl.BlockSpec(memory_space=pltpu.VMEM)
NT = (((1,), (1,)), ((), ()))
NN = (((1,), (0,)), ((), ()))


def dot(a, b, dims=NN):
    return lax.dot_general(a, b, dims, preferred_element_type=F32)


def traded(block, axis, k):
    count = lax.axis_size(axis)
    return lax.ppermute(block, axis, [(i, i ^ k) for i in range(count)])


def phasor(rows, cols, period, sign):
    turns = np.outer(rows, cols) % period
    angles = turns * (2.0 * math.pi / period)
    return np.cos(angles), sign * np.sin(angles)


def fourier(values, sign):
    count = len(values)
    if count == 1:
        return values
    even = fourier(values[0::2], sign)
    odd = fourier(values[1::2], sign)
    out = [None] * count
    for k in range(count // 2):
        er, ei = even[k]
        a, b = odd[k]
        angle = sign * 2.0 * math.pi * k / count
        if 4 * k == count:
            tr, ti = (-b, a) if sign > 0 else (b, -a)
        elif k == 0:
            tr, ti = a, b
        elif 8 * k == count:
            h = math.sqrt(0.5)
            tr, ti = ((a - b) * h, (a + b) * h) if sign > 0 else ((a + b) * h, (b - a) * h)
        elif 8 * k == 3 * count:
            h = math.sqrt(0.5)
            tr, ti = (-(a + b) * h, (a - b) * h) if sign > 0 else ((b - a) * h, -(a + b) * h)
        else:
            c, s = math.cos(angle), math.sin(angle)
            tr, ti = a * c - b * s, a * s + b * c
        out[k] = (er + tr, ei + ti)
        out[k + count // 2] = (er - tr, ei - ti)
    return out


def pulse_kernel(n_parts, n_z, per, spare, *refs):
    parts = refs[:n_parts]
    first, turn, second = refs[n_parts : n_parts + 3]
    outs = refs[n_parts + 3 : n_parts + 3 + n_z]
    lines = refs[n_parts + 3 + n_z]
    my_x = lax.axis_index("range")
    my_z = lax.axis_index("pulse")
    tiles = parts[0].shape[2] // LANES
    total = tiles * n_parts
    for k in range(n_parts):
        base = (my_x ^ k) * (tiles * spare)
        for c in range(2):
            for t in range(tiles):
                row = pl.multiple_of(base + t * spare, spare)
                lines[c, pl.ds(row, per), :] = parts[k][c, :, t * LANES : (t + 1) * LANES].astype(F32)
    data = jnp.concatenate(
        [
            jnp.concatenate(
                [lines[c, pl.ds(p, total, stride=spare), :].astype(BF16) for p in range(per)], axis=1
            )
            for c in range(2)
        ],
        axis=0,
    )
    mixed = dot(first[...], data)
    half = mixed.shape[0] // 2
    band = half // n_z
    picks = []
    for k in range(n_z):
        for c in range(2):
            row = pl.multiple_of(c * LANES + (my_z ^ k) * band, band)
            picks.append(second[pl.ds(row, band), :])
    table = jnp.concatenate(picks, axis=0)
    tc, ts = turn[0], turn[1]
    for p in range(per):
        re = mixed[:half, p * LANES : (p + 1) * LANES]
        im = mixed[half:, p * LANES : (p + 1) * LANES]
        spun = jnp.concatenate([re * tc - im * ts, re * ts + im * tc], axis=1).astype(BF16)
        done = dot(table, spun, NT).astype(BF16)
        for k in range(n_z):
            outs[k][:, p * LANES : (p + 1) * LANES] = done[2 * band * k : 2 * band * (k + 1), :]


def line_kernel(n_z, per, blocks, quads, total_blocks, n_dest, *refs):
    chunks = refs[:n_z]
    taps, turn, last, out = refs[n_z : n_z + 4]
    bins, sums, rows = refs[n_z + 4 :]
    my_z = lax.axis_index("pulse")
    band = blocks * quads
    pulses = n_z * per
    for k in range(n_z):
        for c in range(2):
            for p in range(per):
                at = pl.multiple_of(((c * n_z + (my_z ^ k)) * per + p) * band, band)
                bins[pl.ds(at, band), :] = chunks[k][
                    c * band : (c + 1) * band, p * LANES : (p + 1) * LANES
                ].astype(F32)
    ky = []
    for b in range(blocks):
        lhs = jnp.concatenate(
            [bins[pl.ds(b * quads + q, 2 * pulses, stride=band), :].astype(BF16) for q in range(quads)],
            axis=1,
        )
        line = dot(lhs, taps[b])
        ky.append((line[:pulses], line[pulses:]))
    quarter = total_blocks // 4
    for y in range(quarter):
        classes = []
        for m in range(4):
            acc = None
            for b in range(m, blocks, 4):
                re, im = ky[b]
                angle = 2.0 * math.pi * (b * y % total_blocks) / total_blocks
                co, si = math.cos(angle), math.sin(angle)
                if b * y == 0:
                    term = (re, im)
                else:
                    term = (re * co - im * si, re * si + im * co)
                acc = term if acc is None else (acc[0] + term[0], acc[1] + term[1])
            if acc is None:
                acc = (jnp.zeros_like(ky[0][0]), jnp.zeros_like(ky[0][1]))
            classes.append(acc)
        for r, (re, im) in enumerate(fourier(classes, 1)):
            at = (y + r * quarter) * pulses
            sums[0, at : at + pulses, :] = re
            sums[1, at : at + pulses, :] = im
    fold = LANES // total_blocks
    tops = last.shape[0] // 2
    for m in range(pulses):
        gr = sums[0, pl.ds(m, total_blocks, stride=pulses), :]
        gi = sums[1, pl.ds(m, total_blocks, stride=pulses), :]
        spun = []
        for f in range(fold):
            tc = turn[0, f * total_blocks : (f + 1) * total_blocks, :]
            ts = turn[1, f * total_blocks : (f + 1) * total_blocks, :]
            spun.append(
                jnp.concatenate([gr * tc - gi * ts, gr * ts + gi * tc], axis=1).astype(BF16)
            )
        done = dot(last[...], jnp.concatenate(spun, axis=0), NT)
        for c in range(2):
            at = (c * pulses + m) * tops
            rows[at : at + tops, :] = done[c * tops : (c + 1) * tops, :]
    share = tops // n_dest
    for d in range(n_dest):
        for s in range(share):
            out[d, :, s * LANES : (s + 1) * LANES] = rows[
                pl.ds(d * share + s, 2 * pulses, stride=tops), :
            ].astype(BF16)


def column_kernel(width, tile_cols, low, taps, table, turn, out, flipped, mixed):
    pulses = taps.shape[0]
    for t in range(taps.shape[1] // LANES):
        block = taps[:, t * LANES : (t + 1) * LANES].astype(F32)
        flipped[t * LANES : (t + 1) * LANES, :] = block.T
    tile = flipped[width : width + 1, :]
    highs = width // low
    high = table.shape[0] // 2
    for r in range(low):
        part = flipped[pl.ds(r, highs, stride=low), :]
        placed = [jnp.where(tile == float(s), part, 0.0) for s in range(tile_cols)]
        rhs = jnp.concatenate(placed, axis=0).astype(BF16)
        mixed[r] = dot(table[...], rhs)
    step = 16

    def rows(i, carry):
        y = pl.multiple_of(i * step, step)
        values = []
        tc = turn[0, pl.ds(y, step), :]
        ts = turn[1, pl.ds(y, step), :]
        for r in range(low):
            re = mixed[r, pl.ds(y, step), :]
            im = mixed[r, pl.ds(y + high, step), :]
            if r == 0:
                values.append((re, im))
                continue
            c, s = tc[:, r : r + 1], ts[:, r : r + 1]
            values.append((re * c - im * s, re * s + im * c))
        for d, (re, im) in enumerate(fourier(values, 1)):
            at = pl.multiple_of(d * high + y, step)
            out[pl.ds(at, step), :] = jnp.concatenate([re, im], axis=1).astype(BF16)
        return carry

    lax.fori_loop(0, high // step, rows, 0)


def factor(parts, n_z, n_x, n_c, per):
    pulses = n_z * per
    summed = {}
    for x in range(n_x):
        for c in range(n_c):
            acc = None
            for z in range(n_z):
                part = parts((z * n_x + x) * n_c + c)
                acc = part if acc is None else acc + part
            summed[x, c] = acc
    out = []
    for comp in range(2):
        for c in range(n_c):
            for z in range(n_z):
                for x in range(n_x):
                    at = comp * pulses + z * per
                    out.append(summed[x, c][at : at + per, :])
    return jnp.concatenate(out, axis=0)


def image_kernel(dims, recv, cols, out, lhs):
    n_z, n_x, n_c, per = dims

    @pl.when(pl.program_id(0) == 0)
    def _():
        lines = factor(lambda s: recv[s].astype(F32), n_z, n_x, n_c, per).T
        half = lines.shape[1] // 2
        re, im = lines[:, :half], lines[:, half:]
        rows = lines.shape[0]
        lhs[:rows, :] = jnp.concatenate([re, -im], axis=1).astype(BF16)
        lhs[rows:, :] = jnp.concatenate([im, re], axis=1).astype(BF16)

    rows = out.shape[1]
    done = dot(lhs[...], cols[...], NT)
    out[0] = done[:rows]
    out[1] = done[rows:]


def image_plain(lhs, cols, out):
    rows = out.shape[1]
    done = dot(lhs[...], cols[...], NT)
    out[0] = done[:rows]
    out[1] = done[rows:]


def table_of(values, dtype=BF16):
    return jnp.asarray(np.asarray(values, np.float32), dtype)


def complex_left(c, s, scale=1.0):
    return np.block([[c, -s], [s, c]]) * scale


def body(raw_echo, range_taps, azim_taps, tile_col):
    n_x, n_z, n_c = lax.axis_size("range"), lax.axis_size("pulse"), lax.axis_size("sub")
    my_x, my_z, my_c = lax.axis_index("range"), lax.axis_index("pulse"), lax.axis_index("sub")
    shard, part = raw_echo.shape[1:]
    per = shard // n_x
    samples = part * n_x
    blocks, block_bins, block_rows = range_taps.shape
    total_blocks = blocks * n_z
    grid = total_blocks * block_rows
    width = azim_taps.shape[1]
    tile_cols = grid // width
    n_dest = n_z * n_x * n_c
    out_rows = grid // n_dest
    pulses = n_z * per

    def mine(x):
        return lax.dynamic_slice_in_dim(raw_echo, x * per, per, 1)

    parts = [mine(my_x)] + [traded(mine(my_x ^ k), "range", k) for k in range(1, n_x)]

    marked = jnp.concatenate(
        [azim_taps, jnp.broadcast_to(tile_col.astype(BF16), (shard, LANES))], axis=1
    )
    along = jnp.zeros((n_z * shard, width + LANES), BF16)
    for k in range(n_z):
        got = marked if k == 0 else traded(marked, "pulse", k)
        along = lax.dynamic_update_slice_in_dim(along, got, (my_z ^ k) * shard, 0)
    everyone = jnp.zeros((n_c * n_z * shard, width + LANES), BF16)
    for k in range(n_c):
        got = along if k == 0 else traded(along, "sub", k)
        everyone = lax.dynamic_update_slice_in_dim(everyone, got, (my_c ^ k) * n_z * shard, 0)

    high = samples // LANES
    n128 = np.arange(LANES)
    nh = np.arange(high)
    first = table_of(complex_left(*phasor(nh, nh, high, -1.0)))
    turn1 = table_of(np.stack(phasor(nh, n128, samples, -1.0)), F32)
    second = table_of(complex_left(*phasor(n128, n128, LANES, -1.0), 1.0 / math.sqrt(samples)))
    band = LANES // n_z
    spare = 8
    chunk = jax.ShapeDtypeStruct((2 * band, per * high), BF16)
    chunks = pl.pallas_call(
        functools.partial(pulse_kernel, n_x, n_z, per, spare),
        in_specs=[VMEM] * (n_x + 3),
        out_specs=[VMEM] * n_z,
        out_shape=[chunk] * n_z,
        scratch_shapes=[pltpu.VMEM((2, high * spare, LANES), F32)],
        name="pulse_transform",
    )(*parts, first, turn1, second)
    chunks = [chunks[0]] + [traded(chunks[k], "pulse", k) for k in range(1, n_z)]

    quads = block_bins // LANES
    tops = grid // LANES
    shift = grid // n_z
    turn2 = np.stack(
        [np.stack(phasor(n128, n128 + shift * z, grid, 1.0)) for z in range(n_z)]
    )
    turn2 = lax.dynamic_index_in_dim(table_of(turn2, F32), my_z, 0, keepdims=False)
    c, s = phasor(np.arange(tops), n128, tops, 1.0)
    last = table_of(complex_left(c, s, 1.0 / math.sqrt(grid)))
    wide = out_rows % LANES == 0
    n_cut = n_dest if wide else n_z
    lines = pl.pallas_call(
        functools.partial(line_kernel, n_z, per, blocks, quads, total_blocks, n_cut),
        in_specs=[VMEM] * (n_z + 3),
        out_specs=VMEM,
        out_shape=jax.ShapeDtypeStruct((n_cut, 2 * pulses, grid // n_cut), BF16),
        scratch_shapes=[
            pltpu.VMEM((2 * pulses * blocks * quads, LANES), F32),
            pltpu.VMEM((2, total_blocks * pulses, LANES), F32),
            pltpu.VMEM((2 * pulses * tops, LANES), F32),
        ],
        name="line_transform",
    )(*chunks, range_taps, turn2, last)
    if not wide:
        lines = lines.reshape(n_z, 2 * pulses, n_x * n_c, out_rows).transpose(0, 2, 1, 3)
        lines = lines.reshape(n_dest, 2 * pulses, out_rows)
    recv = lax.all_to_all(lines, ("pulse", "range", "sub"), 0, 0, tiled=True)

    low = 16
    tall = grid // low
    nt = np.arange(tall)
    c, s = phasor(nt, nt, tall, 1.0)
    table = table_of(np.concatenate([c, s], axis=0) / math.sqrt(grid))
    turn3 = table_of(np.stack(phasor(nt, np.arange(low), grid, 1.0)), F32)
    group = 64
    all_pulses = n_c * n_z * shard
    cuts = all_pulses // group
    cols = pl.pallas_call(
        functools.partial(column_kernel, width, tile_cols, low),
        grid=(cuts,),
        in_specs=[
            pl.BlockSpec((group, width + LANES), lambda i: (i, 0)),
            pl.BlockSpec((2 * tall, tall), lambda i: (0, 0)),
            pl.BlockSpec((2, tall, low), lambda i: (0, 0, 0)),
        ],
        out_specs=pl.BlockSpec((grid, 2 * group), lambda i: (0, i)),
        out_shape=jax.ShapeDtypeStruct((grid, 2 * all_pulses), BF16),
        scratch_shapes=[
            pltpu.VMEM((width + LANES, group), F32),
            pltpu.VMEM((low, 2 * tall, group), F32),
        ],
        name="column_transform",
    )(everyone, table, turn3)

    wide_x = 512
    depth = 2 * all_pulses
    col_spec = pl.BlockSpec((wide_x, depth), lambda i: (i, 0))
    out_spec = pl.BlockSpec((2, out_rows, wide_x), lambda i: (0, 0, i))
    out_shape = jax.ShapeDtypeStruct((2, out_rows, grid), F32)
    if cuts == 1 and wide:
        return pl.pallas_call(
            functools.partial(image_kernel, (n_z, n_x, n_c, per)),
            grid=(grid // wide_x,),
            in_specs=[pl.BlockSpec(recv.shape, lambda i: (0, 0, 0)), col_spec],
            out_specs=out_spec,
            out_shape=out_shape,
            scratch_shapes=[pltpu.VMEM((2 * out_rows, depth), BF16)],
            name="image",
        )(recv, cols)
    lines = factor(lambda i: recv[i].astype(F32), n_z, n_x, n_c, per).T
    re = lines[:, :all_pulses].reshape(out_rows, cuts, 1, group)
    im = lines[:, all_pulses:].reshape(out_rows, cuts, 1, group)
    lhs = jnp.stack(
        [jnp.concatenate([re, -im], axis=2), jnp.concatenate([im, re], axis=2)]
    ).reshape(2 * out_rows, depth).astype(BF16)
    return pl.pallas_call(
        image_plain,
        grid=(grid // wide_x,),
        in_specs=[pl.BlockSpec(lhs.shape, lambda i: (0, 0)), col_spec],
        out_specs=out_spec,
        out_shape=out_shape,
        name="image",
    )(lhs, cols)


def solution(mesh):
    placed = (
        P(None, ("groups", "pulse", "sub"), "range"),
        P("pulse", None, None),
        P(("groups", "pulse", "sub"), None),
        P(("groups", "pulse", "sub"), None),
    )
    return jax.shard_map(
        body,
        mesh=mesh,
        in_specs=placed,
        out_specs=P(None, ("groups", "pulse", "range", "sub"), None),
        check_vma=False,
    )
```

```python
import functools
import math

import jax
import jax.numpy as jnp
import numpy as np
from jax import lax
from jax.experimental import pallas as pl
from jax.experimental.pallas import tpu as pltpu
from jax.sharding import PartitionSpec as P


LANES = 128
F32 = jnp.float32
BF16 = jnp.bfloat16
VMEM = pl.BlockSpec(memory_space=pltpu.VMEM)
HELD = pl.BlockSpec(memory_space=pltpu.HBM)
NT = (((1,), (1,)), ((), ()))
NN = (((1,), (0,)), ((), ()))


def dot(a, b, dims=NN):
    return lax.dot_general(a, b, dims, preferred_element_type=F32)


def traded(block, axis, k):
    count = math.prod(lax.axis_size(a) for a in ((axis,) if isinstance(axis, str) else axis))
    return lax.ppermute(block, axis, [(i, i ^ k) for i in range(count)])


def near(*values):
    return [pltpu.with_memory_space_constraint(v, pltpu.VMEM) for v in values]


def far(*values):
    return [pltpu.with_memory_space_constraint(v, pltpu.HBM) for v in values]


def phasor(rows, cols, period, sign):
    turns = np.outer(rows, cols) % period
    angles = turns * (2.0 * math.pi / period)
    return np.cos(angles), sign * np.sin(angles)


def fourier(values, sign):
    count = len(values)
    if count == 1:
        return values
    even = fourier(values[0::2], sign)
    odd = fourier(values[1::2], sign)
    out = [None] * count
    for k in range(count // 2):
        er, ei = even[k]
        a, b = odd[k]
        angle = sign * 2.0 * math.pi * k / count
        if 4 * k == count:
            tr, ti = (-b, a) if sign > 0 else (b, -a)
        elif k == 0:
            tr, ti = a, b
        elif 8 * k == count:
            h = math.sqrt(0.5)
            tr, ti = ((a - b) * h, (a + b) * h) if sign > 0 else ((a + b) * h, (b - a) * h)
        elif 8 * k == 3 * count:
            h = math.sqrt(0.5)
            tr, ti = (-(a + b) * h, (a - b) * h) if sign > 0 else ((b - a) * h, -(a + b) * h)
        else:
            c, s = math.cos(angle), math.sin(angle)
            tr, ti = a * c - b * s, a * s + b * c
        out[k] = (er + tr, ei + ti)
        out[k + count // 2] = (er - tr, ei - ti)
    return out


def split_kernel(n_x, per, raw, taps, tile, *refs):
    outs = refs[:n_x]
    marked, held, lines, sent = refs[n_x:]
    my_x = lax.axis_index("range")
    copies = [pltpu.make_async_copy(raw.at[c], held.at[c], sent.at[c]) for c in range(2)]
    for copy in copies:
        copy.start()
    shard = raw.shape[1]
    tiles = raw.shape[2] // LANES
    width = taps.shape[1]
    row = lax.broadcasted_iota(jnp.int32, (per, LANES), 0)
    for k in range(n_x):
        rows = slice(k * per, (k + 1) * per)
        values = taps[:per, :].astype(F32)
        for x in range(1, n_x):
            pick = taps[x * per : (x + 1) * per, :].astype(F32)
            values = jnp.where((my_x ^ k) == x, pick, values)
        ids = jnp.zeros((per, LANES), jnp.int32)
        for p in range(per):
            ids = jnp.where(row == p, tile[0, (my_x ^ k) * per + p], ids)
        marked[rows, :width] = values.astype(BF16)
        marked[rows, width:] = ids.astype(F32).astype(BF16)
    for c in range(2):
        copies[c].wait()
        for t in range(tiles):
            lines[c, t * shard : (t + 1) * shard, :] = held[
                c, :, t * LANES : (t + 1) * LANES
            ].astype(F32)
        for k in range(n_x):
            for p in range(per):
                outs[k][c * tiles : (c + 1) * tiles, p * LANES : (p + 1) * LANES] = lines[
                    c, pl.ds((my_x ^ k) * per + p, tiles, stride=shard), :
                ].astype(BF16)


def ready_kernel(n_fixed, own, first, turn, *refs):
    fixed = refs[:n_fixed]
    part, rest, turned = refs[n_fixed : n_fixed + 3]
    brought = refs[n_fixed + 3 : 2 * n_fixed + 3]
    mine, sent = refs[2 * n_fixed + 3 :]
    my_x = lax.axis_index("range")
    copies = [
        pltpu.make_async_copy(first.at[my_x, 0], mine, sent.at[0]),
        pltpu.make_async_copy(first.at[my_x, pl.ds(1, rest.shape[0])], rest, sent.at[1]),
        pltpu.make_async_copy(turn.at[lax.axis_index("pulse")], turned, sent.at[2]),
    ]
    for i in range(n_fixed):
        copies.append(pltpu.make_async_copy(fixed[i], brought[i], sent.at[i + 3]))
    for copy in copies:
        copy.start()
    copies[0].wait()
    part[...] = dot(mine[...], own[...])
    for copy in copies[1:]:
        copy.wait()


def pulse_kernel(n_parts, n_z, per, *refs):
    parts = refs[: n_parts - 1]
    mixed, first, turn, second = refs[n_parts - 1 : n_parts + 3]
    outs = refs[n_parts + 3 :]
    my_z = lax.axis_index("pulse")
    mixed = mixed[...]
    for k, part in enumerate(parts):
        mixed = mixed + dot(first[k], part[...])
    half = mixed.shape[0] // 2
    band = LANES // n_z
    picks = []
    for k in range(n_z):
        for c in range(2):
            row = pl.multiple_of(c * LANES + (my_z ^ k) * band, band)
            picks.append(second[pl.ds(row, band), :])
    table = jnp.concatenate(picks, axis=0)
    tc, ts = turn[0], turn[1]
    for p in range(per):
        re = mixed[:half, p * LANES : (p + 1) * LANES]
        im = mixed[half:, p * LANES : (p + 1) * LANES]
        spun = jnp.concatenate([re * tc - im * ts, re * ts + im * tc], axis=1).astype(BF16)
        done = dot(table, spun, NT).astype(BF16)
        for k in range(n_z):
            outs[k][:, p * half : (p + 1) * half] = done[2 * band * k : 2 * band * (k + 1), :]


def line_kernel(n_z, per, blocks, quads, total_blocks, *refs):
    chunks = refs[:n_z]
    taps, turn, last = refs[n_z : n_z + 3]
    outs = refs[n_z + 3 : 2 * n_z + 3]
    bins, sums, rows = refs[2 * n_z + 3 :]
    my_z = lax.axis_index("pulse")
    band = blocks * quads
    pulses = n_z * per
    for k in range(n_z):
        for c in range(2):
            for p in range(per):
                at = ((c * n_z + k) * per + p) * band
                bins[at : at + band, :] = chunks[k][
                    c * band : (c + 1) * band, p * LANES : (p + 1) * LANES
                ].astype(F32)
    ky = []
    for b in range(blocks):
        lhs = jnp.concatenate(
            [bins[pl.ds(b * quads + q, 2 * pulses, stride=band), :].astype(BF16) for q in range(quads)],
            axis=1,
        )
        line = dot(lhs, taps[b])
        ky.append((line[:pulses], line[pulses:]))
    quarter = total_blocks // 4
    for y in range(quarter):
        classes = []
        for m in range(4):
            acc = None
            for b in range(m, blocks, 4):
                re, im = ky[b]
                angle = 2.0 * math.pi * (b * y % total_blocks) / total_blocks
                co, si = math.cos(angle), math.sin(angle)
                if b * y == 0:
                    term = (re, im)
                else:
                    term = (re * co - im * si, re * si + im * co)
                acc = term if acc is None else (acc[0] + term[0], acc[1] + term[1])
            if acc is None:
                acc = (jnp.zeros_like(ky[0][0]), jnp.zeros_like(ky[0][1]))
            classes.append(acc)
        for r, (re, im) in enumerate(fourier(classes, 1)):
            at = (y + r * quarter) * pulses
            sums[0, at : at + pulses, :] = re
            sums[1, at : at + pulses, :] = im
    fold = LANES // total_blocks
    tops = last.shape[0] // 2
    for m in range(pulses):
        gr = sums[0, pl.ds(m, total_blocks, stride=pulses), :]
        gi = sums[1, pl.ds(m, total_blocks, stride=pulses), :]
        spun = []
        for f in range(fold):
            tc = turn[0, f * total_blocks : (f + 1) * total_blocks, :]
            ts = turn[1, f * total_blocks : (f + 1) * total_blocks, :]
            spun.append(
                jnp.concatenate([gr * tc - gi * ts, gr * ts + gi * tc], axis=1).astype(BF16)
            )
        done = dot(last[...], jnp.concatenate(spun, axis=0), NT)
        for c in range(2):
            at = (c * pulses + m) * tops
            rows[at : at + tops, :] = done[c * tops : (c + 1) * tops, :]
    share = tops // n_z
    for k in range(n_z):
        for s in range(share):
            line = rows[pl.ds((my_z ^ k) * share + s, 2 * pulses, stride=tops), :]
            blocks_of = [
                line[c * pulses + (z ^ k) * per : c * pulses + (z ^ k) * per + per]
                for c in range(2)
                for z in range(n_z)
            ]
            outs[k][:, s * LANES : (s + 1) * LANES] = jnp.concatenate(blocks_of, axis=0).astype(BF16)


def fold_kernel(n_z, n_c, *refs):
    parts, outs, total = refs[:n_z], refs[n_z:-1], refs[-1]
    acc = parts[0][...].astype(F32)
    for part in parts[1:]:
        acc = acc + part[...].astype(F32)
    total[...] = acc.astype(BF16)
    mine = lax.axis_index("range") * n_c + lax.axis_index("sub")
    wide = outs[0].shape[1]
    for k, out in enumerate(outs):
        out[...] = total[:, pl.ds(pl.multiple_of((mine ^ k) * wide, wide), wide)]


def column_kernel(width, tile_cols, low, taps, table, turn, out, flipped, mixed):
    for t in range(taps.shape[1] // LANES):
        block = taps[:, t * LANES : (t + 1) * LANES].astype(F32)
        flipped[t * LANES : (t + 1) * LANES, :] = block.T
    tile = flipped[width : width + 1, :]
    highs = width // low
    high = table.shape[0] // 2
    for r in range(low):
        part = flipped[pl.ds(r, highs, stride=low), :]
        placed = [jnp.where(tile == float(s), part, 0.0) for s in range(tile_cols)]
        rhs = jnp.concatenate(placed, axis=0).astype(BF16)
        mixed[r] = dot(table[...], rhs)
    step = 16

    def rows(i, carry):
        y = pl.multiple_of(i * step, step)
        values = []
        tc = turn[0, pl.ds(y, step), :]
        ts = turn[1, pl.ds(y, step), :]
        for r in range(low):
            re = mixed[r, pl.ds(y, step), :]
            im = mixed[r, pl.ds(y + high, step), :]
            if r == 0:
                values.append((re, im))
                continue
            c, s = tc[:, r : r + 1], ts[:, r : r + 1]
            values.append((re * c - im * s, re * s + im * c))
        for d, (re, im) in enumerate(fourier(values, 1)):
            at = pl.multiple_of(d * high + y, step)
            out[pl.ds(at, step), :] = jnp.concatenate([re, im], axis=1).astype(BF16)
        return carry

    lax.fori_loop(0, high // step, rows, 0)


def factor(parts, n_z, n_x, n_c, per):
    pulses = n_z * per
    out = []
    for comp in range(2):
        for c in range(n_c):
            for z in range(n_z):
                for x in range(n_x):
                    at = comp * pulses + z * per
                    out.append(parts[x * n_c + c][at : at + per, :])
    return jnp.concatenate(out, axis=0)


def image_kernel(dims, step, *refs):
    n_z, n_x, n_c, per = dims
    count = n_x * n_c
    parts = [ref[...].astype(F32) for ref in refs[:count]]
    cols, out, held, sent = refs[count:]
    lines = factor(parts, n_z, n_x, n_c, per).T
    half = lines.shape[1] // 2
    re, im = lines[:, :half], lines[:, half:]
    rows = lines.shape[0]
    lhs = jnp.concatenate(
        [jnp.concatenate([re, -im], axis=1), jnp.concatenate([im, re], axis=1)], axis=0
    ).astype(BF16)
    copies = []
    for i in range(cols.shape[0] // step):
        done = dot(lhs, cols[i * step : (i + 1) * step, :], NT)
        at = pl.ds(i * step, step)
        held[0, :, at] = done[:rows]
        held[1, :, at] = done[rows:]
        copies.append(pltpu.make_async_copy(held.at[:, :, at], out.at[:, :, at], sent.at[i]))
        copies[-1].start()
    for copy in copies:
        copy.wait()


def image_plain(lhs, cols, out):
    rows = out.shape[1]
    done = dot(lhs[...], cols[...], NT)
    out[0] = done[:rows]
    out[1] = done[rows:]


def table_of(values, dtype=BF16):
    return jnp.asarray(np.asarray(values, np.float32), dtype)


def complex_left(c, s, scale=1.0):
    return np.block([[c, -s], [s, c]]) * scale


def program(raw_echo, range_taps, azim_taps, tile_col):
    n_x, n_z, n_c = lax.axis_size("range"), lax.axis_size("pulse"), lax.axis_size("sub")
    my_x, my_c = lax.axis_index("range"), lax.axis_index("sub")
    shard, part = raw_echo.shape[1:]
    per = shard // n_x
    samples = part * n_x
    blocks, block_bins, block_rows = range_taps.shape
    total_blocks = blocks * n_z
    grid = total_blocks * block_rows
    width = azim_taps.shape[1]
    tile_cols = grid // width
    quad = n_x * n_c
    out_rows = grid // (n_z * quad)
    pulses = n_z * per
    wide = out_rows % LANES == 0
    room = {}
    if wide:
        room = {"compiler_params": pltpu.CompilerParams(vmem_limit_bytes=24 << 20)}

    high = samples // LANES
    tiles = high // n_x
    n128 = np.arange(LANES)
    nh = np.arange(high)
    first = complex_left(*phasor(nh, nh, high, -1.0)).reshape(2 * high, 2, n_x, tiles)
    first = [first[:, :, [x ^ k for k in range(n_x)]].transpose(2, 0, 1, 3) for x in range(n_x)]
    first = table_of(np.stack(first).reshape(n_x, n_x, 2 * high, 2 * tiles))
    turn1 = table_of(np.stack(phasor(nh, n128, samples, -1.0)), F32)
    second = table_of(complex_left(*phasor(n128, n128, LANES, -1.0), 1.0 / math.sqrt(samples)))
    tops = grid // LANES
    shift = grid // n_z
    turn2 = np.stack([np.stack(phasor(n128, n128 + shift * z, grid, 1.0)) for z in range(n_z)])
    turn2 = table_of(turn2, F32)
    c, s = phasor(np.arange(tops), n128, tops, 1.0)
    last = table_of(complex_left(c, s, 1.0 / math.sqrt(grid)))
    low = 16
    tall = grid // low
    nt = np.arange(tall)
    c, s = phasor(nt, nt, tall, 1.0)
    table = table_of(np.concatenate([c, s], axis=0) / math.sqrt(grid))
    turn3 = table_of(np.stack(phasor(nt, np.arange(low), grid, 1.0)), F32)

    piece = pltpu.VMEM((2 * tiles, per * LANES), BF16)
    *pieces, marked = pl.pallas_call(
        functools.partial(split_kernel, n_x, per),
        in_specs=[HELD, VMEM, pl.BlockSpec(memory_space=pltpu.SMEM)],
        out_specs=[VMEM] * (n_x + 1),
        out_shape=[piece] * n_x + [pltpu.VMEM((shard, width + LANES), BF16)],
        scratch_shapes=[
            pltpu.VMEM(raw_echo.shape, BF16),
            pltpu.VMEM((2, tiles * shard, LANES), F32),
            pltpu.SemaphoreType.DMA((2,)),
        ],
        name="split",
        **room,
    )(*far(raw_echo, azim_taps), tile_col.T)
    parts = []
    for k in range(1, n_x):
        parts.append(traded(pieces[k], "range", k))

    everyone = marked
    for axis, count in (("pulse", n_z), ("sub", n_c)):
        k = 1
        while k < count:
            everyone = jnp.concatenate([everyone, traded(everyone, axis, k)], axis=0)
            k *= 2

    fixed = (turn1, second, last, range_taps, table, turn3)
    part1, rest, turn2, *brought = pl.pallas_call(
        functools.partial(ready_kernel, len(fixed)),
        in_specs=[VMEM] + [HELD] * (2 + len(fixed)),
        out_specs=[VMEM] * (3 + len(fixed)),
        out_shape=[
            pltpu.VMEM((2 * high, per * LANES), F32),
            pltpu.VMEM((max(n_x - 1, 1), 2 * high, 2 * tiles), BF16),
            pltpu.VMEM(turn2.shape[1:], F32),
        ]
        + [pltpu.VMEM(f.shape, f.dtype) for f in fixed],
        scratch_shapes=[
            pltpu.VMEM((2 * high, 2 * tiles), BF16),
            pltpu.SemaphoreType.DMA((3 + len(fixed),)),
        ],
        name="ready",
        **room,
    )(*near(pieces[0]), *far(first, turn2, *fixed))
    turn1, second, last, range_taps, table, turn3 = brought

    band = LANES // n_z
    chunk = pltpu.VMEM((2 * band, per * high), BF16)
    chunks = pl.pallas_call(
        functools.partial(pulse_kernel, n_x, n_z, per),
        in_specs=[VMEM] * (n_x + 3),
        out_specs=[VMEM] * n_z,
        out_shape=[chunk] * n_z,
        name="pulse_transform",
        **room,
    )(*near(*parts, part1, rest, turn1, second))
    moved = [chunks[0]]
    for k in range(1, n_z):
        moved.append(traded(chunks[k], "pulse", k))

    group = 64
    all_pulses = n_c * n_z * shard
    cuts = all_pulses // group
    scratch = [
        pltpu.VMEM((width + LANES, group), F32),
        pltpu.VMEM((low, 2 * tall, group), F32),
    ]
    make = functools.partial(column_kernel, width, tile_cols, low)
    if cuts == 1:
        cols = pl.pallas_call(
            make,
            in_specs=[VMEM] * 3,
            out_specs=VMEM,
            out_shape=pltpu.VMEM((grid, 2 * group), BF16),
            scratch_shapes=scratch,
            name="column_transform",
            **room,
        )(*near(everyone, table, turn3))
    else:
        cols = pl.pallas_call(
            make,
            grid=(cuts,),
            in_specs=[
                pl.BlockSpec((group, width + LANES), lambda i: (i, 0)),
                pl.BlockSpec((2 * tall, tall), lambda i: (0, 0)),
                pl.BlockSpec((2, tall, low), lambda i: (0, 0, 0)),
            ],
            out_specs=pl.BlockSpec((grid, 2 * group), lambda i: (0, i)),
            out_shape=jax.ShapeDtypeStruct((grid, 2 * all_pulses), BF16),
            scratch_shapes=scratch,
            name="column_transform",
        )(everyone, table, turn3)

    quads = block_bins // LANES
    lines = pl.pallas_call(
        functools.partial(line_kernel, n_z, per, blocks, quads, total_blocks),
        in_specs=[VMEM] * (n_z + 3),
        out_specs=[VMEM] * n_z,
        out_shape=[pltpu.VMEM((2 * pulses, grid // n_z), BF16)] * n_z,
        scratch_shapes=[
            pltpu.VMEM((2 * pulses * blocks * quads, LANES), F32),
            pltpu.VMEM((2, total_blocks * pulses, LANES), F32),
            pltpu.VMEM((2 * pulses * tops, LANES), F32),
        ],
        name="line_transform",
        **room,
    )(*near(*moved, range_taps, turn2, last))
    moved = [lines[0]]
    for k in range(1, n_z):
        moved.append(traded(lines[k], "pulse", k))
    if wide:
        pieces = pl.pallas_call(
            functools.partial(fold_kernel, n_z, n_c),
            in_specs=[VMEM] * n_z,
            out_specs=[VMEM] * quad,
            out_shape=[pltpu.VMEM((2 * pulses, out_rows), BF16)] * quad,
            scratch_shapes=[pltpu.VMEM((2 * pulses, grid // n_z), BF16)],
            name="fold",
            **room,
        )(*near(*moved))
    else:
        acc = sum(m.astype(F32) for m in moved).astype(BF16)
        mine = my_x * n_c + my_c
        pieces = [
            lax.dynamic_slice_in_dim(acc, (mine ^ k) * out_rows, out_rows, 1)
            for k in range(quad)
        ]
    parts = [pieces[0]]
    for k in range(1, quad):
        parts.append(traded(pieces[k], ("range", "sub"), k))

    wide_x = 512
    depth = 2 * all_pulses
    out_shape = jax.ShapeDtypeStruct((2, out_rows, grid), F32)
    if cuts == 1 and wide:
        return pl.pallas_call(
            functools.partial(image_kernel, (n_z, n_x, n_c, per), wide_x),
            in_specs=[VMEM] * (quad + 1),
            out_specs=HELD,
            out_shape=out_shape,
            scratch_shapes=[
                pltpu.VMEM((2, out_rows, grid), F32),
                pltpu.SemaphoreType.DMA((grid // wide_x,)),
            ],
            name="image",
            **room,
        )(*near(*parts, cols))
    lines = factor([p.astype(F32) for p in parts], n_z, n_x, n_c, per).T
    re = lines[:, :all_pulses].reshape(out_rows, cuts, 1, group)
    im = lines[:, all_pulses:].reshape(out_rows, cuts, 1, group)
    lhs = jnp.stack(
        [jnp.concatenate([re, -im], axis=2), jnp.concatenate([im, re], axis=2)]
    ).reshape(2 * out_rows, depth).astype(BF16)
    return pl.pallas_call(
        image_plain,
        grid=(grid // wide_x,),
        in_specs=[
            pl.BlockSpec(lhs.shape, lambda i: (0, 0)),
            pl.BlockSpec((wide_x, depth), lambda i: (i, 0)),
        ],
        out_specs=pl.BlockSpec((2, out_rows, wide_x), lambda i: (0, 0, i)),
        out_shape=out_shape,
        name="image",
    )(lhs, cols)


def solution(mesh):
    placed = (
        P(None, ("groups", "pulse", "sub"), "range"),
        P("pulse", None, None),
        P(("groups", "pulse", "sub"), None),
        P(("groups", "pulse", "sub"), None),
    )
    return jax.shard_map(
        program,
        mesh=mesh,
        in_specs=placed,
        out_specs=P(None, ("groups", "pulse", "range", "sub"), None),
        check_vma=False,
    )
```

```python
import functools
import math

import jax
import jax.numpy as jnp
import numpy as np
from jax import lax
from jax.experimental import pallas as pl
from jax.experimental.pallas import tpu as pltpu
from jax.sharding import PartitionSpec as P


LANES = 128
F32 = jnp.float32
BF16 = jnp.bfloat16
VMEM = pl.BlockSpec(memory_space=pltpu.VMEM)
HELD = pl.BlockSpec(memory_space=pltpu.HBM)
NT = (((1,), (1,)), ((), ()))
NN = (((1,), (0,)), ((), ()))


def dot(a, b, dims=NN):
    return lax.dot_general(a, b, dims, preferred_element_type=F32)


def traded(block, axis, k):
    count = math.prod(lax.axis_size(a) for a in ((axis,) if isinstance(axis, str) else axis))
    return lax.ppermute(block, axis, [(i, i ^ k) for i in range(count)])


def near(*values):
    return [pltpu.with_memory_space_constraint(v, pltpu.VMEM) for v in values]


def far(*values):
    return [pltpu.with_memory_space_constraint(v, pltpu.HBM) for v in values]


def phasor(rows, cols, period, sign):
    turns = np.outer(rows, cols) % period
    angles = turns * (2.0 * math.pi / period)
    return np.cos(angles), sign * np.sin(angles)


def add(a, b):
    return b if a is None else a if b is None else a + b


def sub(a, b):
    return a if b is None else -b if a is None else a - b


def scaled(a, factor):
    return None if a is None else a * factor


def fourier(values, sign):
    count = len(values)
    if count == 1:
        return values
    even = fourier(values[0::2], sign)
    odd = fourier(values[1::2], sign)
    out = [None] * count
    for k in range(count // 2):
        er, ei = even[k]
        a, b = odd[k]
        if 4 * k == count:
            tr, ti = (sub(None, b), a) if sign > 0 else (b, sub(None, a))
        elif k == 0:
            tr, ti = a, b
        elif 8 * k in (count, 3 * count):
            h = math.sqrt(0.5)
            c = h if 8 * k == count else -h
            if sign < 0:
                b, a, c = a, b, c
                tr, ti = (sub(scaled(b, c), scaled(a, -h)), sub(scaled(a, c), scaled(b, h)))
            else:
                tr, ti = (sub(scaled(a, c), scaled(b, h)), add(scaled(a, h), scaled(b, c)))
        else:
            angle = sign * 2.0 * math.pi * k / count
            c, s = math.cos(angle), math.sin(angle)
            tr = sub(scaled(a, c), scaled(b, s))
            ti = add(scaled(a, s), scaled(b, c))
        out[k] = (add(er, tr), add(ei, ti))
        out[k + count // 2] = (sub(er, tr), sub(ei, ti))
    return out


def split_kernel(n_x, per, raw, taps_in, tile_in, *refs):
    outs = refs[:n_x]
    marked, held, taps, tile, lines, sent = refs[n_x:]
    my_x = lax.axis_index("range")
    copies = [pltpu.make_async_copy(raw.at[c], held.at[c], sent.at[c]) for c in range(2)]
    copies.append(pltpu.make_async_copy(taps_in, taps, sent.at[2]))
    copies.append(pltpu.make_async_copy(tile_in, tile, sent.at[3]))
    for copy in copies:
        copy.start()
    shard = raw.shape[1]
    tiles = raw.shape[2] // LANES
    width = taps.shape[1]
    copies[2].wait()
    copies[3].wait()
    row = lax.broadcasted_iota(jnp.int32, (per, LANES), 0)
    for k in range(n_x):
        rows = slice(k * per, (k + 1) * per)
        values = taps[:per, :].astype(F32)
        for x in range(1, n_x):
            pick = taps[x * per : (x + 1) * per, :].astype(F32)
            values = jnp.where((my_x ^ k) == x, pick, values)
        ids = jnp.zeros((per, LANES), jnp.int32)
        for p in range(per):
            ids = jnp.where(row == p, tile[0, (my_x ^ k) * per + p], ids)
        marked[rows, :width] = values.astype(BF16)
        marked[rows, width:] = ids.astype(F32).astype(BF16)
    for c in range(2):
        copies[c].wait()
        for t in range(tiles):
            lines[c, t * shard : (t + 1) * shard, :] = held[
                c, :, t * LANES : (t + 1) * LANES
            ].astype(F32)
        for k in range(n_x):
            for p in range(per):
                outs[k][c * tiles : (c + 1) * tiles, p * LANES : (p + 1) * LANES] = lines[
                    c, pl.ds((my_x ^ k) * per + p, tiles, stride=shard), :
                ].astype(BF16)


def ready_kernel(n_fixed, own, first, turn, *refs):
    fixed = refs[:n_fixed]
    part, rest, turned = refs[n_fixed : n_fixed + 3]
    brought = refs[n_fixed + 3 : 2 * n_fixed + 3]
    mine, sent = refs[2 * n_fixed + 3 :]
    my_x = lax.axis_index("range")
    copies = [
        pltpu.make_async_copy(first.at[my_x, 0], mine, sent.at[0]),
        pltpu.make_async_copy(first.at[my_x, pl.ds(1, rest.shape[0])], rest, sent.at[1]),
        pltpu.make_async_copy(turn.at[lax.axis_index("pulse")], turned, sent.at[2]),
    ]
    for i in range(n_fixed):
        copies.append(pltpu.make_async_copy(fixed[i], brought[i], sent.at[i + 3]))
    for copy in copies:
        copy.start()
    copies[0].wait()
    part[...] = dot(mine[...], own[...])
    for copy in copies[1:]:
        copy.wait()


def pulse_kernel(n_parts, n_z, per, *refs):
    parts = refs[: n_parts - 1]
    mixed, first, turn, second = refs[n_parts - 1 : n_parts + 3]
    outs = refs[n_parts + 3 :]
    my_z = lax.axis_index("pulse")
    mixed = mixed[...]
    for k, part in enumerate(parts):
        mixed = mixed + dot(first[k], part[...])
    half = mixed.shape[0] // 2
    band = LANES // n_z
    picks = []
    for k in range(n_z):
        for c in range(2):
            row = pl.multiple_of(c * LANES + (my_z ^ k) * band, band)
            picks.append(second[pl.ds(row, band), :])
    table = jnp.concatenate(picks, axis=0)
    tc, ts = turn[0], turn[1]
    for p in range(per):
        re = mixed[:half, p * LANES : (p + 1) * LANES]
        im = mixed[half:, p * LANES : (p + 1) * LANES]
        spun = jnp.concatenate([re * tc - im * ts, re * ts + im * tc], axis=1).astype(BF16)
        done = dot(table, spun, NT).astype(BF16)
        for k in range(n_z):
            outs[k][:, p * half : (p + 1) * half] = done[2 * band * k : 2 * band * (k + 1), :]


def line_kernel(n_z, per, blocks, quads, total_blocks, *refs):
    chunks = refs[:n_z]
    taps, turn, last = refs[n_z : n_z + 3]
    outs = refs[n_z + 3 : 2 * n_z + 3]
    bins, sums, rows = refs[2 * n_z + 3 :]
    my_z = lax.axis_index("pulse")
    band = blocks * quads
    pulses = n_z * per
    for k in range(n_z):
        for c in range(2):
            for p in range(per):
                at = ((c * n_z + k) * per + p) * band
                bins[at : at + band, :] = chunks[k][
                    c * band : (c + 1) * band, p * LANES : (p + 1) * LANES
                ].astype(F32)
    ky = []
    for b in range(blocks):
        lhs = jnp.concatenate(
            [bins[pl.ds(b * quads + q, 2 * pulses, stride=band), :].astype(BF16) for q in range(quads)],
            axis=1,
        )
        line = dot(lhs, taps[b])
        ky.append((line[:pulses], line[pulses:]))
    quarter = total_blocks // 4
    for y in range(quarter):
        classes = []
        for m in range(4):
            acc = None
            for b in range(m, blocks, 4):
                re, im = ky[b]
                angle = 2.0 * math.pi * (b * y % total_blocks) / total_blocks
                co, si = math.cos(angle), math.sin(angle)
                if b * y == 0:
                    term = (re, im)
                else:
                    term = (re * co - im * si, re * si + im * co)
                acc = term if acc is None else (acc[0] + term[0], acc[1] + term[1])
            if acc is None:
                acc = (jnp.zeros_like(ky[0][0]), jnp.zeros_like(ky[0][1]))
            classes.append(acc)
        for r, (re, im) in enumerate(fourier(classes, 1)):
            at = (y + r * quarter) * pulses
            sums[0, at : at + pulses, :] = re
            sums[1, at : at + pulses, :] = im
    fold = LANES // total_blocks
    tops = last.shape[0] // 2
    for m in range(pulses):
        gr = sums[0, pl.ds(m, total_blocks, stride=pulses), :]
        gi = sums[1, pl.ds(m, total_blocks, stride=pulses), :]
        spun = []
        for f in range(fold):
            tc = turn[0, f * total_blocks : (f + 1) * total_blocks, :]
            ts = turn[1, f * total_blocks : (f + 1) * total_blocks, :]
            spun.append(
                jnp.concatenate([gr * tc - gi * ts, gr * ts + gi * tc], axis=1).astype(BF16)
            )
        done = dot(last[...], jnp.concatenate(spun, axis=0), NT)
        for c in range(2):
            at = (c * pulses + m) * tops
            rows[at : at + tops, :] = done[c * tops : (c + 1) * tops, :]
    share = tops // n_z
    for k in range(n_z):
        for s in range(share):
            line = rows[pl.ds((my_z ^ k) * share + s, 2 * pulses, stride=tops), :]
            blocks_of = [
                line[c * pulses + (z ^ k) * per : c * pulses + (z ^ k) * per + per]
                for c in range(2)
                for z in range(n_z)
            ]
            outs[k][:, s * LANES : (s + 1) * LANES] = jnp.concatenate(blocks_of, axis=0).astype(BF16)


def fold_kernel(n_z, n_c, *refs):
    parts, outs, total = refs[:n_z], refs[n_z:-1], refs[-1]
    acc = parts[0][...].astype(F32)
    for part in parts[1:]:
        acc = acc + part[...].astype(F32)
    total[...] = acc.astype(BF16)
    mine = lax.axis_index("range") * n_c + lax.axis_index("sub")
    wide = outs[0].shape[1]
    for k, out in enumerate(outs):
        out[...] = total[:, pl.ds(pl.multiple_of((mine ^ k) * wide, wide), wide)]


def column_kernel(width, tile_cols, taps, table, turn, out, mixed, spread):
    pulses = taps.shape[0]
    low = mixed.shape[0]
    high = out.shape[0] // low
    steps = width // high
    step = 16
    for v in range(high // LANES):
        for r in range(0, pulses, step):
            tile = taps[r : r + step, width:].astype(F32)
            inside = [tile == float(t) for t in range(tile_cols)]
            values = []
            for t in range(tile_cols):
                for i in range(steps):
                    at = i * high + v * LANES
                    value = taps[r : r + step, at : at + LANES].astype(F32)
                    values.append((jnp.where(inside[t], value, 0.0), None))
            left, right = slice(v * LANES, (v + 1) * LANES), slice(high + v * LANES, high + (v + 1) * LANES)
            for d, (re, im) in enumerate(fourier(values, 1)):
                tc, ts = turn[0, d : d + 1, left], turn[1, d : d + 1, left]
                if im is None:
                    re, im = re * tc, re * ts
                else:
                    re, im = re * tc - im * ts, re * ts + im * tc
                mixed[d, r : r + step, left] = re.astype(BF16)
                mixed[d, r : r + step, right] = (-im).astype(BF16)
                mixed[d, pulses + r : pulses + r + step, left] = im.astype(BF16)
                mixed[d, pulses + r : pulses + r + step, right] = re.astype(BF16)
    for d in range(0, low, 2):
        both = jnp.concatenate([mixed[d], mixed[d + 1]], axis=0)
        done = dot(table[...], both, NT)
        spread[pl.ds(d, high, stride=low), :] = done[:, : 2 * pulses]
        spread[pl.ds(d + 1, high, stride=low), :] = done[:, 2 * pulses :]
    out[...] = spread[...].astype(BF16)


def factor(parts, n_z, n_x, n_c, per):
    pulses = n_z * per
    out = []
    for comp in range(2):
        for c in range(n_c):
            for z in range(n_z):
                for x in range(n_x):
                    at = comp * pulses + z * per
                    out.append(parts[x * n_c + c][at : at + per, :])
    return jnp.concatenate(out, axis=0)


def image_kernel(dims, step, *refs):
    n_z, n_x, n_c, per = dims
    count = n_x * n_c
    parts = [ref[...].astype(F32) for ref in refs[:count]]
    cols, out, held, sent = refs[count:]
    lines = factor(parts, n_z, n_x, n_c, per).T
    half = lines.shape[1] // 2
    re, im = lines[:, :half], lines[:, half:]
    rows = lines.shape[0]
    lhs = jnp.concatenate(
        [jnp.concatenate([re, -im], axis=1), jnp.concatenate([im, re], axis=1)], axis=0
    ).astype(BF16)
    copies = []
    for i in range(cols.shape[0] // step):
        done = dot(lhs, cols[i * step : (i + 1) * step, :], NT)
        at = pl.ds(i * step, step)
        held[0, :, at] = done[:rows]
        held[1, :, at] = done[rows:]
        copies.append(pltpu.make_async_copy(held.at[:, :, at], out.at[:, :, at], sent.at[i]))
        copies[-1].start()
    for copy in copies:
        copy.wait()


def image_plain(lhs, cols, out):
    rows = out.shape[1]
    done = dot(lhs[...], cols[...], NT)
    out[0] = done[:rows]
    out[1] = done[rows:]


def table_of(values, dtype=BF16):
    return jnp.asarray(np.asarray(values, np.float32), dtype)


def complex_left(c, s, scale=1.0):
    return np.block([[c, -s], [s, c]]) * scale


def program(raw_echo, range_taps, azim_taps, tile_col):
    n_x, n_z, n_c = lax.axis_size("range"), lax.axis_size("pulse"), lax.axis_size("sub")
    my_x, my_c = lax.axis_index("range"), lax.axis_index("sub")
    shard, part = raw_echo.shape[1:]
    per = shard // n_x
    samples = part * n_x
    blocks, block_bins, block_rows = range_taps.shape
    total_blocks = blocks * n_z
    grid = total_blocks * block_rows
    width = azim_taps.shape[1]
    tile_cols = grid // width
    quad = n_x * n_c
    out_rows = grid // (n_z * quad)
    pulses = n_z * per
    wide = out_rows % LANES == 0
    room = {}
    if wide:
        room = {"compiler_params": pltpu.CompilerParams(vmem_limit_bytes=24 << 20)}

    high = samples // LANES
    tiles = high // n_x
    n128 = np.arange(LANES)
    nh = np.arange(high)
    first = complex_left(*phasor(nh, nh, high, -1.0)).reshape(2 * high, 2, n_x, tiles)
    first = [first[:, :, [x ^ k for k in range(n_x)]].transpose(2, 0, 1, 3) for x in range(n_x)]
    first = table_of(np.stack(first).reshape(n_x, n_x, 2 * high, 2 * tiles))
    turn1 = table_of(np.stack(phasor(nh, n128, samples, -1.0)), F32)
    second = table_of(complex_left(*phasor(n128, n128, LANES, -1.0), 1.0 / math.sqrt(samples)))
    tops = grid // LANES
    shift = grid // n_z
    turn2 = np.stack([np.stack(phasor(n128, n128 + shift * z, grid, 1.0)) for z in range(n_z)])
    turn2 = table_of(turn2, F32)
    c, s = phasor(np.arange(tops), n128, tops, 1.0)
    last = table_of(complex_left(c, s, 1.0 / math.sqrt(grid)))
    low = 16
    tall = grid // low
    nt = np.arange(tall)
    c, s = phasor(nt, nt, tall, 1.0)
    table = table_of(np.concatenate([c, s], axis=1) / math.sqrt(grid))
    turn3 = table_of(np.stack(phasor(np.arange(low), nt, grid, 1.0)), F32)

    piece = pltpu.VMEM((2 * tiles, per * LANES), BF16)
    *pieces, marked = pl.pallas_call(
        functools.partial(split_kernel, n_x, per),
        in_specs=[HELD] * 3,
        out_specs=[VMEM] * (n_x + 1),
        out_shape=[piece] * n_x + [pltpu.VMEM((shard, width + LANES), BF16)],
        scratch_shapes=[
            pltpu.VMEM(raw_echo.shape, BF16),
            pltpu.VMEM(azim_taps.shape, BF16),
            pltpu.SMEM((1, shard), jnp.int32),
            pltpu.VMEM((2, tiles * shard, LANES), F32),
            pltpu.SemaphoreType.DMA((4,)),
        ],
        name="split",
        **room,
    )(*far(raw_echo, azim_taps, tile_col.T))
    parts = []
    for k in range(1, n_x):
        parts.append(traded(pieces[k], "range", k))

    everyone = marked
    for axis, count in (("pulse", n_z), ("sub", n_c)):
        k = 1
        while k < count:
            everyone = jnp.concatenate([everyone, traded(everyone, axis, k)], axis=0)
            k *= 2

    fixed = (turn1, second, last, range_taps, table, turn3)
    part1, rest, turn2, *brought = pl.pallas_call(
        functools.partial(ready_kernel, len(fixed)),
        in_specs=[VMEM] + [HELD] * (2 + len(fixed)),
        out_specs=[VMEM] * (3 + len(fixed)),
        out_shape=[
            pltpu.VMEM((2 * high, per * LANES), F32),
            pltpu.VMEM((max(n_x - 1, 1), 2 * high, 2 * tiles), BF16),
            pltpu.VMEM(turn2.shape[1:], F32),
        ]
        + [pltpu.VMEM(f.shape, f.dtype) for f in fixed],
        scratch_shapes=[
            pltpu.VMEM((2 * high, 2 * tiles), BF16),
            pltpu.SemaphoreType.DMA((3 + len(fixed),)),
        ],
        name="ready",
        **room,
    )(*near(pieces[0]), *far(first, turn2, *fixed))
    turn1, second, last, range_taps, table, turn3 = brought

    band = LANES // n_z
    chunk = pltpu.VMEM((2 * band, per * high), BF16)
    chunks = pl.pallas_call(
        functools.partial(pulse_kernel, n_x, n_z, per),
        in_specs=[VMEM] * (n_x + 3),
        out_specs=[VMEM] * n_z,
        out_shape=[chunk] * n_z,
        name="pulse_transform",
        **room,
    )(*near(*parts, part1, rest, turn1, second))
    moved = [chunks[0]]
    for k in range(1, n_z):
        moved.append(traded(chunks[k], "pulse", k))

    group = 64
    all_pulses = n_c * n_z * shard
    cuts = all_pulses // group
    scratch = [
        pltpu.VMEM((low, 2 * group, 2 * tall), BF16),
        pltpu.VMEM((grid, 2 * group), F32),
    ]
    make = functools.partial(column_kernel, width, tile_cols)
    if cuts == 1:
        cols = pl.pallas_call(
            make,
            in_specs=[VMEM] * 3,
            out_specs=VMEM,
            out_shape=pltpu.VMEM((grid, 2 * group), BF16),
            scratch_shapes=scratch,
            name="column_transform",
            **room,
        )(*near(everyone, table, turn3))
    else:
        cols = pl.pallas_call(
            make,
            grid=(cuts,),
            in_specs=[
                pl.BlockSpec((group, width + LANES), lambda i: (i, 0)),
                pl.BlockSpec((tall, 2 * tall), lambda i: (0, 0)),
                pl.BlockSpec((2, low, tall), lambda i: (0, 0, 0)),
            ],
            out_specs=pl.BlockSpec((grid, 2 * group), lambda i: (0, i)),
            out_shape=jax.ShapeDtypeStruct((grid, 2 * all_pulses), BF16),
            scratch_shapes=scratch,
            name="column_transform",
        )(everyone, table, turn3)

    quads = block_bins // LANES
    lines = pl.pallas_call(
        functools.partial(line_kernel, n_z, per, blocks, quads, total_blocks),
        in_specs=[VMEM] * (n_z + 3),
        out_specs=[VMEM] * n_z,
        out_shape=[pltpu.VMEM((2 * pulses, grid // n_z), BF16)] * n_z,
        scratch_shapes=[
            pltpu.VMEM((2 * pulses * blocks * quads, LANES), F32),
            pltpu.VMEM((2, total_blocks * pulses, LANES), F32),
            pltpu.VMEM((2 * pulses * tops, LANES), F32),
        ],
        name="line_transform",
        **room,
    )(*near(*moved, range_taps, turn2, last))
    moved = [lines[0]]
    for k in range(1, n_z):
        moved.append(traded(lines[k], "pulse", k))
    if wide:
        pieces = pl.pallas_call(
            functools.partial(fold_kernel, n_z, n_c),
            in_specs=[VMEM] * n_z,
            out_specs=[VMEM] * quad,
            out_shape=[pltpu.VMEM((2 * pulses, out_rows), BF16)] * quad,
            scratch_shapes=[pltpu.VMEM((2 * pulses, grid // n_z), BF16)],
            name="fold",
            **room,
        )(*near(*moved))
    else:
        acc = sum(m.astype(F32) for m in moved).astype(BF16)
        mine = my_x * n_c + my_c
        pieces = [
            lax.dynamic_slice_in_dim(acc, (mine ^ k) * out_rows, out_rows, 1)
            for k in range(quad)
        ]
    parts = [pieces[0]]
    for k in range(1, quad):
        parts.append(traded(pieces[k], ("range", "sub"), k))

    wide_x = 512
    depth = 2 * all_pulses
    out_shape = jax.ShapeDtypeStruct((2, out_rows, grid), F32)
    if cuts == 1 and wide:
        return pl.pallas_call(
            functools.partial(image_kernel, (n_z, n_x, n_c, per), wide_x),
            in_specs=[VMEM] * (quad + 1),
            out_specs=HELD,
            out_shape=out_shape,
            scratch_shapes=[
                pltpu.VMEM((2, out_rows, grid), F32),
                pltpu.SemaphoreType.DMA((grid // wide_x,)),
            ],
            name="image",
            **room,
        )(*near(*parts, cols))
    lines = factor([p.astype(F32) for p in parts], n_z, n_x, n_c, per).T
    re = lines[:, :all_pulses].reshape(out_rows, cuts, 1, group)
    im = lines[:, all_pulses:].reshape(out_rows, cuts, 1, group)
    lhs = jnp.stack(
        [jnp.concatenate([re, -im], axis=2), jnp.concatenate([im, re], axis=2)]
    ).reshape(2 * out_rows, depth).astype(BF16)
    return pl.pallas_call(
        image_plain,
        grid=(grid // wide_x,),
        in_specs=[
            pl.BlockSpec(lhs.shape, lambda i: (0, 0)),
            pl.BlockSpec((wide_x, depth), lambda i: (i, 0)),
        ],
        out_specs=pl.BlockSpec((2, out_rows, wide_x), lambda i: (0, 0, i)),
        out_shape=out_shape,
        name="image",
    )(lhs, cols)


def solution(mesh):
    placed = (
        P(None, ("groups", "pulse", "sub"), "range"),
        P("pulse", None, None),
        P(("groups", "pulse", "sub"), None),
        P(("groups", "pulse", "sub"), None),
    )
    return jax.shard_map(
        program,
        mesh=mesh,
        in_specs=placed,
        out_specs=P(None, ("groups", "pulse", "range", "sub"), None),
        check_vma=False,
    )
```

```python
import functools
import math

import jax
import jax.numpy as jnp
import numpy as np
from jax import lax
from jax.experimental import pallas as pl
from jax.experimental.pallas import tpu as pltpu
from jax.sharding import PartitionSpec as P


LANES = 128
F32 = jnp.float32
BF16 = jnp.bfloat16
VMEM = pl.BlockSpec(memory_space=pltpu.VMEM)
HELD = pl.BlockSpec(memory_space=pltpu.HBM)
NT = (((1,), (1,)), ((), ()))
NN = (((1,), (0,)), ((), ()))


def dot(a, b, dims=NN):
    return lax.dot_general(a, b, dims, preferred_element_type=F32)


def traded(block, axis, k):
    count = math.prod(lax.axis_size(a) for a in ((axis,) if isinstance(axis, str) else axis))
    return lax.ppermute(block, axis, [(i, i ^ k) for i in range(count)])


def near(*values):
    return [pltpu.with_memory_space_constraint(v, pltpu.VMEM) for v in values]


def far(*values):
    return [pltpu.with_memory_space_constraint(v, pltpu.HBM) for v in values]


def phasor(rows, cols, period, sign):
    turns = np.outer(rows, cols) % period
    angles = turns * (2.0 * math.pi / period)
    return np.cos(angles), sign * np.sin(angles)


def add(a, b):
    return b if a is None else a if b is None else a + b


def sub(a, b):
    return a if b is None else -b if a is None else a - b


def scaled(a, factor):
    return None if a is None else a * factor


def fourier(values, sign):
    count = len(values)
    if count == 1:
        return values
    even = fourier(values[0::2], sign)
    odd = fourier(values[1::2], sign)
    out = [None] * count
    for k in range(count // 2):
        er, ei = even[k]
        a, b = odd[k]
        if 4 * k == count:
            tr, ti = (sub(None, b), a) if sign > 0 else (b, sub(None, a))
        elif k == 0:
            tr, ti = a, b
        elif 8 * k in (count, 3 * count):
            h = math.sqrt(0.5)
            c = h if 8 * k == count else -h
            if sign < 0:
                b, a, c = a, b, c
                tr, ti = (sub(scaled(b, c), scaled(a, -h)), sub(scaled(a, c), scaled(b, h)))
            else:
                tr, ti = (sub(scaled(a, c), scaled(b, h)), add(scaled(a, h), scaled(b, c)))
        else:
            angle = sign * 2.0 * math.pi * k / count
            c, s = math.cos(angle), math.sin(angle)
            tr = sub(scaled(a, c), scaled(b, s))
            ti = add(scaled(a, s), scaled(b, c))
        out[k] = (add(er, tr), add(ei, ti))
        out[k + count // 2] = (sub(er, tr), sub(ei, ti))
    return out


def split_kernel(n_x, per, raw, taps_in, tile_in, *refs):
    outs = refs[:n_x]
    marked, held, taps, tile, lines, sent = refs[n_x:]
    my_x = lax.axis_index("range")
    copies = [pltpu.make_async_copy(raw.at[c], held.at[c], sent.at[c]) for c in range(2)]
    copies.append(pltpu.make_async_copy(taps_in, taps, sent.at[2]))
    copies.append(pltpu.make_async_copy(tile_in, tile, sent.at[3]))
    for copy in copies:
        copy.start()
    shard = raw.shape[1]
    tiles = raw.shape[2] // LANES
    width = taps.shape[1]
    copies[2].wait()
    copies[3].wait()
    row = lax.broadcasted_iota(jnp.int32, (per, LANES), 0)
    for k in range(n_x):
        rows = slice(k * per, (k + 1) * per)
        values = taps[:per, :].astype(F32)
        for x in range(1, n_x):
            pick = taps[x * per : (x + 1) * per, :].astype(F32)
            values = jnp.where((my_x ^ k) == x, pick, values)
        ids = jnp.zeros((per, LANES), jnp.int32)
        for p in range(per):
            ids = jnp.where(row == p, tile[0, (my_x ^ k) * per + p], ids)
        marked[rows, :width] = values.astype(BF16)
        marked[rows, width:] = ids.astype(F32).astype(BF16)
    for c in range(2):
        copies[c].wait()
        for t in range(tiles):
            lines[c, t * shard : (t + 1) * shard, :] = held[
                c, :, t * LANES : (t + 1) * LANES
            ].astype(F32)
        for k in range(n_x):
            for p in range(per):
                outs[k][c * tiles : (c + 1) * tiles, p * LANES : (p + 1) * LANES] = lines[
                    c, pl.ds((my_x ^ k) * per + p, tiles, stride=shard), :
                ].astype(BF16)


def ready_kernel(n_fixed, own, first, *refs):
    fixed = refs[:n_fixed]
    part, rest = refs[n_fixed : n_fixed + 2]
    brought = refs[n_fixed + 2 : 2 * n_fixed + 2]
    mine, sent = refs[2 * n_fixed + 2 :]
    my_x = lax.axis_index("range")
    copies = [
        pltpu.make_async_copy(first.at[my_x, 0], mine, sent.at[0]),
        pltpu.make_async_copy(first.at[my_x, pl.ds(1, rest.shape[0])], rest, sent.at[1]),
    ]
    for i in range(n_fixed):
        copies.append(pltpu.make_async_copy(fixed[i], brought[i], sent.at[i + 2]))
    for copy in copies:
        copy.start()
    copies[0].wait()
    part[...] = dot(mine[...], own[...])
    for copy in copies[1:]:
        copy.wait()


def bring_kernel(n_fixed, turn, *refs):
    fixed, turned_in, brought, sent = refs[:n_fixed], refs[n_fixed], refs[n_fixed + 1 : -1], refs[-1]
    copies = [pltpu.make_async_copy(turn.at[lax.axis_index("pulse")], turned_in, sent.at[n_fixed])]
    for i in range(n_fixed):
        copies.append(pltpu.make_async_copy(fixed[i], brought[i], sent.at[i]))
    for copy in copies:
        copy.start()
    for copy in copies:
        copy.wait()


def pulse_kernel(n_parts, n_z, per, *refs):
    parts = refs[: n_parts - 1]
    mixed, first, turn, second = refs[n_parts - 1 : n_parts + 3]
    outs = refs[n_parts + 3 :]
    my_z = lax.axis_index("pulse")
    mixed = mixed[...]
    for k, part in enumerate(parts):
        mixed = mixed + dot(first[k], part[...])
    half = mixed.shape[0] // 2
    band = LANES // n_z
    picks = []
    for k in range(n_z):
        for c in range(2):
            row = pl.multiple_of(c * LANES + (my_z ^ k) * band, band)
            picks.append(second[pl.ds(row, band), :])
    table = jnp.concatenate(picks, axis=0)
    tc, ts = turn[0], turn[1]
    for p in range(per):
        re = mixed[:half, p * LANES : (p + 1) * LANES]
        im = mixed[half:, p * LANES : (p + 1) * LANES]
        spun = jnp.concatenate([re * tc - im * ts, re * ts + im * tc], axis=1).astype(BF16)
        done = dot(table, spun, NT).astype(BF16)
        for k in range(n_z):
            outs[k][:, p * half : (p + 1) * half] = done[2 * band * k : 2 * band * (k + 1), :]


def line_kernel(n_z, per, blocks, quads, total_blocks, *refs):
    chunks = refs[:n_z]
    taps, turn, last = refs[n_z : n_z + 3]
    outs = refs[n_z + 3 : 2 * n_z + 3]
    bins, sums, rows = refs[2 * n_z + 3 :]
    my_z = lax.axis_index("pulse")
    band = blocks * quads
    pulses = n_z * per
    for k in range(n_z):
        for c in range(2):
            for p in range(per):
                at = ((c * n_z + k) * per + p) * band
                bins[at : at + band, :] = chunks[k][
                    c * band : (c + 1) * band, p * LANES : (p + 1) * LANES
                ].astype(F32)
    ky = []
    for b in range(blocks):
        lhs = jnp.concatenate(
            [bins[pl.ds(b * quads + q, 2 * pulses, stride=band), :].astype(BF16) for q in range(quads)],
            axis=1,
        )
        line = dot(lhs, taps[b])
        ky.append((line[:pulses], line[pulses:]))
    quarter = total_blocks // 4
    for y in range(quarter):
        classes = []
        for m in range(4):
            acc = None
            for b in range(m, blocks, 4):
                re, im = ky[b]
                angle = 2.0 * math.pi * (b * y % total_blocks) / total_blocks
                co, si = math.cos(angle), math.sin(angle)
                if b * y == 0:
                    term = (re, im)
                else:
                    term = (re * co - im * si, re * si + im * co)
                acc = term if acc is None else (acc[0] + term[0], acc[1] + term[1])
            if acc is None:
                acc = (jnp.zeros_like(ky[0][0]), jnp.zeros_like(ky[0][1]))
            classes.append(acc)
        for r, (re, im) in enumerate(fourier(classes, 1)):
            at = (y + r * quarter) * pulses
            sums[0, at : at + pulses, :] = re
            sums[1, at : at + pulses, :] = im
    fold = LANES // total_blocks
    tops = last.shape[0] // 2
    for m in range(pulses):
        gr = sums[0, pl.ds(m, total_blocks, stride=pulses), :]
        gi = sums[1, pl.ds(m, total_blocks, stride=pulses), :]
        spun = []
        for f in range(fold):
            tc = turn[0, f * total_blocks : (f + 1) * total_blocks, :]
            ts = turn[1, f * total_blocks : (f + 1) * total_blocks, :]
            spun.append(
                jnp.concatenate([gr * tc - gi * ts, gr * ts + gi * tc], axis=1).astype(BF16)
            )
        done = dot(last[...], jnp.concatenate(spun, axis=0), NT)
        for c in range(2):
            at = (c * pulses + m) * tops
            rows[at : at + tops, :] = done[c * tops : (c + 1) * tops, :]
    share = tops // n_z
    for k in range(n_z):
        for s in range(share):
            line = rows[pl.ds((my_z ^ k) * share + s, 2 * pulses, stride=tops), :]
            blocks_of = [
                line[c * pulses + (z ^ k) * per : c * pulses + (z ^ k) * per + per]
                for c in range(2)
                for z in range(n_z)
            ]
            outs[k][:, s * LANES : (s + 1) * LANES] = jnp.concatenate(blocks_of, axis=0).astype(BF16)


def fold_kernel(n_z, n_c, *refs):
    parts, outs, total = refs[:n_z], refs[n_z:-1], refs[-1]
    acc = parts[0][...].astype(F32)
    for part in parts[1:]:
        acc = acc + part[...].astype(F32)
    total[...] = acc.astype(BF16)
    mine = lax.axis_index("range") * n_c + lax.axis_index("sub")
    wide = outs[0].shape[1]
    for k, out in enumerate(outs):
        out[...] = total[:, pl.ds(pl.multiple_of((mine ^ k) * wide, wide), wide)]


def column_kernel(width, tile_cols, taps, table, turn, out, mixed, spread):
    pulses = taps.shape[0]
    low = mixed.shape[0]
    high = out.shape[0] // low
    steps = width // high
    step = 16
    for v in range(high // LANES):
        for r in range(0, pulses, step):
            tile = taps[r : r + step, width:].astype(F32)
            inside = [tile == float(t) for t in range(tile_cols)]
            values = []
            for t in range(tile_cols):
                for i in range(steps):
                    at = i * high + v * LANES
                    value = taps[r : r + step, at : at + LANES].astype(F32)
                    values.append((jnp.where(inside[t], value, 0.0), None))
            left, right = slice(v * LANES, (v + 1) * LANES), slice(high + v * LANES, high + (v + 1) * LANES)
            for d, (re, im) in enumerate(fourier(values, 1)):
                tc, ts = turn[0, d : d + 1, left], turn[1, d : d + 1, left]
                if im is None:
                    re, im = re * tc, re * ts
                else:
                    re, im = re * tc - im * ts, re * ts + im * tc
                mixed[d, r : r + step, left] = re.astype(BF16)
                mixed[d, r : r + step, right] = (-im).astype(BF16)
                mixed[d, pulses + r : pulses + r + step, left] = im.astype(BF16)
                mixed[d, pulses + r : pulses + r + step, right] = re.astype(BF16)
    for d in range(0, low, 2):
        both = jnp.concatenate([mixed[d], mixed[d + 1]], axis=0)
        done = dot(table[...], both, NT)
        spread[pl.ds(d, high, stride=low), :] = done[:, : 2 * pulses]
        spread[pl.ds(d + 1, high, stride=low), :] = done[:, 2 * pulses :]
    out[...] = spread[...].astype(BF16)


def turned(count):
    order, k = [0], count // 2
    while k > 0:
        order, k = order + [o ^ k for o in order], k // 2
    return order


def factor(parts, n_z, n_x, n_c, per):
    pulses = n_z * per
    out = []
    for comp in range(2):
        for c in turned(n_c):
            for z in turned(n_z):
                for x in range(n_x):
                    at = comp * pulses + z * per
                    out.append(parts[x * n_c + c][at : at + per, :])
    return jnp.concatenate(out, axis=0)


def image_kernel(dims, step, *refs):
    n_z, n_x, n_c, per = dims
    count = n_x * n_c
    parts = [ref[...].astype(F32) for ref in refs[:count]]
    cols, out, held, sent = refs[count:]
    lines = factor(parts, n_z, n_x, n_c, per).T
    half = lines.shape[1] // 2
    re, im = lines[:, :half], lines[:, half:]
    rows = lines.shape[0]
    lhs = jnp.concatenate(
        [jnp.concatenate([re, -im], axis=1), jnp.concatenate([im, re], axis=1)], axis=0
    ).astype(BF16)
    copies = []
    for i in range(cols.shape[0] // step):
        done = dot(lhs, cols[i * step : (i + 1) * step, :], NT)
        at = pl.ds(i * step, step)
        held[0, :, at] = done[:rows]
        held[1, :, at] = done[rows:]
        copies.append(pltpu.make_async_copy(held.at[:, :, at], out.at[:, :, at], sent.at[i]))
        copies[-1].start()
    for copy in copies:
        copy.wait()


def image_plain(lhs, cols, out):
    rows = out.shape[1]
    done = dot(lhs[...], cols[...], NT)
    out[0] = done[:rows]
    out[1] = done[rows:]


def table_of(values, dtype=BF16):
    return jnp.asarray(np.asarray(values, np.float32), dtype)


def complex_left(c, s, scale=1.0):
    return np.block([[c, -s], [s, c]]) * scale


def program(raw_echo, range_taps, azim_taps, tile_col):
    n_x, n_z, n_c = lax.axis_size("range"), lax.axis_size("pulse"), lax.axis_size("sub")
    my_x, my_c = lax.axis_index("range"), lax.axis_index("sub")
    shard, part = raw_echo.shape[1:]
    per = shard // n_x
    samples = part * n_x
    blocks, block_bins, block_rows = range_taps.shape
    total_blocks = blocks * n_z
    grid = total_blocks * block_rows
    width = azim_taps.shape[1]
    tile_cols = grid // width
    quad = n_x * n_c
    out_rows = grid // (n_z * quad)
    pulses = n_z * per
    wide = out_rows % LANES == 0
    room = {}
    if wide:
        room = {"compiler_params": pltpu.CompilerParams(vmem_limit_bytes=24 << 20)}

    high = samples // LANES
    tiles = high // n_x
    n128 = np.arange(LANES)
    nh = np.arange(high)
    first = complex_left(*phasor(nh, nh, high, -1.0)).reshape(2 * high, 2, n_x, tiles)
    first = [first[:, :, [x ^ k for k in range(n_x)]].transpose(2, 0, 1, 3) for x in range(n_x)]
    first = table_of(np.stack(first).reshape(n_x, n_x, 2 * high, 2 * tiles))
    turn1 = table_of(np.stack(phasor(nh, n128, samples, -1.0)), F32)
    second = table_of(complex_left(*phasor(n128, n128, LANES, -1.0), 1.0 / math.sqrt(samples)))
    tops = grid // LANES
    shift = grid // n_z
    turn2 = np.stack([np.stack(phasor(n128, n128 + shift * z, grid, 1.0)) for z in range(n_z)])
    turn2 = table_of(turn2, F32)
    c, s = phasor(np.arange(tops), n128, tops, 1.0)
    last = table_of(complex_left(c, s, 1.0 / math.sqrt(grid)))
    low = 16
    tall = grid // low
    nt = np.arange(tall)
    c, s = phasor(nt, nt, tall, 1.0)
    table = table_of(np.concatenate([c, s], axis=1) / math.sqrt(grid))
    turn3 = table_of(np.stack(phasor(np.arange(low), nt, grid, 1.0)), F32)

    piece = pltpu.VMEM((2 * tiles, per * LANES), BF16)
    *pieces, marked = pl.pallas_call(
        functools.partial(split_kernel, n_x, per),
        in_specs=[HELD] * 3,
        out_specs=[VMEM] * (n_x + 1),
        out_shape=[piece] * n_x + [pltpu.VMEM((shard, width + LANES), BF16)],
        scratch_shapes=[
            pltpu.VMEM(raw_echo.shape, BF16),
            pltpu.VMEM(azim_taps.shape, BF16),
            pltpu.SMEM((1, shard), jnp.int32),
            pltpu.VMEM((2, tiles * shard, LANES), F32),
            pltpu.SemaphoreType.DMA((4,)),
        ],
        name="split",
        **room,
    )(*far(raw_echo, azim_taps, tile_col.T))
    parts = []
    for k in range(1, n_x):
        parts.append(traded(pieces[k], "range", k))

    everyone = marked
    for axis, count in (("pulse", n_z), ("sub", n_c)):
        k = count // 2
        while k > 0:
            everyone = jnp.concatenate([everyone, traded(everyone, axis, k)], axis=0)
            k //= 2

    fixed = (turn1, second)
    part1, rest, turn1, second = pl.pallas_call(
        functools.partial(ready_kernel, len(fixed)),
        in_specs=[VMEM] + [HELD] * (1 + len(fixed)),
        out_specs=[VMEM] * (2 + len(fixed)),
        out_shape=[
            pltpu.VMEM((2 * high, per * LANES), F32),
            pltpu.VMEM((max(n_x - 1, 1), 2 * high, 2 * tiles), BF16),
        ]
        + [pltpu.VMEM(f.shape, f.dtype) for f in fixed],
        scratch_shapes=[
            pltpu.VMEM((2 * high, 2 * tiles), BF16),
            pltpu.SemaphoreType.DMA((2 + len(fixed),)),
        ],
        name="ready",
        **room,
    )(*near(pieces[0]), *far(first, *fixed))
    fixed = (last, range_taps, table, turn3)
    turn2, last, range_taps, table, turn3 = pl.pallas_call(
        functools.partial(bring_kernel, len(fixed)),
        in_specs=[HELD] * (1 + len(fixed)),
        out_specs=[VMEM] * (1 + len(fixed)),
        out_shape=[pltpu.VMEM(turn2.shape[1:], F32)]
        + [pltpu.VMEM(f.shape, f.dtype) for f in fixed],
        scratch_shapes=[pltpu.SemaphoreType.DMA((1 + len(fixed),))],
        name="bring",
        **room,
    )(*far(turn2, *fixed))

    band = LANES // n_z
    chunk = pltpu.VMEM((2 * band, per * high), BF16)
    chunks = pl.pallas_call(
        functools.partial(pulse_kernel, n_x, n_z, per),
        in_specs=[VMEM] * (n_x + 3),
        out_specs=[VMEM] * n_z,
        out_shape=[chunk] * n_z,
        name="pulse_transform",
        **room,
    )(*near(*parts, part1, rest, turn1, second))
    moved = [chunks[0]]
    for k in range(1, n_z):
        moved.append(traded(chunks[k], "pulse", k))

    group = 64
    all_pulses = n_c * n_z * shard
    cuts = all_pulses // group
    scratch = [
        pltpu.VMEM((low, 2 * group, 2 * tall), BF16),
        pltpu.VMEM((grid, 2 * group), F32),
    ]
    make = functools.partial(column_kernel, width, tile_cols)
    if cuts == 1:
        cols = pl.pallas_call(
            make,
            in_specs=[VMEM] * 3,
            out_specs=VMEM,
            out_shape=pltpu.VMEM((grid, 2 * group), BF16),
            scratch_shapes=scratch,
            name="column_transform",
            **room,
        )(*near(everyone, table, turn3))
    else:
        cols = pl.pallas_call(
            make,
            grid=(cuts,),
            in_specs=[
                pl.BlockSpec((group, width + LANES), lambda i: (i, 0)),
                pl.BlockSpec((tall, 2 * tall), lambda i: (0, 0)),
                pl.BlockSpec((2, low, tall), lambda i: (0, 0, 0)),
            ],
            out_specs=pl.BlockSpec((grid, 2 * group), lambda i: (0, i)),
            out_shape=jax.ShapeDtypeStruct((grid, 2 * all_pulses), BF16),
            scratch_shapes=scratch,
            name="column_transform",
        )(everyone, table, turn3)

    quads = block_bins // LANES
    lines = pl.pallas_call(
        functools.partial(line_kernel, n_z, per, blocks, quads, total_blocks),
        in_specs=[VMEM] * (n_z + 3),
        out_specs=[VMEM] * n_z,
        out_shape=[pltpu.VMEM((2 * pulses, grid // n_z), BF16)] * n_z,
        scratch_shapes=[
            pltpu.VMEM((2 * pulses * blocks * quads, LANES), F32),
            pltpu.VMEM((2, total_blocks * pulses, LANES), F32),
            pltpu.VMEM((2 * pulses * tops, LANES), F32),
        ],
        name="line_transform",
        **room,
    )(*near(*moved, range_taps, turn2, last))
    moved = [lines[0]]
    for k in range(1, n_z):
        moved.append(traded(lines[k], "pulse", k))
    if wide:
        pieces = pl.pallas_call(
            functools.partial(fold_kernel, n_z, n_c),
            in_specs=[VMEM] * n_z,
            out_specs=[VMEM] * quad,
            out_shape=[pltpu.VMEM((2 * pulses, out_rows), BF16)] * quad,
            scratch_shapes=[pltpu.VMEM((2 * pulses, grid // n_z), BF16)],
            name="fold",
            **room,
        )(*near(*moved))
    else:
        acc = sum(m.astype(F32) for m in moved).astype(BF16)
        mine = my_x * n_c + my_c
        pieces = [
            lax.dynamic_slice_in_dim(acc, (mine ^ k) * out_rows, out_rows, 1)
            for k in range(quad)
        ]
    parts = [pieces[0]]
    for k in range(1, quad):
        parts.append(traded(pieces[k], ("range", "sub"), k))

    wide_x = 512
    depth = 2 * all_pulses
    out_shape = jax.ShapeDtypeStruct((2, out_rows, grid), F32)
    if cuts == 1 and wide:
        return pl.pallas_call(
            functools.partial(image_kernel, (n_z, n_x, n_c, per), wide_x),
            in_specs=[VMEM] * (quad + 1),
            out_specs=HELD,
            out_shape=out_shape,
            scratch_shapes=[
                pltpu.VMEM((2, out_rows, grid), F32),
                pltpu.SemaphoreType.DMA((grid // wide_x,)),
            ],
            name="image",
            **room,
        )(*near(*parts, cols))
    lines = factor([p.astype(F32) for p in parts], n_z, n_x, n_c, per).T
    re = lines[:, :all_pulses].reshape(out_rows, cuts, 1, group)
    im = lines[:, all_pulses:].reshape(out_rows, cuts, 1, group)
    lhs = jnp.stack(
        [jnp.concatenate([re, -im], axis=2), jnp.concatenate([im, re], axis=2)]
    ).reshape(2 * out_rows, depth).astype(BF16)
    return pl.pallas_call(
        image_plain,
        grid=(grid // wide_x,),
        in_specs=[
            pl.BlockSpec(lhs.shape, lambda i: (0, 0)),
            pl.BlockSpec((wide_x, depth), lambda i: (i, 0)),
        ],
        out_specs=pl.BlockSpec((2, out_rows, wide_x), lambda i: (0, 0, i)),
        out_shape=out_shape,
        name="image",
    )(lhs, cols)


def solution(mesh):
    placed = (
        P(None, ("groups", "pulse", "sub"), "range"),
        P("pulse", None, None),
        P(("groups", "pulse", "sub"), None),
        P(("groups", "pulse", "sub"), None),
    )
    return jax.shard_map(
        program,
        mesh=mesh,
        in_specs=placed,
        out_specs=P(None, ("groups", "pulse", "range", "sub"), None),
        check_vma=False,
    )
```

```python
import functools
import math

import jax
import jax.numpy as jnp
import numpy as np
from jax import lax
from jax.experimental import pallas as pl
from jax.experimental.pallas import tpu as pltpu
from jax.sharding import PartitionSpec as P


LANES = 128
F32 = jnp.float32
BF16 = jnp.bfloat16
VMEM = pl.BlockSpec(memory_space=pltpu.VMEM)
HELD = pl.BlockSpec(memory_space=pltpu.HBM)
NT = (((1,), (1,)), ((), ()))
NN = (((1,), (0,)), ((), ()))


def dot(a, b, dims=NN):
    return lax.dot_general(a, b, dims, preferred_element_type=F32)


def traded(block, axis, k):
    count = math.prod(lax.axis_size(a) for a in ((axis,) if isinstance(axis, str) else axis))
    return lax.ppermute(block, axis, [(i, i ^ k) for i in range(count)])


def near(*values):
    return [pltpu.with_memory_space_constraint(v, pltpu.VMEM) for v in values]


def far(*values):
    return [pltpu.with_memory_space_constraint(v, pltpu.HBM) for v in values]


def phasor(rows, cols, period, sign):
    turns = np.outer(rows, cols) % period
    angles = turns * (2.0 * math.pi / period)
    return np.cos(angles), sign * np.sin(angles)


def add(a, b):
    return b if a is None else a if b is None else a + b


def sub(a, b):
    return a if b is None else -b if a is None else a - b


def scaled(a, factor):
    return None if a is None else a * factor


def fourier(values, sign):
    count = len(values)
    if count == 1:
        return values
    even = fourier(values[0::2], sign)
    odd = fourier(values[1::2], sign)
    out = [None] * count
    for k in range(count // 2):
        er, ei = even[k]
        a, b = odd[k]
        if 4 * k == count:
            tr, ti = (sub(None, b), a) if sign > 0 else (b, sub(None, a))
        elif k == 0:
            tr, ti = a, b
        elif 8 * k in (count, 3 * count):
            h = math.sqrt(0.5)
            c = h if 8 * k == count else -h
            if sign < 0:
                b, a, c = a, b, c
                tr, ti = (sub(scaled(b, c), scaled(a, -h)), sub(scaled(a, c), scaled(b, h)))
            else:
                tr, ti = (sub(scaled(a, c), scaled(b, h)), add(scaled(a, h), scaled(b, c)))
        else:
            angle = sign * 2.0 * math.pi * k / count
            c, s = math.cos(angle), math.sin(angle)
            tr = sub(scaled(a, c), scaled(b, s))
            ti = add(scaled(a, s), scaled(b, c))
        out[k] = (add(er, tr), add(ei, ti))
        out[k + count // 2] = (sub(er, tr), sub(ei, ti))
    return out


def split_kernel(n_x, n_fixed, per, raw, taps_in, tile_in, first_in, *refs):
    fixed, refs = refs[:n_fixed], refs[n_fixed:]
    outs, refs = refs[:n_x], refs[n_x:]
    marked, first = refs[:2]
    brought, refs = refs[2 : n_fixed + 2], refs[n_fixed + 2 :]
    held, taps, tile, lines, sent = refs
    my_x = lax.axis_index("range")
    copies = [pltpu.make_async_copy(raw.at[c], held.at[c], sent.at[c]) for c in range(2)]
    copies.append(pltpu.make_async_copy(taps_in, taps, sent.at[2]))
    copies.append(pltpu.make_async_copy(tile_in, tile, sent.at[3]))
    copies.append(pltpu.make_async_copy(first_in.at[my_x], first, sent.at[4]))
    for i in range(n_fixed):
        copies.append(pltpu.make_async_copy(fixed[i], brought[i], sent.at[i + 5]))
    for copy in copies:
        copy.start()
    shard = raw.shape[1]
    tiles = raw.shape[2] // LANES
    width = taps.shape[1]
    copies[2].wait()
    copies[3].wait()
    row = lax.broadcasted_iota(jnp.int32, (per, LANES), 0)
    for k in range(n_x):
        rows = slice(k * per, (k + 1) * per)
        values = taps[:per, :].astype(F32)
        for x in range(1, n_x):
            pick = taps[x * per : (x + 1) * per, :].astype(F32)
            values = jnp.where((my_x ^ k) == x, pick, values)
        ids = jnp.zeros((per, LANES), jnp.int32)
        for p in range(per):
            ids = jnp.where(row == p, tile[0, (my_x ^ k) * per + p], ids)
        marked[rows, :width] = values.astype(BF16)
        marked[rows, width:] = ids.astype(F32).astype(BF16)
    for c in range(2):
        copies[c].wait()
        for t in range(tiles):
            lines[c, t * shard : (t + 1) * shard, :] = held[
                c, :, t * LANES : (t + 1) * LANES
            ].astype(F32)
        for k in range(n_x):
            for p in range(per):
                outs[k][c * tiles : (c + 1) * tiles, p * LANES : (p + 1) * LANES] = lines[
                    c, pl.ds((my_x ^ k) * per + p, tiles, stride=shard), :
                ].astype(BF16)
    for copy in copies[4:]:
        copy.wait()


def bring_kernel(n_fixed, turn, *refs):
    fixed, turned_in, brought, sent = refs[:n_fixed], refs[n_fixed], refs[n_fixed + 1 : -1], refs[-1]
    copies = [pltpu.make_async_copy(turn.at[lax.axis_index("pulse")], turned_in, sent.at[n_fixed])]
    for i in range(n_fixed):
        copies.append(pltpu.make_async_copy(fixed[i], brought[i], sent.at[i]))
    for copy in copies:
        copy.start()
    for copy in copies:
        copy.wait()


def pulse_kernel(n_parts, n_z, per, *refs):
    parts = refs[:n_parts]
    first, turn, second = refs[n_parts : n_parts + 3]
    outs = refs[n_parts + 3 :]
    my_z = lax.axis_index("pulse")
    mixed = dot(first[0], parts[0][...])
    for k in range(1, n_parts):
        mixed = mixed + dot(first[k], parts[k][...])
    half = mixed.shape[0] // 2
    band = LANES // n_z
    picks = []
    for k in range(n_z):
        for c in range(2):
            row = pl.multiple_of(c * LANES + (my_z ^ k) * band, band)
            picks.append(second[pl.ds(row, band), :])
    table = jnp.concatenate(picks, axis=0)
    tc, ts = turn[0], turn[1]
    for p in range(per):
        re = mixed[:half, p * LANES : (p + 1) * LANES]
        im = mixed[half:, p * LANES : (p + 1) * LANES]
        spun = jnp.concatenate([re * tc - im * ts, re * ts + im * tc], axis=1).astype(BF16)
        done = dot(table, spun, NT).astype(BF16)
        for k in range(n_z):
            outs[k][:, p * half : (p + 1) * half] = done[2 * band * k : 2 * band * (k + 1), :]


def line_kernel(n_z, per, blocks, quads, total_blocks, *refs):
    chunks = refs[:n_z]
    taps, turn, last = refs[n_z : n_z + 3]
    outs = refs[n_z + 3 : 2 * n_z + 3]
    bins, sums, rows = refs[2 * n_z + 3 :]
    my_z = lax.axis_index("pulse")
    band = blocks * quads
    pulses = n_z * per
    for k in range(n_z):
        for c in range(2):
            for p in range(per):
                at = ((c * n_z + k) * per + p) * band
                bins[at : at + band, :] = chunks[k][
                    c * band : (c + 1) * band, p * LANES : (p + 1) * LANES
                ].astype(F32)
    ky = []
    for b in range(blocks):
        lhs = jnp.concatenate(
            [bins[pl.ds(b * quads + q, 2 * pulses, stride=band), :].astype(BF16) for q in range(quads)],
            axis=1,
        )
        line = dot(lhs, taps[b])
        ky.append((line[:pulses], line[pulses:]))
    quarter = total_blocks // 4
    for y in range(quarter):
        classes = []
        for m in range(4):
            acc = None
            for b in range(m, blocks, 4):
                re, im = ky[b]
                angle = 2.0 * math.pi * (b * y % total_blocks) / total_blocks
                co, si = math.cos(angle), math.sin(angle)
                if b * y == 0:
                    term = (re, im)
                else:
                    term = (re * co - im * si, re * si + im * co)
                acc = term if acc is None else (acc[0] + term[0], acc[1] + term[1])
            if acc is None:
                acc = (jnp.zeros_like(ky[0][0]), jnp.zeros_like(ky[0][1]))
            classes.append(acc)
        for r, (re, im) in enumerate(fourier(classes, 1)):
            at = (y + r * quarter) * pulses
            sums[0, at : at + pulses, :] = re
            sums[1, at : at + pulses, :] = im
    fold = LANES // total_blocks
    tops = last.shape[0] // 2
    for m in range(pulses):
        gr = sums[0, pl.ds(m, total_blocks, stride=pulses), :]
        gi = sums[1, pl.ds(m, total_blocks, stride=pulses), :]
        spun = []
        for f in range(fold):
            tc = turn[0, f * total_blocks : (f + 1) * total_blocks, :]
            ts = turn[1, f * total_blocks : (f + 1) * total_blocks, :]
            spun.append(
                jnp.concatenate([gr * tc - gi * ts, gr * ts + gi * tc], axis=1).astype(BF16)
            )
        done = dot(last[...], jnp.concatenate(spun, axis=0), NT)
        for c in range(2):
            at = (c * pulses + m) * tops
            rows[at : at + tops, :] = done[c * tops : (c + 1) * tops, :]
    share = tops // n_z
    for k in range(n_z):
        for s in range(share):
            line = rows[pl.ds((my_z ^ k) * share + s, 2 * pulses, stride=tops), :]
            blocks_of = [
                line[c * pulses + (z ^ k) * per : c * pulses + (z ^ k) * per + per]
                for c in range(2)
                for z in range(n_z)
            ]
            outs[k][:, s * LANES : (s + 1) * LANES] = jnp.concatenate(blocks_of, axis=0).astype(BF16)


def fold_kernel(n_z, n_c, *refs):
    parts, outs, total = refs[:n_z], refs[n_z:-1], refs[-1]
    acc = parts[0][...].astype(F32)
    for part in parts[1:]:
        acc = acc + part[...].astype(F32)
    total[...] = acc.astype(BF16)
    mine = lax.axis_index("range") * n_c + lax.axis_index("sub")
    wide = outs[0].shape[1]
    for k, out in enumerate(outs):
        out[...] = total[:, pl.ds(pl.multiple_of((mine ^ k) * wide, wide), wide)]


def column_kernel(width, tile_cols, taps, table, turn, out, mixed, spread):
    pulses = taps.shape[0]
    low = mixed.shape[0]
    high = out.shape[0] // low
    steps = width // high
    step = 16
    for v in range(high // LANES):
        for r in range(0, pulses, step):
            tile = taps[r : r + step, width:].astype(F32)
            inside = [tile == float(t) for t in range(tile_cols)]
            values = []
            for t in range(tile_cols):
                for i in range(steps):
                    at = i * high + v * LANES
                    value = taps[r : r + step, at : at + LANES].astype(F32)
                    values.append((jnp.where(inside[t], value, 0.0), None))
            left, right = slice(v * LANES, (v + 1) * LANES), slice(high + v * LANES, high + (v + 1) * LANES)
            for d, (re, im) in enumerate(fourier(values, 1)):
                tc, ts = turn[0, d : d + 1, left], turn[1, d : d + 1, left]
                if im is None:
                    re, im = re * tc, re * ts
                else:
                    re, im = re * tc - im * ts, re * ts + im * tc
                mixed[d, r : r + step, left] = re.astype(BF16)
                mixed[d, r : r + step, right] = (-im).astype(BF16)
                mixed[d, pulses + r : pulses + r + step, left] = im.astype(BF16)
                mixed[d, pulses + r : pulses + r + step, right] = re.astype(BF16)
    for d in range(0, low, 2):
        both = jnp.concatenate([mixed[d], mixed[d + 1]], axis=0)
        done = dot(table[...], both, NT)
        spread[pl.ds(d, high, stride=low), :] = done[:, : 2 * pulses]
        spread[pl.ds(d + 1, high, stride=low), :] = done[:, 2 * pulses :]
    out[...] = spread[...].astype(BF16)


def turned(count):
    order, k = [0], count // 2
    while k > 0:
        order, k = order + [o ^ k for o in order], k // 2
    return order


def factor(parts, n_z, n_x, n_c, per):
    pulses = n_z * per
    out = []
    for comp in range(2):
        for c in turned(n_c):
            for z in turned(n_z):
                for x in range(n_x):
                    at = comp * pulses + z * per
                    out.append(parts[x * n_c + c][at : at + per, :])
    return jnp.concatenate(out, axis=0)


def image_kernel(dims, step, *refs):
    n_z, n_x, n_c, per = dims
    count = n_x * n_c
    parts = [ref[...].astype(F32) for ref in refs[:count]]
    cols, out, held, sent = refs[count:]
    lines = factor(parts, n_z, n_x, n_c, per).T
    half = lines.shape[1] // 2
    re, im = lines[:, :half], lines[:, half:]
    rows = lines.shape[0]
    lhs = jnp.concatenate(
        [jnp.concatenate([re, -im], axis=1), jnp.concatenate([im, re], axis=1)], axis=0
    ).astype(BF16)
    copies = []
    for i in range(cols.shape[0] // step):
        done = dot(lhs, cols[i * step : (i + 1) * step, :], NT)
        at = pl.ds(i * step, step)
        held[0, :, at] = done[:rows]
        held[1, :, at] = done[rows:]
        copies.append(pltpu.make_async_copy(held.at[:, :, at], out.at[:, :, at], sent.at[i]))
        copies[-1].start()
    for copy in copies:
        copy.wait()


def image_plain(lhs, cols, out):
    rows = out.shape[1]
    done = dot(lhs[...], cols[...], NT)
    out[0] = done[:rows]
    out[1] = done[rows:]


def table_of(values, dtype=BF16):
    return jnp.asarray(np.asarray(values, np.float32), dtype)


def complex_left(c, s, scale=1.0):
    return np.block([[c, -s], [s, c]]) * scale


def program(raw_echo, range_taps, azim_taps, tile_col):
    n_x, n_z, n_c = lax.axis_size("range"), lax.axis_size("pulse"), lax.axis_size("sub")
    my_x, my_c = lax.axis_index("range"), lax.axis_index("sub")
    shard, part = raw_echo.shape[1:]
    per = shard // n_x
    samples = part * n_x
    blocks, block_bins, block_rows = range_taps.shape
    total_blocks = blocks * n_z
    grid = total_blocks * block_rows
    width = azim_taps.shape[1]
    tile_cols = grid // width
    quad = n_x * n_c
    out_rows = grid // (n_z * quad)
    pulses = n_z * per
    wide = out_rows % LANES == 0
    room = {}
    if wide:
        room = {"compiler_params": pltpu.CompilerParams(vmem_limit_bytes=24 << 20)}

    high = samples // LANES
    tiles = high // n_x
    n128 = np.arange(LANES)
    nh = np.arange(high)
    first = complex_left(*phasor(nh, nh, high, -1.0)).reshape(2 * high, 2, n_x, tiles)
    first = [first[:, :, [x ^ k for k in range(n_x)]].transpose(2, 0, 1, 3) for x in range(n_x)]
    first = table_of(np.stack(first).reshape(n_x, n_x, 2 * high, 2 * tiles))
    turn1 = table_of(np.stack(phasor(nh, n128, samples, -1.0)), F32)
    second = table_of(complex_left(*phasor(n128, n128, LANES, -1.0), 1.0 / math.sqrt(samples)))
    tops = grid // LANES
    shift = grid // n_z
    turn2 = np.stack([np.stack(phasor(n128, n128 + shift * z, grid, 1.0)) for z in range(n_z)])
    turn2 = table_of(turn2, F32)
    c, s = phasor(np.arange(tops), n128, tops, 1.0)
    last = table_of(complex_left(c, s, 1.0 / math.sqrt(grid)))
    low = 16
    tall = grid // low
    nt = np.arange(tall)
    c, s = phasor(nt, nt, tall, 1.0)
    table = table_of(np.concatenate([c, s], axis=1) / math.sqrt(grid))
    turn3 = table_of(np.stack(phasor(np.arange(low), nt, grid, 1.0)), F32)

    piece = pltpu.VMEM((2 * tiles, per * LANES), BF16)
    fixed = (turn1, second)
    split = pl.pallas_call(
        functools.partial(split_kernel, n_x, len(fixed), per),
        in_specs=[HELD] * (4 + len(fixed)),
        out_specs=[VMEM] * (n_x + 2 + len(fixed)),
        out_shape=[piece] * n_x
        + [pltpu.VMEM((shard, width + LANES), BF16)]
        + [pltpu.VMEM(first.shape[1:], BF16)]
        + [pltpu.VMEM(f.shape, f.dtype) for f in fixed],
        scratch_shapes=[
            pltpu.VMEM(raw_echo.shape, BF16),
            pltpu.VMEM(azim_taps.shape, BF16),
            pltpu.SMEM((1, shard), jnp.int32),
            pltpu.VMEM((2, tiles * shard, LANES), F32),
            pltpu.SemaphoreType.DMA((5 + len(fixed),)),
        ],
        name="split",
        **room,
    )(*far(raw_echo, azim_taps, tile_col.T, first, *fixed))
    pieces, (marked, first, turn1, second) = split[:n_x], split[n_x:]
    parts = [pieces[0]]
    for k in range(1, n_x):
        parts.append(traded(pieces[k], "range", k))

    everyone = marked
    for axis, count in (("pulse", n_z), ("sub", n_c)):
        k = count // 2
        while k > 0:
            everyone = jnp.concatenate([everyone, traded(everyone, axis, k)], axis=0)
            k //= 2

    fixed = (last, range_taps, table, turn3)
    turn2, last, range_taps, table, turn3 = pl.pallas_call(
        functools.partial(bring_kernel, len(fixed)),
        in_specs=[HELD] * (1 + len(fixed)),
        out_specs=[VMEM] * (1 + len(fixed)),
        out_shape=[pltpu.VMEM(turn2.shape[1:], F32)]
        + [pltpu.VMEM(f.shape, f.dtype) for f in fixed],
        scratch_shapes=[pltpu.SemaphoreType.DMA((1 + len(fixed),))],
        name="bring",
        **room,
    )(*far(turn2, *fixed))

    band = LANES // n_z
    chunk = pltpu.VMEM((2 * band, per * high), BF16)
    chunks = pl.pallas_call(
        functools.partial(pulse_kernel, n_x, n_z, per),
        in_specs=[VMEM] * (n_x + 3),
        out_specs=[VMEM] * n_z,
        out_shape=[chunk] * n_z,
        name="pulse_transform",
        **room,
    )(*near(*parts, first, turn1, second))
    moved = [chunks[0]]
    for k in range(1, n_z):
        moved.append(traded(chunks[k], "pulse", k))

    group = 64
    all_pulses = n_c * n_z * shard
    cuts = all_pulses // group
    scratch = [
        pltpu.VMEM((low, 2 * group, 2 * tall), BF16),
        pltpu.VMEM((grid, 2 * group), F32),
    ]
    make = functools.partial(column_kernel, width, tile_cols)
    if cuts == 1:
        cols = pl.pallas_call(
            make,
            in_specs=[VMEM] * 3,
            out_specs=VMEM,
            out_shape=pltpu.VMEM((grid, 2 * group), BF16),
            scratch_shapes=scratch,
            name="column_transform",
            **room,
        )(*near(everyone, table, turn3))
    else:
        cols = pl.pallas_call(
            make,
            grid=(cuts,),
            in_specs=[
                pl.BlockSpec((group, width + LANES), lambda i: (i, 0)),
                pl.BlockSpec((tall, 2 * tall), lambda i: (0, 0)),
                pl.BlockSpec((2, low, tall), lambda i: (0, 0, 0)),
            ],
            out_specs=pl.BlockSpec((grid, 2 * group), lambda i: (0, i)),
            out_shape=jax.ShapeDtypeStruct((grid, 2 * all_pulses), BF16),
            scratch_shapes=scratch,
            name="column_transform",
        )(everyone, table, turn3)

    quads = block_bins // LANES
    lines = pl.pallas_call(
        functools.partial(line_kernel, n_z, per, blocks, quads, total_blocks),
        in_specs=[VMEM] * (n_z + 3),
        out_specs=[VMEM] * n_z,
        out_shape=[pltpu.VMEM((2 * pulses, grid // n_z), BF16)] * n_z,
        scratch_shapes=[
            pltpu.VMEM((2 * pulses * blocks * quads, LANES), F32),
            pltpu.VMEM((2, total_blocks * pulses, LANES), F32),
            pltpu.VMEM((2 * pulses * tops, LANES), F32),
        ],
        name="line_transform",
        **room,
    )(*near(*moved, range_taps, turn2, last))
    moved = [lines[0]]
    for k in range(1, n_z):
        moved.append(traded(lines[k], "pulse", k))
    if wide:
        pieces = pl.pallas_call(
            functools.partial(fold_kernel, n_z, n_c),
            in_specs=[VMEM] * n_z,
            out_specs=[VMEM] * quad,
            out_shape=[pltpu.VMEM((2 * pulses, out_rows), BF16)] * quad,
            scratch_shapes=[pltpu.VMEM((2 * pulses, grid // n_z), BF16)],
            name="fold",
            **room,
        )(*near(*moved))
    else:
        acc = sum(m.astype(F32) for m in moved).astype(BF16)
        mine = my_x * n_c + my_c
        pieces = [
            lax.dynamic_slice_in_dim(acc, (mine ^ k) * out_rows, out_rows, 1)
            for k in range(quad)
        ]
    parts = [pieces[0]]
    for k in range(1, quad):
        parts.append(traded(pieces[k], ("range", "sub"), k))

    wide_x = 512
    depth = 2 * all_pulses
    out_shape = jax.ShapeDtypeStruct((2, out_rows, grid), F32)
    if cuts == 1 and wide:
        return pl.pallas_call(
            functools.partial(image_kernel, (n_z, n_x, n_c, per), wide_x),
            in_specs=[VMEM] * (quad + 1),
            out_specs=HELD,
            out_shape=out_shape,
            scratch_shapes=[
                pltpu.VMEM((2, out_rows, grid), F32),
                pltpu.SemaphoreType.DMA((grid // wide_x,)),
            ],
            name="image",
            **room,
        )(*near(*parts, cols))
    lines = factor([p.astype(F32) for p in parts], n_z, n_x, n_c, per).T
    re = lines[:, :all_pulses].reshape(out_rows, cuts, 1, group)
    im = lines[:, all_pulses:].reshape(out_rows, cuts, 1, group)
    lhs = jnp.stack(
        [jnp.concatenate([re, -im], axis=2), jnp.concatenate([im, re], axis=2)]
    ).reshape(2 * out_rows, depth).astype(BF16)
    return pl.pallas_call(
        image_plain,
        grid=(grid // wide_x,),
        in_specs=[
            pl.BlockSpec(lhs.shape, lambda i: (0, 0)),
            pl.BlockSpec((wide_x, depth), lambda i: (i, 0)),
        ],
        out_specs=pl.BlockSpec((2, out_rows, wide_x), lambda i: (0, 0, i)),
        out_shape=out_shape,
        name="image",
    )(lhs, cols)


def solution(mesh):
    placed = (
        P(None, ("groups", "pulse", "sub"), "range"),
        P("pulse", None, None),
        P(("groups", "pulse", "sub"), None),
        P(("groups", "pulse", "sub"), None),
    )
    return jax.shard_map(
        program,
        mesh=mesh,
        in_specs=placed,
        out_specs=P(None, ("groups", "pulse", "range", "sub"), None),
        check_vma=False,
    )
```

```python
import functools
import math

import jax
import jax.numpy as jnp
import numpy as np
from jax import lax
from jax.experimental import pallas as pl
from jax.experimental.pallas import tpu as pltpu
from jax.sharding import PartitionSpec as P


LANES = 128
F32 = jnp.float32
BF16 = jnp.bfloat16
VMEM = pl.BlockSpec(memory_space=pltpu.VMEM)
HELD = pl.BlockSpec(memory_space=pltpu.HBM)
NT = (((1,), (1,)), ((), ()))
NN = (((1,), (0,)), ((), ()))


def dot(a, b, dims=NN):
    return lax.dot_general(a, b, dims, preferred_element_type=F32)


def traded(block, axis, k):
    count = math.prod(lax.axis_size(a) for a in ((axis,) if isinstance(axis, str) else axis))
    return lax.ppermute(block, axis, [(i, i ^ k) for i in range(count)])


def near(*values):
    return [pltpu.with_memory_space_constraint(v, pltpu.VMEM) for v in values]


def far(*values):
    return [pltpu.with_memory_space_constraint(v, pltpu.HBM) for v in values]


def phasor(rows, cols, period, sign):
    turns = np.outer(rows, cols) % period
    angles = turns * (2.0 * math.pi / period)
    return np.cos(angles), sign * np.sin(angles)


def add(a, b):
    return b if a is None else a if b is None else a + b


def sub(a, b):
    return a if b is None else -b if a is None else a - b


def scaled(a, factor):
    return None if a is None else a * factor


def fourier(values, sign):
    count = len(values)
    if count == 1:
        return values
    even = fourier(values[0::2], sign)
    odd = fourier(values[1::2], sign)
    out = [None] * count
    for k in range(count // 2):
        er, ei = even[k]
        a, b = odd[k]
        if 4 * k == count:
            tr, ti = (sub(None, b), a) if sign > 0 else (b, sub(None, a))
        elif k == 0:
            tr, ti = a, b
        elif 8 * k in (count, 3 * count):
            h = math.sqrt(0.5)
            c = h if 8 * k == count else -h
            if sign < 0:
                b, a, c = a, b, c
                tr, ti = (sub(scaled(b, c), scaled(a, -h)), sub(scaled(a, c), scaled(b, h)))
            else:
                tr, ti = (sub(scaled(a, c), scaled(b, h)), add(scaled(a, h), scaled(b, c)))
        else:
            angle = sign * 2.0 * math.pi * k / count
            c, s = math.cos(angle), math.sin(angle)
            tr = sub(scaled(a, c), scaled(b, s))
            ti = add(scaled(a, s), scaled(b, c))
        out[k] = (add(er, tr), add(ei, ti))
        out[k + count // 2] = (sub(er, tr), sub(ei, ti))
    return out


def split_kernel(n_x, per, raw, taps_in, tile_in, *refs):
    outs = refs[:n_x]
    marked, held, taps, tile, lines, sent = refs[n_x:]
    my_x = lax.axis_index("range")
    copies = [pltpu.make_async_copy(raw.at[c], held.at[c], sent.at[c]) for c in range(2)]
    copies.append(pltpu.make_async_copy(taps_in, taps, sent.at[2]))
    copies.append(pltpu.make_async_copy(tile_in, tile, sent.at[3]))
    for copy in copies:
        copy.start()
    shard = raw.shape[1]
    tiles = raw.shape[2] // LANES
    width = taps.shape[1]
    copies[2].wait()
    copies[3].wait()
    row = lax.broadcasted_iota(jnp.int32, (per, LANES), 0)
    for k in range(n_x):
        rows = slice(k * per, (k + 1) * per)
        values = taps[:per, :].astype(F32)
        for x in range(1, n_x):
            pick = taps[x * per : (x + 1) * per, :].astype(F32)
            values = jnp.where((my_x ^ k) == x, pick, values)
        ids = jnp.zeros((per, LANES), jnp.int32)
        for p in range(per):
            ids = jnp.where(row == p, tile[0, (my_x ^ k) * per + p], ids)
        marked[rows, :width] = values.astype(BF16)
        marked[rows, width:] = ids.astype(F32).astype(BF16)
    for c in range(2):
        copies[c].wait()
        for t in range(tiles):
            lines[c, t * shard : (t + 1) * shard, :] = held[
                c, :, t * LANES : (t + 1) * LANES
            ].astype(F32)
        for k in range(n_x):
            for p in range(per):
                outs[k][c * tiles : (c + 1) * tiles, p * LANES : (p + 1) * LANES] = lines[
                    c, pl.ds((my_x ^ k) * per + p, tiles, stride=shard), :
                ].astype(BF16)


def ready_kernel(n_fixed, own, first, *refs):
    fixed = refs[:n_fixed]
    part, rest = refs[n_fixed : n_fixed + 2]
    brought = refs[n_fixed + 2 : 2 * n_fixed + 2]
    mine, sent = refs[2 * n_fixed + 2 :]
    my_x = lax.axis_index("range")
    copies = [
        pltpu.make_async_copy(first.at[my_x, 0], mine, sent.at[0]),
        pltpu.make_async_copy(first.at[my_x, pl.ds(1, rest.shape[0])], rest, sent.at[1]),
    ]
    for i in range(n_fixed):
        copies.append(pltpu.make_async_copy(fixed[i], brought[i], sent.at[i + 2]))
    for copy in copies:
        copy.start()
    copies[0].wait()
    part[...] = dot(mine[...], own[...])
    for copy in copies[1:]:
        copy.wait()


def bring_kernel(n_fixed, turn, *refs):
    fixed, turned_in, brought, sent = refs[:n_fixed], refs[n_fixed], refs[n_fixed + 1 : -1], refs[-1]
    copies = [pltpu.make_async_copy(turn.at[lax.axis_index("pulse")], turned_in, sent.at[n_fixed])]
    for i in range(n_fixed):
        copies.append(pltpu.make_async_copy(fixed[i], brought[i], sent.at[i]))
    for copy in copies:
        copy.start()
    for copy in copies:
        copy.wait()


def pulse_kernel(n_parts, n_z, per, *refs):
    parts = refs[: n_parts - 1]
    mixed, first, turn, second = refs[n_parts - 1 : n_parts + 3]
    outs = refs[n_parts + 3 :]
    my_z = lax.axis_index("pulse")
    mixed = mixed[...]
    for k, part in enumerate(parts):
        mixed = mixed + dot(first[k], part[...])
    half = mixed.shape[0] // 2
    band = LANES // n_z
    picks = []
    for k in range(n_z):
        for c in range(2):
            row = pl.multiple_of(c * LANES + (my_z ^ k) * band, band)
            picks.append(second[pl.ds(row, band), :])
    table = jnp.concatenate(picks, axis=0)
    tc, ts = turn[0], turn[1]
    for p in range(per):
        re = mixed[:half, p * LANES : (p + 1) * LANES]
        im = mixed[half:, p * LANES : (p + 1) * LANES]
        spun = jnp.concatenate([re * tc - im * ts, re * ts + im * tc], axis=1).astype(BF16)
        done = dot(table, spun, NT).astype(BF16)
        for k in range(n_z):
            outs[k][:, p * half : (p + 1) * half] = done[2 * band * k : 2 * band * (k + 1), :]


def line_plain(n_z, per, blocks, quads, total_blocks, *refs):
    chunks = refs[:n_z]
    taps, turn, last = refs[n_z : n_z + 3]
    outs = refs[n_z + 3 : 2 * n_z + 3]
    bins, sums, rows = refs[2 * n_z + 3 :]
    my_z = lax.axis_index("pulse")
    band = blocks * quads
    pulses = n_z * per
    for k in range(n_z):
        for c in range(2):
            for p in range(per):
                at = ((c * n_z + k) * per + p) * band
                bins[at : at + band, :] = chunks[k][
                    c * band : (c + 1) * band, p * LANES : (p + 1) * LANES
                ].astype(F32)
    ky = []
    for b in range(blocks):
        lhs = jnp.concatenate(
            [bins[pl.ds(b * quads + q, 2 * pulses, stride=band), :].astype(BF16) for q in range(quads)],
            axis=1,
        )
        line = dot(lhs, taps[b])
        ky.append((line[:pulses], line[pulses:]))
    quarter = total_blocks // 4
    for y in range(quarter):
        classes = []
        for m in range(4):
            acc = None
            for b in range(m, blocks, 4):
                re, im = ky[b]
                angle = 2.0 * math.pi * (b * y % total_blocks) / total_blocks
                co, si = math.cos(angle), math.sin(angle)
                if b * y == 0:
                    term = (re, im)
                else:
                    term = (re * co - im * si, re * si + im * co)
                acc = term if acc is None else (acc[0] + term[0], acc[1] + term[1])
            if acc is None:
                acc = (jnp.zeros_like(ky[0][0]), jnp.zeros_like(ky[0][1]))
            classes.append(acc)
        for r, (re, im) in enumerate(fourier(classes, 1)):
            at = (y + r * quarter) * pulses
            sums[0, at : at + pulses, :] = re
            sums[1, at : at + pulses, :] = im
    fold = LANES // total_blocks
    tops = last.shape[0] // 2
    for m in range(pulses):
        gr = sums[0, pl.ds(m, total_blocks, stride=pulses), :]
        gi = sums[1, pl.ds(m, total_blocks, stride=pulses), :]
        spun = []
        for f in range(fold):
            tc = turn[0, f * total_blocks : (f + 1) * total_blocks, :]
            ts = turn[1, f * total_blocks : (f + 1) * total_blocks, :]
            spun.append(
                jnp.concatenate([gr * tc - gi * ts, gr * ts + gi * tc], axis=1).astype(BF16)
            )
        done = dot(last[...], jnp.concatenate(spun, axis=0), NT)
        for c in range(2):
            at = (c * pulses + m) * tops
            rows[at : at + tops, :] = done[c * tops : (c + 1) * tops, :]
    share = tops // n_z
    for k in range(n_z):
        for s in range(share):
            line = rows[pl.ds((my_z ^ k) * share + s, 2 * pulses, stride=tops), :]
            blocks_of = [
                line[c * pulses + (z ^ k) * per : c * pulses + (z ^ k) * per + per]
                for c in range(2)
                for z in range(n_z)
            ]
            outs[k][:, s * LANES : (s + 1) * LANES] = jnp.concatenate(blocks_of, axis=0).astype(BF16)


def swapped_rows(values):
    row = lax.broadcasted_iota(jnp.int32, values[0].shape, 0)
    for d in (4, 2, 1):
        lower = (row & d) == 0
        out = list(values)
        for i in range(8):
            if i & d == 0:
                a, b = values[i], values[i + d]
                out[i] = jnp.where(lower, a, pltpu.roll(b, d, 0))
                out[i + d] = jnp.where(lower, pltpu.roll(a, 8 - d, 0), b)
        values = out
    return values


def line_kernel(n_z, per, blocks, quads, total_blocks, *refs):
    chunks = refs[:n_z]
    taps, turn, last = refs[n_z : n_z + 3]
    outs = refs[n_z + 3 : 2 * n_z + 3]
    sums, spun, rows = refs[2 * n_z + 3 :]
    my_z = lax.axis_index("pulse")
    band = blocks * quads
    pulses = n_z * per
    ky = []
    for t in range(0, band, 16):
        groups = []
        for c in range(2):
            for g in range(0, pulses, 8):
                tiles = []
                for k, p in (divmod(m, per) for m in range(g, g + 8)):
                    tiles.append(
                        chunks[k][
                            c * band + t : c * band + t + 16, p * LANES : (p + 1) * LANES
                        ].astype(F32)
                    )
                groups.append(
                    swapped_rows([v[:8] for v in tiles]) + swapped_rows([v[8:] for v in tiles])
                )
        for b in range(16 // quads):
            lhs = jnp.concatenate(
                [
                    jnp.concatenate([g[b * quads + q] for g in groups], axis=0).astype(BF16)
                    for q in range(quads)
                ],
                axis=1,
            )
            line = dot(lhs, taps[t // quads + b])
            ky.append((line[:pulses], line[pulses:]))
    quarter = total_blocks // 4
    for y in range(quarter):
        classes = []
        for m in range(4):
            acc = None
            for b in range(m, blocks, 4):
                re, im = ky[b]
                angle = 2.0 * math.pi * (b * y % total_blocks) / total_blocks
                co, si = math.cos(angle), math.sin(angle)
                if b * y == 0:
                    term = (re, im)
                else:
                    term = (re * co - im * si, re * si + im * co)
                acc = term if acc is None else (acc[0] + term[0], acc[1] + term[1])
            classes.append(acc)
        for r, (re, im) in enumerate(fourier(classes, 1)):
            at = (y + r * quarter) * pulses
            sums[0, at : at + pulses, :] = re
            sums[1, at : at + pulses, :] = im
    fold = LANES // total_blocks
    for g in range(0, pulses, 8):
        for y in range(0, total_blocks, 16):
            parts = []
            for c in range(2):
                halves = [
                    swapped_rows(
                        [sums[c, u * pulses + g : u * pulses + g + 8, :] for u in range(h, h + 8)]
                    )
                    for h in (y, y + 8)
                ]
                parts.append([jnp.concatenate(pair, axis=0) for pair in zip(*halves)])
            for f in range(fold):
                at = slice(f * total_blocks + y, f * total_blocks + y + 16)
                tc, ts = turn[0, at, :], turn[1, at, :]
                for i in range(8):
                    re, im = parts[0][i], parts[1][i]
                    spun[g + i, at, :LANES] = (re * tc - im * ts).astype(BF16)
                    spun[g + i, at, LANES:] = (re * ts + im * tc).astype(BF16)
    tops = last.shape[0] // 2
    for m in range(pulses):
        done = dot(last[...], spun[m], NT)
        for c in range(2):
            at = (c * pulses + m) * tops
            rows[at : at + tops, :] = done[c * tops : (c + 1) * tops, :]
    share = tops // n_z
    for k in range(n_z):
        for s in range(0, share, 8):
            for c in range(2):
                groups = []
                for g in range(0, pulses, 8):
                    tiles = []
                    for z, p in (divmod(m, per) for m in range(g, g + 8)):
                        at = (c * pulses + (z ^ k) * per + p) * tops + s
                        at = pl.multiple_of(at + (my_z ^ k) * share, 8)
                        tiles.append(rows[pl.ds(at, 8), :])
                    groups.append(swapped_rows(tiles))
                for i in range(8):
                    outs[k][
                        c * pulses : (c + 1) * pulses, (s + i) * LANES : (s + i + 1) * LANES
                    ] = jnp.concatenate([g[i] for g in groups], axis=0).astype(BF16)


def fold_kernel(n_z, n_c, *refs):
    parts, outs, total = refs[:n_z], refs[n_z:-1], refs[-1]
    acc = parts[0][...].astype(F32)
    for part in parts[1:]:
        acc = acc + part[...].astype(F32)
    total[...] = acc.astype(BF16)
    mine = lax.axis_index("range") * n_c + lax.axis_index("sub")
    wide = outs[0].shape[1]
    for k, out in enumerate(outs):
        out[...] = total[:, pl.ds(pl.multiple_of((mine ^ k) * wide, wide), wide)]


def column_kernel(width, tile_cols, taps, table, turn, out, mixed, spread):
    pulses = taps.shape[0]
    low = mixed.shape[0]
    high = out.shape[0] // low
    steps = width // high
    step = 16
    for v in range(high // LANES):
        for r in range(0, pulses, step):
            tile = taps[r : r + step, width:].astype(F32)
            inside = [tile == float(t) for t in range(tile_cols)]
            values = []
            for t in range(tile_cols):
                for i in range(steps):
                    at = i * high + v * LANES
                    value = taps[r : r + step, at : at + LANES].astype(F32)
                    values.append((jnp.where(inside[t], value, 0.0), None))
            left, right = slice(v * LANES, (v + 1) * LANES), slice(high + v * LANES, high + (v + 1) * LANES)
            for d, (re, im) in enumerate(fourier(values, 1)):
                tc, ts = turn[0, d : d + 1, left], turn[1, d : d + 1, left]
                if im is None:
                    re, im = re * tc, re * ts
                else:
                    re, im = re * tc - im * ts, re * ts + im * tc
                mixed[d, r : r + step, left] = re.astype(BF16)
                mixed[d, r : r + step, right] = (-im).astype(BF16)
                mixed[d, pulses + r : pulses + r + step, left] = im.astype(BF16)
                mixed[d, pulses + r : pulses + r + step, right] = re.astype(BF16)
    for d in range(0, low, 2):
        both = jnp.concatenate([mixed[d], mixed[d + 1]], axis=0)
        done = dot(table[...], both, NT)
        spread[pl.ds(d, high, stride=low), :] = done[:, : 2 * pulses]
        spread[pl.ds(d + 1, high, stride=low), :] = done[:, 2 * pulses :]
    out[...] = spread[...].astype(BF16)


def turned(count):
    order, k = [0], count // 2
    while k > 0:
        order, k = order + [o ^ k for o in order], k // 2
    return order


def factor(parts, n_z, n_x, n_c, per):
    pulses = n_z * per
    out = []
    for comp in range(2):
        for c in turned(n_c):
            for z in turned(n_z):
                for x in range(n_x):
                    at = comp * pulses + z * per
                    out.append(parts[x * n_c + c][at : at + per, :])
    return jnp.concatenate(out, axis=0)


def image_kernel(dims, step, *refs):
    n_z, n_x, n_c, per = dims
    count = n_x * n_c
    parts = [ref[...].astype(F32) for ref in refs[:count]]
    cols, out, held, sent = refs[count:]
    lines = factor(parts, n_z, n_x, n_c, per).T
    half = lines.shape[1] // 2
    re, im = lines[:, :half], lines[:, half:]
    rows = lines.shape[0]
    lhs = jnp.concatenate(
        [jnp.concatenate([re, -im], axis=1), jnp.concatenate([im, re], axis=1)], axis=0
    ).astype(BF16)
    copies = []
    for i in range(cols.shape[0] // step):
        done = dot(lhs, cols[i * step : (i + 1) * step, :], NT)
        at = pl.ds(i * step, step)
        held[0, :, at] = done[:rows]
        held[1, :, at] = done[rows:]
        copies.append(pltpu.make_async_copy(held.at[:, :, at], out.at[:, :, at], sent.at[i]))
        copies[-1].start()
    for copy in copies:
        copy.wait()


def image_plain(lhs, cols, out):
    rows = out.shape[1]
    done = dot(lhs[...], cols[...], NT)
    out[0] = done[:rows]
    out[1] = done[rows:]


def table_of(values, dtype=BF16):
    return jnp.asarray(np.asarray(values, np.float32), dtype)


def complex_left(c, s, scale=1.0):
    return np.block([[c, -s], [s, c]]) * scale


def program(raw_echo, range_taps, azim_taps, tile_col):
    n_x, n_z, n_c = lax.axis_size("range"), lax.axis_size("pulse"), lax.axis_size("sub")
    my_x, my_c = lax.axis_index("range"), lax.axis_index("sub")
    shard, part = raw_echo.shape[1:]
    per = shard // n_x
    samples = part * n_x
    blocks, block_bins, block_rows = range_taps.shape
    total_blocks = blocks * n_z
    grid = total_blocks * block_rows
    width = azim_taps.shape[1]
    tile_cols = grid // width
    quad = n_x * n_c
    out_rows = grid // (n_z * quad)
    pulses = n_z * per
    wide = out_rows % LANES == 0
    room = {}
    if wide:
        room = {"compiler_params": pltpu.CompilerParams(vmem_limit_bytes=24 << 20)}

    high = samples // LANES
    tiles = high // n_x
    n128 = np.arange(LANES)
    nh = np.arange(high)
    first = complex_left(*phasor(nh, nh, high, -1.0)).reshape(2 * high, 2, n_x, tiles)
    first = [first[:, :, [x ^ k for k in range(n_x)]].transpose(2, 0, 1, 3) for x in range(n_x)]
    first = table_of(np.stack(first).reshape(n_x, n_x, 2 * high, 2 * tiles))
    turn1 = table_of(np.stack(phasor(nh, n128, samples, -1.0)), F32)
    second = table_of(complex_left(*phasor(n128, n128, LANES, -1.0), 1.0 / math.sqrt(samples)))
    tops = grid // LANES
    shift = grid // n_z
    turn2 = np.stack([np.stack(phasor(n128, n128 + shift * z, grid, 1.0)) for z in range(n_z)])
    turn2 = table_of(turn2, F32)
    c, s = phasor(np.arange(tops), n128, tops, 1.0)
    last = table_of(complex_left(c, s, 1.0 / math.sqrt(grid)))
    low = 16
    tall = grid // low
    nt = np.arange(tall)
    c, s = phasor(nt, nt, tall, 1.0)
    table = table_of(np.concatenate([c, s], axis=1) / math.sqrt(grid))
    turn3 = table_of(np.stack(phasor(np.arange(low), nt, grid, 1.0)), F32)

    piece = pltpu.VMEM((2 * tiles, per * LANES), BF16)
    *pieces, marked = pl.pallas_call(
        functools.partial(split_kernel, n_x, per),
        in_specs=[HELD] * 3,
        out_specs=[VMEM] * (n_x + 1),
        out_shape=[piece] * n_x + [pltpu.VMEM((shard, width + LANES), BF16)],
        scratch_shapes=[
            pltpu.VMEM(raw_echo.shape, BF16),
            pltpu.VMEM(azim_taps.shape, BF16),
            pltpu.SMEM((1, shard), jnp.int32),
            pltpu.VMEM((2, tiles * shard, LANES), F32),
            pltpu.SemaphoreType.DMA((4,)),
        ],
        name="split",
        **room,
    )(*far(raw_echo, azim_taps, tile_col.T))
    parts = []
    for k in range(1, n_x):
        parts.append(traded(pieces[k], "range", k))

    everyone = marked
    for axis, count in (("pulse", n_z), ("sub", n_c)):
        k = count // 2
        while k > 0:
            everyone = jnp.concatenate([everyone, traded(everyone, axis, k)], axis=0)
            k //= 2

    fixed = (turn1, second)
    part1, rest, turn1, second = pl.pallas_call(
        functools.partial(ready_kernel, len(fixed)),
        in_specs=[VMEM] + [HELD] * (1 + len(fixed)),
        out_specs=[VMEM] * (2 + len(fixed)),
        out_shape=[
            pltpu.VMEM((2 * high, per * LANES), F32),
            pltpu.VMEM((max(n_x - 1, 1), 2 * high, 2 * tiles), BF16),
        ]
        + [pltpu.VMEM(f.shape, f.dtype) for f in fixed],
        scratch_shapes=[
            pltpu.VMEM((2 * high, 2 * tiles), BF16),
            pltpu.SemaphoreType.DMA((2 + len(fixed),)),
        ],
        name="ready",
        **room,
    )(*near(pieces[0]), *far(first, *fixed))
    fixed = (last, range_taps, table, turn3)
    turn2, last, range_taps, table, turn3 = pl.pallas_call(
        functools.partial(bring_kernel, len(fixed)),
        in_specs=[HELD] * (1 + len(fixed)),
        out_specs=[VMEM] * (1 + len(fixed)),
        out_shape=[pltpu.VMEM(turn2.shape[1:], F32)]
        + [pltpu.VMEM(f.shape, f.dtype) for f in fixed],
        scratch_shapes=[pltpu.SemaphoreType.DMA((1 + len(fixed),))],
        name="bring",
        **room,
    )(*far(turn2, *fixed))

    band = LANES // n_z
    chunk = pltpu.VMEM((2 * band, per * high), BF16)
    chunks = pl.pallas_call(
        functools.partial(pulse_kernel, n_x, n_z, per),
        in_specs=[VMEM] * (n_x + 3),
        out_specs=[VMEM] * n_z,
        out_shape=[chunk] * n_z,
        name="pulse_transform",
        **room,
    )(*near(*parts, part1, rest, turn1, second))
    moved = [chunks[0]]
    for k in range(1, n_z):
        moved.append(traded(chunks[k], "pulse", k))

    group = 64
    all_pulses = n_c * n_z * shard
    cuts = all_pulses // group
    scratch = [
        pltpu.VMEM((low, 2 * group, 2 * tall), BF16),
        pltpu.VMEM((grid, 2 * group), F32),
    ]
    make = functools.partial(column_kernel, width, tile_cols)
    if cuts == 1:
        cols = pl.pallas_call(
            make,
            in_specs=[VMEM] * 3,
            out_specs=VMEM,
            out_shape=pltpu.VMEM((grid, 2 * group), BF16),
            scratch_shapes=scratch,
            name="column_transform",
            **room,
        )(*near(everyone, table, turn3))
    else:
        cols = pl.pallas_call(
            make,
            grid=(cuts,),
            in_specs=[
                pl.BlockSpec((group, width + LANES), lambda i: (i, 0)),
                pl.BlockSpec((tall, 2 * tall), lambda i: (0, 0)),
                pl.BlockSpec((2, low, tall), lambda i: (0, 0, 0)),
            ],
            out_specs=pl.BlockSpec((grid, 2 * group), lambda i: (0, i)),
            out_shape=jax.ShapeDtypeStruct((grid, 2 * all_pulses), BF16),
            scratch_shapes=scratch,
            name="column_transform",
        )(everyone, table, turn3)

    quads = block_bins // LANES
    paired = blocks >= 4 and blocks * quads % 16 == 0 and tops // n_z % 8 == 0 and pulses % 16 == 0
    if paired:
        line_make, first_scratch = line_kernel, []
        spun = [pltpu.VMEM((pulses, LANES, 2 * LANES), BF16)]
    else:
        line_make, spun = line_plain, []
        first_scratch = [pltpu.VMEM((2 * pulses * blocks * quads, LANES), F32)]
    lines = pl.pallas_call(
        functools.partial(line_make, n_z, per, blocks, quads, total_blocks),
        in_specs=[VMEM] * (n_z + 3),
        out_specs=[VMEM] * n_z,
        out_shape=[pltpu.VMEM((2 * pulses, grid // n_z), BF16)] * n_z,
        scratch_shapes=first_scratch
        + [pltpu.VMEM((2, total_blocks * pulses, LANES), F32)]
        + spun
        + [pltpu.VMEM((2 * pulses * tops, LANES), F32)],
        name="line_transform",
        **room,
    )(*near(*moved, range_taps, turn2, last))
    moved = [lines[0]]
    for k in range(1, n_z):
        moved.append(traded(lines[k], "pulse", k))
    if wide:
        pieces = pl.pallas_call(
            functools.partial(fold_kernel, n_z, n_c),
            in_specs=[VMEM] * n_z,
            out_specs=[VMEM] * quad,
            out_shape=[pltpu.VMEM((2 * pulses, out_rows), BF16)] * quad,
            scratch_shapes=[pltpu.VMEM((2 * pulses, grid // n_z), BF16)],
            name="fold",
            **room,
        )(*near(*moved))
    else:
        acc = sum(m.astype(F32) for m in moved).astype(BF16)
        mine = my_x * n_c + my_c
        pieces = [
            lax.dynamic_slice_in_dim(acc, (mine ^ k) * out_rows, out_rows, 1)
            for k in range(quad)
        ]
    parts = [pieces[0]]
    for k in range(1, quad):
        parts.append(traded(pieces[k], ("range", "sub"), k))

    wide_x = 512
    depth = 2 * all_pulses
    out_shape = jax.ShapeDtypeStruct((2, out_rows, grid), F32)
    if cuts == 1 and wide:
        return pl.pallas_call(
            functools.partial(image_kernel, (n_z, n_x, n_c, per), wide_x),
            in_specs=[VMEM] * (quad + 1),
            out_specs=HELD,
            out_shape=out_shape,
            scratch_shapes=[
                pltpu.VMEM((2, out_rows, grid), F32),
                pltpu.SemaphoreType.DMA((grid // wide_x,)),
            ],
            name="image",
            **room,
        )(*near(*parts, cols))
    lines = factor([p.astype(F32) for p in parts], n_z, n_x, n_c, per).T
    re = lines[:, :all_pulses].reshape(out_rows, cuts, 1, group)
    im = lines[:, all_pulses:].reshape(out_rows, cuts, 1, group)
    lhs = jnp.stack(
        [jnp.concatenate([re, -im], axis=2), jnp.concatenate([im, re], axis=2)]
    ).reshape(2 * out_rows, depth).astype(BF16)
    return pl.pallas_call(
        image_plain,
        grid=(grid // wide_x,),
        in_specs=[
            pl.BlockSpec(lhs.shape, lambda i: (0, 0)),
            pl.BlockSpec((wide_x, depth), lambda i: (i, 0)),
        ],
        out_specs=pl.BlockSpec((2, out_rows, wide_x), lambda i: (0, 0, i)),
        out_shape=out_shape,
        name="image",
    )(lhs, cols)


def solution(mesh):
    placed = (
        P(None, ("groups", "pulse", "sub"), "range"),
        P("pulse", None, None),
        P(("groups", "pulse", "sub"), None),
        P(("groups", "pulse", "sub"), None),
    )
    return jax.shard_map(
        program,
        mesh=mesh,
        in_specs=placed,
        out_specs=P(None, ("groups", "pulse", "range", "sub"), None),
        check_vma=False,
    )
```

```python
import functools
import math

import jax
import jax.numpy as jnp
import numpy as np
from jax import lax
from jax.experimental import pallas as pl
from jax.experimental.pallas import tpu as pltpu
from jax.sharding import PartitionSpec as P


LANES = 128
F32 = jnp.float32
BF16 = jnp.bfloat16
VMEM = pl.BlockSpec(memory_space=pltpu.VMEM)
HELD = pl.BlockSpec(memory_space=pltpu.HBM)
NT = (((1,), (1,)), ((), ()))
NN = (((1,), (0,)), ((), ()))


def dot(a, b, dims=NN):
    return lax.dot_general(a, b, dims, preferred_element_type=F32)


def traded(block, axis, k):
    count = math.prod(lax.axis_size(a) for a in ((axis,) if isinstance(axis, str) else axis))
    return lax.ppermute(block, axis, [(i, i ^ k) for i in range(count)])


def near(*values):
    return [pltpu.with_memory_space_constraint(v, pltpu.VMEM) for v in values]


def far(*values):
    return [pltpu.with_memory_space_constraint(v, pltpu.HBM) for v in values]


def phasor(rows, cols, period, sign):
    turns = np.outer(rows, cols) % period
    angles = turns * (2.0 * math.pi / period)
    return np.cos(angles), sign * np.sin(angles)


def add(a, b):
    return b if a is None else a if b is None else a + b


def sub(a, b):
    return a if b is None else -b if a is None else a - b


def scaled(a, factor):
    return None if a is None else a * factor


def fourier(values, sign):
    count = len(values)
    if count == 1:
        return values
    even = fourier(values[0::2], sign)
    odd = fourier(values[1::2], sign)
    out = [None] * count
    for k in range(count // 2):
        er, ei = even[k]
        a, b = odd[k]
        if 4 * k == count:
            tr, ti = (sub(None, b), a) if sign > 0 else (b, sub(None, a))
        elif k == 0:
            tr, ti = a, b
        elif 8 * k in (count, 3 * count):
            h = math.sqrt(0.5)
            c = h if 8 * k == count else -h
            if sign < 0:
                b, a, c = a, b, c
                tr, ti = (sub(scaled(b, c), scaled(a, -h)), sub(scaled(a, c), scaled(b, h)))
            else:
                tr, ti = (sub(scaled(a, c), scaled(b, h)), add(scaled(a, h), scaled(b, c)))
        else:
            angle = sign * 2.0 * math.pi * k / count
            c, s = math.cos(angle), math.sin(angle)
            tr = sub(scaled(a, c), scaled(b, s))
            ti = add(scaled(a, s), scaled(b, c))
        out[k] = (add(er, tr), add(ei, ti))
        out[k + count // 2] = (sub(er, tr), sub(ei, ti))
    return out


def split_kernel(n_x, per, raw, taps_in, tile_in, *refs):
    outs = refs[:n_x]
    marked, held, taps, tile, lines, sent = refs[n_x:]
    my_x = lax.axis_index("range")
    copies = [pltpu.make_async_copy(raw.at[c], held.at[c], sent.at[c]) for c in range(2)]
    copies.append(pltpu.make_async_copy(taps_in, taps, sent.at[2]))
    copies.append(pltpu.make_async_copy(tile_in, tile, sent.at[3]))
    for copy in copies:
        copy.start()
    shard = raw.shape[1]
    tiles = raw.shape[2] // LANES
    width = taps.shape[1]
    copies[2].wait()
    copies[3].wait()
    row = lax.broadcasted_iota(jnp.int32, (per, LANES), 0)
    for k in range(n_x):
        rows = slice(k * per, (k + 1) * per)
        values = taps[:per, :].astype(F32)
        for x in range(1, n_x):
            pick = taps[x * per : (x + 1) * per, :].astype(F32)
            values = jnp.where((my_x ^ k) == x, pick, values)
        ids = jnp.zeros((per, LANES), jnp.int32)
        for p in range(per):
            ids = jnp.where(row == p, tile[0, (my_x ^ k) * per + p], ids)
        marked[rows, :width] = values.astype(BF16)
        marked[rows, width:] = ids.astype(F32).astype(BF16)
    for c in range(2):
        copies[c].wait()
        for t in range(tiles):
            lines[c, t * shard : (t + 1) * shard, :] = held[
                c, :, t * LANES : (t + 1) * LANES
            ].astype(F32)
        for k in range(n_x):
            for p in range(per):
                outs[k][c * tiles : (c + 1) * tiles, p * LANES : (p + 1) * LANES] = lines[
                    c, pl.ds((my_x ^ k) * per + p, tiles, stride=shard), :
                ].astype(BF16)


def ready_kernel(n_fixed, own, first, *refs):
    fixed = refs[:n_fixed]
    part, rest = refs[n_fixed : n_fixed + 2]
    brought = refs[n_fixed + 2 : 2 * n_fixed + 2]
    mine, sent = refs[2 * n_fixed + 2 :]
    my_x = lax.axis_index("range")
    copies = [
        pltpu.make_async_copy(first.at[my_x, 0], mine, sent.at[0]),
        pltpu.make_async_copy(first.at[my_x, pl.ds(1, rest.shape[0])], rest, sent.at[1]),
    ]
    for i in range(n_fixed):
        copies.append(pltpu.make_async_copy(fixed[i], brought[i], sent.at[i + 2]))
    for copy in copies:
        copy.start()
    copies[0].wait()
    part[...] = dot(mine[...], own[...])
    for copy in copies[1:]:
        copy.wait()


def bring_kernel(n_fixed, turn, *refs):
    fixed, turned_in, brought, sent = refs[:n_fixed], refs[n_fixed], refs[n_fixed + 1 : -1], refs[-1]
    copies = [pltpu.make_async_copy(turn.at[lax.axis_index("pulse")], turned_in, sent.at[n_fixed])]
    for i in range(n_fixed):
        copies.append(pltpu.make_async_copy(fixed[i], brought[i], sent.at[i]))
    for copy in copies:
        copy.start()
    for copy in copies:
        copy.wait()


def pulse_kernel(n_parts, n_z, per, *refs):
    parts = refs[: n_parts - 1]
    mixed, first, turn, second = refs[n_parts - 1 : n_parts + 3]
    outs = refs[n_parts + 3 :]
    my_z = lax.axis_index("pulse")
    mixed = mixed[...]
    for k, part in enumerate(parts):
        mixed = mixed + dot(first[k], part[...])
    half = mixed.shape[0] // 2
    band = LANES // n_z
    picks = []
    for k in range(n_z):
        for c in range(2):
            row = pl.multiple_of(c * LANES + (my_z ^ k) * band, band)
            picks.append(second[pl.ds(row, band), :])
    table = jnp.concatenate(picks, axis=0)
    tc, ts = turn[0], turn[1]
    for p in range(per):
        re = mixed[:half, p * LANES : (p + 1) * LANES]
        im = mixed[half:, p * LANES : (p + 1) * LANES]
        spun = jnp.concatenate([re * tc - im * ts, re * ts + im * tc], axis=1).astype(BF16)
        done = dot(table, spun, NT).astype(BF16)
        for k in range(n_z):
            outs[k][:, p * half : (p + 1) * half] = done[2 * band * k : 2 * band * (k + 1), :]


def line_plain(n_z, per, blocks, quads, total_blocks, *refs):
    chunks = refs[:n_z]
    taps, turn, last = refs[n_z : n_z + 3]
    outs = refs[n_z + 3 : 2 * n_z + 3]
    bins, sums, rows = refs[2 * n_z + 3 :]
    my_z = lax.axis_index("pulse")
    band = blocks * quads
    pulses = n_z * per
    for k in range(n_z):
        for c in range(2):
            for p in range(per):
                at = ((c * n_z + k) * per + p) * band
                bins[at : at + band, :] = chunks[k][
                    c * band : (c + 1) * band, p * LANES : (p + 1) * LANES
                ].astype(F32)
    ky = []
    for b in range(blocks):
        lhs = jnp.concatenate(
            [bins[pl.ds(b * quads + q, 2 * pulses, stride=band), :].astype(BF16) for q in range(quads)],
            axis=1,
        )
        line = dot(lhs, taps[b])
        ky.append((line[:pulses], line[pulses:]))
    quarter = total_blocks // 4
    for y in range(quarter):
        classes = []
        for m in range(4):
            acc = None
            for b in range(m, blocks, 4):
                re, im = ky[b]
                angle = 2.0 * math.pi * (b * y % total_blocks) / total_blocks
                co, si = math.cos(angle), math.sin(angle)
                if b * y == 0:
                    term = (re, im)
                else:
                    term = (re * co - im * si, re * si + im * co)
                acc = term if acc is None else (acc[0] + term[0], acc[1] + term[1])
            if acc is None:
                acc = (jnp.zeros_like(ky[0][0]), jnp.zeros_like(ky[0][1]))
            classes.append(acc)
        for r, (re, im) in enumerate(fourier(classes, 1)):
            at = (y + r * quarter) * pulses
            sums[0, at : at + pulses, :] = re
            sums[1, at : at + pulses, :] = im
    fold = LANES // total_blocks
    tops = last.shape[0] // 2
    for m in range(pulses):
        gr = sums[0, pl.ds(m, total_blocks, stride=pulses), :]
        gi = sums[1, pl.ds(m, total_blocks, stride=pulses), :]
        spun = []
        for f in range(fold):
            tc = turn[0, f * total_blocks : (f + 1) * total_blocks, :]
            ts = turn[1, f * total_blocks : (f + 1) * total_blocks, :]
            spun.append(
                jnp.concatenate([gr * tc - gi * ts, gr * ts + gi * tc], axis=1).astype(BF16)
            )
        done = dot(last[...], jnp.concatenate(spun, axis=0), NT)
        for c in range(2):
            at = (c * pulses + m) * tops
            rows[at : at + tops, :] = done[c * tops : (c + 1) * tops, :]
    share = tops // n_z
    for k in range(n_z):
        for s in range(share):
            line = rows[pl.ds((my_z ^ k) * share + s, 2 * pulses, stride=tops), :]
            blocks_of = [
                line[c * pulses + (z ^ k) * per : c * pulses + (z ^ k) * per + per]
                for c in range(2)
                for z in range(n_z)
            ]
            outs[k][:, s * LANES : (s + 1) * LANES] = jnp.concatenate(blocks_of, axis=0).astype(BF16)


def swapped_rows(values):
    row = lax.broadcasted_iota(jnp.int32, values[0].shape, 0)
    for d in (4, 2, 1):
        lower = (row & d) == 0
        out = list(values)
        for i in range(8):
            if i & d == 0:
                a, b = values[i], values[i + d]
                out[i] = jnp.where(lower, a, pltpu.roll(b, d, 0))
                out[i + d] = jnp.where(lower, pltpu.roll(a, 8 - d, 0), b)
        values = out
    return values


def line_rows(chunks, per, blocks, quads, total_blocks, taps, turn, last, rows, sums, spun):
    band = blocks * quads
    pulses = len(chunks) * per
    ky = []
    for t in range(0, band, 16):
        groups = []
        for c in range(2):
            tiles = [
                chunk[c * band + t : c * band + t + 16, p * LANES : (p + 1) * LANES].astype(F32)
                for chunk in chunks
                for p in range(per)
            ]
            groups.append(
                swapped_rows([v[:8] for v in tiles]) + swapped_rows([v[8:] for v in tiles])
            )
        for b in range(16 // quads):
            lhs = jnp.concatenate(
                [
                    jnp.concatenate([g[b * quads + q] for g in groups], axis=0).astype(BF16)
                    for q in range(quads)
                ],
                axis=1,
            )
            line = dot(lhs, taps[t // quads + b])
            ky.append((line[:pulses], line[pulses:]))
    quarter = total_blocks // 4
    for y in range(quarter):
        classes = []
        for m in range(4):
            acc = None
            for b in range(m, blocks, 4):
                re, im = ky[b]
                angle = 2.0 * math.pi * (b * y % total_blocks) / total_blocks
                co, si = math.cos(angle), math.sin(angle)
                if b * y == 0:
                    term = (re, im)
                else:
                    term = (re * co - im * si, re * si + im * co)
                acc = term if acc is None else (acc[0] + term[0], acc[1] + term[1])
            classes.append(acc)
        for r, (re, im) in enumerate(fourier(classes, 1)):
            at = (y + r * quarter) * pulses
            sums[0, at : at + pulses, :] = re
            sums[1, at : at + pulses, :] = im
    for y in range(0, total_blocks, 16):
        parts = []
        for c in range(2):
            halves = [
                swapped_rows([sums[c, u * pulses : (u + 1) * pulses, :] for u in range(h, h + 8)])
                for h in (y, y + 8)
            ]
            parts.append([jnp.concatenate(pair, axis=0) for pair in zip(*halves)])
        for f in range(LANES // total_blocks):
            at = slice(f * total_blocks + y, f * total_blocks + y + 16)
            tc, ts = turn[0, at, :], turn[1, at, :]
            for i in range(pulses):
                re, im = parts[0][i], parts[1][i]
                spun[i, at, :LANES] = (re * tc - im * ts).astype(BF16)
                spun[i, at, LANES:] = (re * ts + im * tc).astype(BF16)
    tops = last.shape[0] // 2
    for m in range(pulses):
        done = dot(last[...], spun[m], NT)
        for c in range(2):
            at = (c * pulses + m) * tops
            rows[at : at + tops, :] = done[c * tops : (c + 1) * tops, :]


def cut_rows(n_z, per, tops, place, rows, k, group, c):
    half = len(place) * per
    share = tops // n_z
    base = (lax.axis_index("pulse") ^ k) * share
    lanes = []
    for s in range(0, share, 8):
        tiles = []
        for z in group:
            for p in range(per):
                at = (c * half + place.index(z ^ k) * per + p) * tops + s
                tiles.append(rows[pl.ds(pl.multiple_of(at + base, 8), 8), :])
        lanes += swapped_rows(tiles)
    return jnp.concatenate(lanes, axis=1).astype(BF16)


def line_head_kernel(n_z, dims, head, tail, one, two, taps, turn, last, early, sums, spun, rows):
    line_rows((one, two), *dims, taps, turn, last, rows, sums, spun)
    tops = last.shape[0] // 2
    for k in range(n_z):
        group = head if k in head else tail
        for c in range(2):
            early[k, c * 8 : (c + 1) * 8, :] = cut_rows(
                n_z, dims[0], tops, head, rows, k, group, c
            )


def line_tail_kernel(n_z, dims, head, tail, *refs):
    chunks, refs = refs[: len(tail)], refs[len(tail) :]
    taps, turn, last, early = refs[:4]
    outs = refs[4 : 4 + n_z]
    sums, spun, rows = refs[4 + n_z :]
    line_rows(chunks, *dims, taps, turn, last, rows, sums, spun)
    tops = last.shape[0] // 2
    for k in range(n_z):
        first = 0 if k in head else 8
        group = tail if k in head else head
        for c in range(2):
            at = c * 16 + first
            outs[k][at : at + 8, :] = early[k, c * 8 : (c + 1) * 8, :]
            at = c * 16 + 8 - first
            outs[k][at : at + 8, :] = cut_rows(n_z, dims[0], tops, tail, rows, k, group, c)


def fold_kernel(n_z, n_c, *refs):
    parts, outs, total = refs[:n_z], refs[n_z:-1], refs[-1]
    acc = parts[0][...].astype(F32)
    for part in parts[1:]:
        acc = acc + part[...].astype(F32)
    total[...] = acc.astype(BF16)
    mine = lax.axis_index("range") * n_c + lax.axis_index("sub")
    wide = outs[0].shape[1]
    for k, out in enumerate(outs):
        out[...] = total[:, pl.ds(pl.multiple_of((mine ^ k) * wide, wide), wide)]


def column_kernel(width, tile_cols, taps, table, turn, out, mixed, spread):
    pulses = taps.shape[0]
    low = mixed.shape[0]
    high = out.shape[0] // low
    steps = width // high
    step = 16
    for v in range(high // LANES):
        for r in range(0, pulses, step):
            tile = taps[r : r + step, width:].astype(F32)
            inside = [tile == float(t) for t in range(tile_cols)]
            values = []
            for t in range(tile_cols):
                for i in range(steps):
                    at = i * high + v * LANES
                    value = taps[r : r + step, at : at + LANES].astype(F32)
                    values.append((jnp.where(inside[t], value, 0.0), None))
            left, right = slice(v * LANES, (v + 1) * LANES), slice(high + v * LANES, high + (v + 1) * LANES)
            for d, (re, im) in enumerate(fourier(values, 1)):
                tc, ts = turn[0, d : d + 1, left], turn[1, d : d + 1, left]
                if im is None:
                    re, im = re * tc, re * ts
                else:
                    re, im = re * tc - im * ts, re * ts + im * tc
                mixed[d, r : r + step, left] = re.astype(BF16)
                mixed[d, r : r + step, right] = (-im).astype(BF16)
                mixed[d, pulses + r : pulses + r + step, left] = im.astype(BF16)
                mixed[d, pulses + r : pulses + r + step, right] = re.astype(BF16)
    for d in range(0, low, 2):
        both = jnp.concatenate([mixed[d], mixed[d + 1]], axis=0)
        done = dot(table[...], both, NT)
        spread[pl.ds(d, high, stride=low), :] = done[:, : 2 * pulses]
        spread[pl.ds(d + 1, high, stride=low), :] = done[:, 2 * pulses :]
    out[...] = spread[...].astype(BF16)


def turned(count):
    order, k = [0], count // 2
    while k > 0:
        order, k = order + [o ^ k for o in order], k // 2
    return order


def factor(parts, order, n_x, n_c, per):
    n_z = len(order)
    pulses = n_z * per
    out = []
    for comp in range(2):
        for c in turned(n_c):
            for z in turned(n_z):
                for x in range(n_x):
                    at = comp * pulses + order.index(z) * per
                    out.append(parts[x * n_c + c][at : at + per, :])
    return jnp.concatenate(out, axis=0)


def image_kernel(dims, step, *refs):
    order, n_x, n_c, per = dims
    count = n_x * n_c
    parts = [ref[...].astype(F32) for ref in refs[:count]]
    cols, out, held, sent = refs[count:]
    lines = factor(parts, order, n_x, n_c, per).T
    half = lines.shape[1] // 2
    re, im = lines[:, :half], lines[:, half:]
    rows = lines.shape[0]
    lhs = jnp.concatenate(
        [jnp.concatenate([re, -im], axis=1), jnp.concatenate([im, re], axis=1)], axis=0
    ).astype(BF16)
    copies = []
    for i in range(cols.shape[0] // step):
        done = dot(lhs, cols[i * step : (i + 1) * step, :], NT)
        at = pl.ds(i * step, step)
        held[0, :, at] = done[:rows]
        held[1, :, at] = done[rows:]
        copies.append(pltpu.make_async_copy(held.at[:, :, at], out.at[:, :, at], sent.at[i]))
        copies[-1].start()
    for copy in copies:
        copy.wait()


def image_plain(lhs, cols, out):
    rows = out.shape[1]
    done = dot(lhs[...], cols[...], NT)
    out[0] = done[:rows]
    out[1] = done[rows:]


def table_of(values, dtype=BF16):
    return jnp.asarray(np.asarray(values, np.float32), dtype)


def complex_left(c, s, scale=1.0):
    return np.block([[c, -s], [s, c]]) * scale


def program(raw_echo, range_taps, azim_taps, tile_col):
    n_x, n_z, n_c = lax.axis_size("range"), lax.axis_size("pulse"), lax.axis_size("sub")
    my_x, my_c = lax.axis_index("range"), lax.axis_index("sub")
    shard, part = raw_echo.shape[1:]
    per = shard // n_x
    samples = part * n_x
    blocks, block_bins, block_rows = range_taps.shape
    total_blocks = blocks * n_z
    grid = total_blocks * block_rows
    width = azim_taps.shape[1]
    tile_cols = grid // width
    quad = n_x * n_c
    out_rows = grid // (n_z * quad)
    pulses = n_z * per
    wide = out_rows % LANES == 0
    room = {}
    if wide:
        room = {"compiler_params": pltpu.CompilerParams(vmem_limit_bytes=24 << 20)}

    high = samples // LANES
    tiles = high // n_x
    n128 = np.arange(LANES)
    nh = np.arange(high)
    first = complex_left(*phasor(nh, nh, high, -1.0)).reshape(2 * high, 2, n_x, tiles)
    first = [first[:, :, [x ^ k for k in range(n_x)]].transpose(2, 0, 1, 3) for x in range(n_x)]
    first = table_of(np.stack(first).reshape(n_x, n_x, 2 * high, 2 * tiles))
    turn1 = table_of(np.stack(phasor(nh, n128, samples, -1.0)), F32)
    second = table_of(complex_left(*phasor(n128, n128, LANES, -1.0), 1.0 / math.sqrt(samples)))
    tops = grid // LANES
    shift = grid // n_z
    turn2 = np.stack([np.stack(phasor(n128, n128 + shift * z, grid, 1.0)) for z in range(n_z)])
    turn2 = table_of(turn2, F32)
    c, s = phasor(np.arange(tops), n128, tops, 1.0)
    last = table_of(complex_left(c, s, 1.0 / math.sqrt(grid)))
    low = 16
    tall = grid // low
    nt = np.arange(tall)
    c, s = phasor(nt, nt, tall, 1.0)
    table = table_of(np.concatenate([c, s], axis=1) / math.sqrt(grid))
    turn3 = table_of(np.stack(phasor(np.arange(low), nt, grid, 1.0)), F32)

    piece = pltpu.VMEM((2 * tiles, per * LANES), BF16)
    *pieces, marked = pl.pallas_call(
        functools.partial(split_kernel, n_x, per),
        in_specs=[HELD] * 3,
        out_specs=[VMEM] * (n_x + 1),
        out_shape=[piece] * n_x + [pltpu.VMEM((shard, width + LANES), BF16)],
        scratch_shapes=[
            pltpu.VMEM(raw_echo.shape, BF16),
            pltpu.VMEM(azim_taps.shape, BF16),
            pltpu.SMEM((1, shard), jnp.int32),
            pltpu.VMEM((2, tiles * shard, LANES), F32),
            pltpu.SemaphoreType.DMA((4,)),
        ],
        name="split",
        **room,
    )(*far(raw_echo, azim_taps, tile_col.T))
    parts = []
    for k in range(1, n_x):
        parts.append(traded(pieces[k], "range", k))

    everyone = marked
    for axis, count in (("pulse", n_z), ("sub", n_c)):
        k = count // 2
        while k > 0:
            everyone = jnp.concatenate([everyone, traded(everyone, axis, k)], axis=0)
            k //= 2

    fixed = (turn1, second)
    part1, rest, turn1, second = pl.pallas_call(
        functools.partial(ready_kernel, len(fixed)),
        in_specs=[VMEM] + [HELD] * (1 + len(fixed)),
        out_specs=[VMEM] * (2 + len(fixed)),
        out_shape=[
            pltpu.VMEM((2 * high, per * LANES), F32),
            pltpu.VMEM((max(n_x - 1, 1), 2 * high, 2 * tiles), BF16),
        ]
        + [pltpu.VMEM(f.shape, f.dtype) for f in fixed],
        scratch_shapes=[
            pltpu.VMEM((2 * high, 2 * tiles), BF16),
            pltpu.SemaphoreType.DMA((2 + len(fixed),)),
        ],
        name="ready",
        **room,
    )(*near(pieces[0]), *far(first, *fixed))
    fixed = (last, range_taps, table, turn3)
    turn2, last, range_taps, table, turn3 = pl.pallas_call(
        functools.partial(bring_kernel, len(fixed)),
        in_specs=[HELD] * (1 + len(fixed)),
        out_specs=[VMEM] * (1 + len(fixed)),
        out_shape=[pltpu.VMEM(turn2.shape[1:], F32)]
        + [pltpu.VMEM(f.shape, f.dtype) for f in fixed],
        scratch_shapes=[pltpu.SemaphoreType.DMA((1 + len(fixed),))],
        name="bring",
        **room,
    )(*far(turn2, *fixed))

    band = LANES // n_z
    chunk = pltpu.VMEM((2 * band, per * high), BF16)
    chunks = pl.pallas_call(
        functools.partial(pulse_kernel, n_x, n_z, per),
        in_specs=[VMEM] * (n_x + 3),
        out_specs=[VMEM] * n_z,
        out_shape=[chunk] * n_z,
        name="pulse_transform",
        **room,
    )(*near(*parts, part1, rest, turn1, second))
    moved = [chunks[0]]
    for k in range(1, n_z):
        moved.append(traded(chunks[k], "pulse", k))

    group = 64
    all_pulses = n_c * n_z * shard
    cuts = all_pulses // group
    scratch = [
        pltpu.VMEM((low, 2 * group, 2 * tall), BF16),
        pltpu.VMEM((grid, 2 * group), F32),
    ]
    make = functools.partial(column_kernel, width, tile_cols)
    if cuts == 1:
        cols = pl.pallas_call(
            make,
            in_specs=[VMEM] * 3,
            out_specs=VMEM,
            out_shape=pltpu.VMEM((grid, 2 * group), BF16),
            scratch_shapes=scratch,
            name="column_transform",
            **room,
        )(*near(everyone, table, turn3))
    else:
        cols = pl.pallas_call(
            make,
            grid=(cuts,),
            in_specs=[
                pl.BlockSpec((group, width + LANES), lambda i: (i, 0)),
                pl.BlockSpec((tall, 2 * tall), lambda i: (0, 0)),
                pl.BlockSpec((2, low, tall), lambda i: (0, 0, 0)),
            ],
            out_specs=pl.BlockSpec((grid, 2 * group), lambda i: (0, i)),
            out_shape=jax.ShapeDtypeStruct((grid, 2 * all_pulses), BF16),
            scratch_shapes=scratch,
            name="column_transform",
        )(everyone, table, turn3)

    quads = block_bins // LANES
    paired = n_z == 4 and per == 4 and blocks >= 4 and blocks * quads % 16 == 0 and tops % 32 == 0
    out_lines = [pltpu.VMEM((2 * pulses, grid // n_z), BF16)] * n_z
    order = tuple(range(n_z))
    if paired:
        head, tail = (0, 2), (1, 3)
        order = head + tail
        dims = (per, blocks, quads, total_blocks)
        scratch = [
            pltpu.VMEM((2, total_blocks * pulses // 2, LANES), F32),
            pltpu.VMEM((pulses // 2, LANES, 2 * LANES), BF16),
            pltpu.VMEM((pulses * tops, LANES), F32),
        ]
        early_rows = pl.pallas_call(
            functools.partial(line_head_kernel, n_z, dims, head, tail),
            in_specs=[VMEM] * 5,
            out_specs=VMEM,
            out_shape=pltpu.VMEM((n_z, pulses, grid // n_z), BF16),
            scratch_shapes=scratch,
            name="line_head",
            **room,
        )(*near(*(moved[k] for k in head), range_taps, turn2, last))
        lines = pl.pallas_call(
            functools.partial(line_tail_kernel, n_z, dims, head, tail),
            in_specs=[VMEM] * 6,
            out_specs=[VMEM] * n_z,
            out_shape=out_lines,
            scratch_shapes=scratch,
            name="line_tail",
            **room,
        )(*near(*(moved[k] for k in tail), range_taps, turn2, last, early_rows))
    else:
        lines = pl.pallas_call(
            functools.partial(line_plain, n_z, per, blocks, quads, total_blocks),
            in_specs=[VMEM] * (n_z + 3),
            out_specs=[VMEM] * n_z,
            out_shape=out_lines,
            scratch_shapes=[
                pltpu.VMEM((2 * pulses * blocks * quads, LANES), F32),
                pltpu.VMEM((2, total_blocks * pulses, LANES), F32),
                pltpu.VMEM((2 * pulses * tops, LANES), F32),
            ],
            name="line_transform",
            **room,
        )(*near(*moved, range_taps, turn2, last))
    moved = [lines[0]]
    for k in range(1, n_z):
        moved.append(traded(lines[k], "pulse", k))
    if wide:
        pieces = pl.pallas_call(
            functools.partial(fold_kernel, n_z, n_c),
            in_specs=[VMEM] * n_z,
            out_specs=[VMEM] * quad,
            out_shape=[pltpu.VMEM((2 * pulses, out_rows), BF16)] * quad,
            scratch_shapes=[pltpu.VMEM((2 * pulses, grid // n_z), BF16)],
            name="fold",
            **room,
        )(*near(*moved))
    else:
        acc = sum(m.astype(F32) for m in moved).astype(BF16)
        mine = my_x * n_c + my_c
        pieces = [
            lax.dynamic_slice_in_dim(acc, (mine ^ k) * out_rows, out_rows, 1)
            for k in range(quad)
        ]
    parts = [pieces[0]]
    for k in range(1, quad):
        parts.append(traded(pieces[k], ("range", "sub"), k))

    wide_x = 512
    depth = 2 * all_pulses
    out_shape = jax.ShapeDtypeStruct((2, out_rows, grid), F32)
    if cuts == 1 and wide:
        return pl.pallas_call(
            functools.partial(image_kernel, (order, n_x, n_c, per), wide_x),
            in_specs=[VMEM] * (quad + 1),
            out_specs=HELD,
            out_shape=out_shape,
            scratch_shapes=[
                pltpu.VMEM((2, out_rows, grid), F32),
                pltpu.SemaphoreType.DMA((grid // wide_x,)),
            ],
            name="image",
            **room,
        )(*near(*parts, cols))
    lines = factor([p.astype(F32) for p in parts], order, n_x, n_c, per).T
    re = lines[:, :all_pulses].reshape(out_rows, cuts, 1, group)
    im = lines[:, all_pulses:].reshape(out_rows, cuts, 1, group)
    lhs = jnp.stack(
        [jnp.concatenate([re, -im], axis=2), jnp.concatenate([im, re], axis=2)]
    ).reshape(2 * out_rows, depth).astype(BF16)
    return pl.pallas_call(
        image_plain,
        grid=(grid // wide_x,),
        in_specs=[
            pl.BlockSpec(lhs.shape, lambda i: (0, 0)),
            pl.BlockSpec((wide_x, depth), lambda i: (i, 0)),
        ],
        out_specs=pl.BlockSpec((2, out_rows, wide_x), lambda i: (0, 0, i)),
        out_shape=out_shape,
        name="image",
    )(lhs, cols)


def solution(mesh):
    placed = (
        P(None, ("groups", "pulse", "sub"), "range"),
        P("pulse", None, None),
        P(("groups", "pulse", "sub"), None),
        P(("groups", "pulse", "sub"), None),
    )
    return jax.shard_map(
        program,
        mesh=mesh,
        in_specs=placed,
        out_specs=P(None, ("groups", "pulse", "range", "sub"), None),
        check_vma=False,
    )
```

```python
import functools
import math

import jax
import jax.numpy as jnp
import numpy as np
from jax import lax
from jax.experimental import pallas as pl
from jax.experimental.pallas import tpu as pltpu
from jax.sharding import PartitionSpec as P


LANES = 128
F32 = jnp.float32
BF16 = jnp.bfloat16
VMEM = pl.BlockSpec(memory_space=pltpu.VMEM)
HELD = pl.BlockSpec(memory_space=pltpu.HBM)
NT = (((1,), (1,)), ((), ()))
NN = (((1,), (0,)), ((), ()))


def dot(a, b, dims=NN):
    return lax.dot_general(a, b, dims, preferred_element_type=F32)


def traded(block, axis, k):
    count = math.prod(lax.axis_size(a) for a in ((axis,) if isinstance(axis, str) else axis))
    return lax.ppermute(block, axis, [(i, i ^ k) for i in range(count)])


def near(*values):
    return [pltpu.with_memory_space_constraint(v, pltpu.VMEM) for v in values]


def far(*values):
    return [pltpu.with_memory_space_constraint(v, pltpu.HBM) for v in values]


def phasor(rows, cols, period, sign):
    turns = np.outer(rows, cols) % period
    angles = turns * (2.0 * math.pi / period)
    return np.cos(angles), sign * np.sin(angles)


def add(a, b):
    return b if a is None else a if b is None else a + b


def sub(a, b):
    return a if b is None else -b if a is None else a - b


def scaled(a, factor):
    return None if a is None else a * factor


def fourier(values, sign):
    count = len(values)
    if count == 1:
        return values
    even = fourier(values[0::2], sign)
    odd = fourier(values[1::2], sign)
    out = [None] * count
    for k in range(count // 2):
        er, ei = even[k]
        a, b = odd[k]
        if 4 * k == count:
            tr, ti = (sub(None, b), a) if sign > 0 else (b, sub(None, a))
        elif k == 0:
            tr, ti = a, b
        elif 8 * k in (count, 3 * count):
            h = math.sqrt(0.5)
            c = h if 8 * k == count else -h
            if sign < 0:
                b, a, c = a, b, c
                tr, ti = (sub(scaled(b, c), scaled(a, -h)), sub(scaled(a, c), scaled(b, h)))
            else:
                tr, ti = (sub(scaled(a, c), scaled(b, h)), add(scaled(a, h), scaled(b, c)))
        else:
            angle = sign * 2.0 * math.pi * k / count
            c, s = math.cos(angle), math.sin(angle)
            tr = sub(scaled(a, c), scaled(b, s))
            ti = add(scaled(a, s), scaled(b, c))
        out[k] = (add(er, tr), add(ei, ti))
        out[k + count // 2] = (sub(er, tr), sub(ei, ti))
    return out


def split_kernel(n_x, per, raw, taps_in, tile_in, *refs):
    outs = refs[:n_x]
    marked, held, taps, tile, lines, sent = refs[n_x:]
    my_x = lax.axis_index("range")
    copies = [pltpu.make_async_copy(raw.at[c], held.at[c], sent.at[c]) for c in range(2)]
    copies.append(pltpu.make_async_copy(taps_in, taps, sent.at[2]))
    copies.append(pltpu.make_async_copy(tile_in, tile, sent.at[3]))
    for copy in copies:
        copy.start()
    shard = raw.shape[1]
    tiles = raw.shape[2] // LANES
    width = taps.shape[1]
    copies[2].wait()
    copies[3].wait()
    row = lax.broadcasted_iota(jnp.int32, (per, LANES), 0)
    for k in range(n_x):
        rows = slice(k * per, (k + 1) * per)
        values = taps[:per, :].astype(F32)
        for x in range(1, n_x):
            pick = taps[x * per : (x + 1) * per, :].astype(F32)
            values = jnp.where((my_x ^ k) == x, pick, values)
        ids = jnp.zeros((per, LANES), jnp.int32)
        for p in range(per):
            ids = jnp.where(row == p, tile[0, (my_x ^ k) * per + p], ids)
        marked[rows, :width] = values.astype(BF16)
        marked[rows, width:] = ids.astype(F32).astype(BF16)
    for c in range(2):
        copies[c].wait()
        for t in range(tiles):
            lines[c, t * shard : (t + 1) * shard, :] = held[
                c, :, t * LANES : (t + 1) * LANES
            ].astype(F32)
        for k in range(n_x):
            for p in range(per):
                outs[k][c * tiles : (c + 1) * tiles, p * LANES : (p + 1) * LANES] = lines[
                    c, pl.ds((my_x ^ k) * per + p, tiles, stride=shard), :
                ].astype(BF16)


def ready_kernel(n_fixed, own, first, *refs):
    fixed = refs[:n_fixed]
    part, rest = refs[n_fixed : n_fixed + 2]
    brought = refs[n_fixed + 2 : 2 * n_fixed + 2]
    mine, sent = refs[2 * n_fixed + 2 :]
    my_x = lax.axis_index("range")
    copies = [
        pltpu.make_async_copy(first.at[my_x, 0], mine, sent.at[0]),
        pltpu.make_async_copy(first.at[my_x, pl.ds(1, rest.shape[0])], rest, sent.at[1]),
    ]
    for i in range(n_fixed):
        copies.append(pltpu.make_async_copy(fixed[i], brought[i], sent.at[i + 2]))
    for copy in copies:
        copy.start()
    copies[0].wait()
    part[...] = dot(mine[...], own[...])
    for copy in copies[1:]:
        copy.wait()


def bring_kernel(n_fixed, turn, *refs):
    fixed, turned_in, brought, sent = refs[:n_fixed], refs[n_fixed], refs[n_fixed + 1 : -1], refs[-1]
    copies = [pltpu.make_async_copy(turn.at[lax.axis_index("pulse")], turned_in, sent.at[n_fixed])]
    for i in range(n_fixed):
        copies.append(pltpu.make_async_copy(fixed[i], brought[i], sent.at[i]))
    for copy in copies:
        copy.start()
    for copy in copies:
        copy.wait()


def pulse_kernel(n_parts, n_z, per, *refs):
    parts = refs[: n_parts - 1]
    mixed, first, turn, second = refs[n_parts - 1 : n_parts + 3]
    outs = refs[n_parts + 3 :]
    my_z = lax.axis_index("pulse")
    mixed = mixed[...]
    for k, part in enumerate(parts):
        mixed = mixed + dot(first[k], part[...])
    half = mixed.shape[0] // 2
    band = LANES // n_z
    picks = []
    for k in range(n_z):
        for c in range(2):
            row = pl.multiple_of(c * LANES + (my_z ^ k) * band, band)
            picks.append(second[pl.ds(row, band), :])
    table = jnp.concatenate(picks, axis=0)
    tc, ts = turn[0], turn[1]
    for p in range(per):
        re = mixed[:half, p * LANES : (p + 1) * LANES]
        im = mixed[half:, p * LANES : (p + 1) * LANES]
        spun = jnp.concatenate([re * tc - im * ts, re * ts + im * tc], axis=1).astype(BF16)
        done = dot(table, spun, NT).astype(BF16)
        for k in range(n_z):
            outs[k][:, p * half : (p + 1) * half] = done[2 * band * k : 2 * band * (k + 1), :]


def line_plain(n_z, per, blocks, quads, total_blocks, *refs):
    chunks = refs[:n_z]
    taps, turn, last = refs[n_z : n_z + 3]
    outs = refs[n_z + 3 : 2 * n_z + 3]
    bins, sums, rows = refs[2 * n_z + 3 :]
    my_z = lax.axis_index("pulse")
    band = blocks * quads
    pulses = n_z * per
    for k in range(n_z):
        for c in range(2):
            for p in range(per):
                at = ((c * n_z + k) * per + p) * band
                bins[at : at + band, :] = chunks[k][
                    c * band : (c + 1) * band, p * LANES : (p + 1) * LANES
                ].astype(F32)
    ky = []
    for b in range(blocks):
        lhs = jnp.concatenate(
            [bins[pl.ds(b * quads + q, 2 * pulses, stride=band), :].astype(BF16) for q in range(quads)],
            axis=1,
        )
        line = dot(lhs, taps[b])
        ky.append((line[:pulses], line[pulses:]))
    quarter = total_blocks // 4
    for y in range(quarter):
        classes = []
        for m in range(4):
            acc = None
            for b in range(m, blocks, 4):
                re, im = ky[b]
                angle = 2.0 * math.pi * (b * y % total_blocks) / total_blocks
                co, si = math.cos(angle), math.sin(angle)
                if b * y == 0:
                    term = (re, im)
                else:
                    term = (re * co - im * si, re * si + im * co)
                acc = term if acc is None else (acc[0] + term[0], acc[1] + term[1])
            if acc is None:
                acc = (jnp.zeros_like(ky[0][0]), jnp.zeros_like(ky[0][1]))
            classes.append(acc)
        for r, (re, im) in enumerate(fourier(classes, 1)):
            at = (y + r * quarter) * pulses
            sums[0, at : at + pulses, :] = re
            sums[1, at : at + pulses, :] = im
    fold = LANES // total_blocks
    tops = last.shape[0] // 2
    for m in range(pulses):
        gr = sums[0, pl.ds(m, total_blocks, stride=pulses), :]
        gi = sums[1, pl.ds(m, total_blocks, stride=pulses), :]
        spun = []
        for f in range(fold):
            tc = turn[0, f * total_blocks : (f + 1) * total_blocks, :]
            ts = turn[1, f * total_blocks : (f + 1) * total_blocks, :]
            spun.append(
                jnp.concatenate([gr * tc - gi * ts, gr * ts + gi * tc], axis=1).astype(BF16)
            )
        done = dot(last[...], jnp.concatenate(spun, axis=0), NT)
        for c in range(2):
            at = (c * pulses + m) * tops
            rows[at : at + tops, :] = done[c * tops : (c + 1) * tops, :]
    share = tops // n_z
    for k in range(n_z):
        for s in range(share):
            line = rows[pl.ds((my_z ^ k) * share + s, 2 * pulses, stride=tops), :]
            blocks_of = [
                line[c * pulses + (z ^ k) * per : c * pulses + (z ^ k) * per + per]
                for c in range(2)
                for z in range(n_z)
            ]
            outs[k][:, s * LANES : (s + 1) * LANES] = jnp.concatenate(blocks_of, axis=0).astype(BF16)


def swapped_rows(values):
    row = lax.broadcasted_iota(jnp.int32, values[0].shape, 0)
    for d in (4, 2, 1):
        lower = (row & d) == 0
        out = list(values)
        for i in range(8):
            if i & d == 0:
                a, b = values[i], values[i + d]
                out[i] = jnp.where(lower, a, pltpu.roll(b, d, 0))
                out[i + d] = jnp.where(lower, pltpu.roll(a, 8 - d, 0), b)
        values = out
    return values


def line_rows(chunks, per, blocks, quads, total_blocks, taps, turn, last, rows, sums, spun):
    band = blocks * quads
    pulses = len(chunks) * per
    ky = []
    for t in range(0, band, 16):
        groups = []
        for c in range(2):
            tiles = [
                chunk[c * band + t : c * band + t + 16, p * LANES : (p + 1) * LANES].astype(F32)
                for chunk in chunks
                for p in range(per)
            ]
            groups.append(
                swapped_rows([v[:8] for v in tiles]) + swapped_rows([v[8:] for v in tiles])
            )
        for b in range(16 // quads):
            lhs = jnp.concatenate(
                [
                    jnp.concatenate([g[b * quads + q] for g in groups], axis=0).astype(BF16)
                    for q in range(quads)
                ],
                axis=1,
            )
            line = dot(lhs, taps[t // quads + b])
            ky.append((line[:pulses], line[pulses:]))
    quarter = total_blocks // 4
    for y in range(quarter):
        classes = []
        for m in range(4):
            acc = None
            for b in range(m, blocks, 4):
                re, im = ky[b]
                angle = 2.0 * math.pi * (b * y % total_blocks) / total_blocks
                co, si = math.cos(angle), math.sin(angle)
                if b * y == 0:
                    term = (re, im)
                else:
                    term = (re * co - im * si, re * si + im * co)
                acc = term if acc is None else (acc[0] + term[0], acc[1] + term[1])
            classes.append(acc)
        for r, (re, im) in enumerate(fourier(classes, 1)):
            at = (y + r * quarter) * pulses
            sums[0, at : at + pulses, :] = re
            sums[1, at : at + pulses, :] = im
    for y in range(0, total_blocks, 16):
        parts = []
        for c in range(2):
            halves = [
                swapped_rows([sums[c, u * pulses : (u + 1) * pulses, :] for u in range(h, h + 8)])
                for h in (y, y + 8)
            ]
            parts.append([jnp.concatenate(pair, axis=0) for pair in zip(*halves)])
        for f in range(LANES // total_blocks):
            at = slice(f * total_blocks + y, f * total_blocks + y + 16)
            tc, ts = turn[0, at, :], turn[1, at, :]
            for i in range(pulses):
                re, im = parts[0][i], parts[1][i]
                spun[i, at, :LANES] = (re * tc - im * ts).astype(BF16)
                spun[i, at, LANES:] = (re * ts + im * tc).astype(BF16)
    tops = last.shape[0] // 2
    for m in range(pulses):
        done = dot(last[...], spun[m], NT)
        for c in range(2):
            at = (c * pulses + m) * tops
            rows[at : at + tops, :] = done[c * tops : (c + 1) * tops, :]


def line_head_kernel(dims, one, two, taps, turn, last, rows, sums, spun):
    line_rows((one, two), *dims, taps, turn, last, rows, sums, spun)


def line_tail_kernel(n_z, dims, head, tail, *refs):
    chunks, refs = refs[: len(tail)], refs[len(tail) :]
    taps, turn, last, early = refs[:4]
    outs = refs[4 : 4 + n_z]
    sums, spun, rows = refs[4 + n_z :]
    line_rows(chunks, *dims, taps, turn, last, rows, sums, spun)
    my_z = lax.axis_index("pulse")
    per = dims[0]
    tops = last.shape[0] // 2
    half, pulses = len(tail) * per, n_z * per
    share = tops // n_z
    for k in range(n_z):
        for s in range(0, share, 8):
            for c in range(2):
                groups = []
                for g in range(0, pulses, 8):
                    tiles = []
                    for z, p in (divmod(m, per) for m in range(g, g + 8)):
                        source, place = (early, head) if z ^ k in head else (rows, tail)
                        at = (c * half + place.index(z ^ k) * per + p) * tops + s
                        at = pl.multiple_of(at + (my_z ^ k) * share, 8)
                        tiles.append(source[pl.ds(at, 8), :])
                    groups.append(swapped_rows(tiles))
                for i in range(8):
                    outs[k][
                        c * pulses : (c + 1) * pulses, (s + i) * LANES : (s + i + 1) * LANES
                    ] = jnp.concatenate([g[i] for g in groups], axis=0).astype(BF16)


def fold_kernel(n_z, n_c, *refs):
    parts, outs, total = refs[:n_z], refs[n_z:-1], refs[-1]
    acc = parts[0][...].astype(F32)
    for part in parts[1:]:
        acc = acc + part[...].astype(F32)
    total[...] = acc.astype(BF16)
    mine = lax.axis_index("range") * n_c + lax.axis_index("sub")
    wide = outs[0].shape[1]
    for k, out in enumerate(outs):
        out[...] = total[:, pl.ds(pl.multiple_of((mine ^ k) * wide, wide), wide)]


def column_kernel(width, tile_cols, taps, table, turn, out, mixed, spread):
    pulses = taps.shape[0]
    low = mixed.shape[0]
    high = out.shape[0] // low
    steps = width // high
    step = 16
    for v in range(high // LANES):
        for r in range(0, pulses, step):
            tile = taps[r : r + step, width:].astype(F32)
            inside = [tile == float(t) for t in range(tile_cols)]
            values = []
            for t in range(tile_cols):
                for i in range(steps):
                    at = i * high + v * LANES
                    value = taps[r : r + step, at : at + LANES].astype(F32)
                    values.append((jnp.where(inside[t], value, 0.0), None))
            left, right = slice(v * LANES, (v + 1) * LANES), slice(high + v * LANES, high + (v + 1) * LANES)
            for d, (re, im) in enumerate(fourier(values, 1)):
                tc, ts = turn[0, d : d + 1, left], turn[1, d : d + 1, left]
                if im is None:
                    re, im = re * tc, re * ts
                else:
                    re, im = re * tc - im * ts, re * ts + im * tc
                mixed[d, r : r + step, left] = re.astype(BF16)
                mixed[d, r : r + step, right] = (-im).astype(BF16)
                mixed[d, pulses + r : pulses + r + step, left] = im.astype(BF16)
                mixed[d, pulses + r : pulses + r + step, right] = re.astype(BF16)
    for d in range(0, low, 2):
        both = jnp.concatenate([mixed[d], mixed[d + 1]], axis=0)
        done = dot(table[...], both, NT)
        spread[pl.ds(d, high, stride=low), :] = done[:, : 2 * pulses]
        spread[pl.ds(d + 1, high, stride=low), :] = done[:, 2 * pulses :]
    out[...] = spread[...].astype(BF16)


def turned(count):
    order, k = [0], count // 2
    while k > 0:
        order, k = order + [o ^ k for o in order], k // 2
    return order


def factor(parts, n_z, n_x, n_c, per):
    pulses = n_z * per
    out = []
    for comp in range(2):
        for c in turned(n_c):
            for z in turned(n_z):
                for x in range(n_x):
                    at = comp * pulses + z * per
                    out.append(parts[x * n_c + c][at : at + per, :])
    return jnp.concatenate(out, axis=0)


def image_kernel(dims, step, *refs):
    n_z, n_x, n_c, per = dims
    count = n_x * n_c
    parts = [ref[...].astype(F32) for ref in refs[:count]]
    cols, out, held, sent = refs[count:]
    lines = factor(parts, n_z, n_x, n_c, per).T
    half = lines.shape[1] // 2
    re, im = lines[:, :half], lines[:, half:]
    rows = lines.shape[0]
    lhs = jnp.concatenate(
        [jnp.concatenate([re, -im], axis=1), jnp.concatenate([im, re], axis=1)], axis=0
    ).astype(BF16)
    copies = []
    for i in range(cols.shape[0] // step):
        done = dot(lhs, cols[i * step : (i + 1) * step, :], NT)
        at = pl.ds(i * step, step)
        held[0, :, at] = done[:rows]
        held[1, :, at] = done[rows:]
        copies.append(pltpu.make_async_copy(held.at[:, :, at], out.at[:, :, at], sent.at[i]))
        copies[-1].start()
    for copy in copies:
        copy.wait()


def image_plain(lhs, cols, out):
    rows = out.shape[1]
    done = dot(lhs[...], cols[...], NT)
    out[0] = done[:rows]
    out[1] = done[rows:]


def table_of(values, dtype=BF16):
    return jnp.asarray(np.asarray(values, np.float32), dtype)


def complex_left(c, s, scale=1.0):
    return np.block([[c, -s], [s, c]]) * scale


def program(raw_echo, range_taps, azim_taps, tile_col):
    n_x, n_z, n_c = lax.axis_size("range"), lax.axis_size("pulse"), lax.axis_size("sub")
    my_x, my_c = lax.axis_index("range"), lax.axis_index("sub")
    shard, part = raw_echo.shape[1:]
    per = shard // n_x
    samples = part * n_x
    blocks, block_bins, block_rows = range_taps.shape
    total_blocks = blocks * n_z
    grid = total_blocks * block_rows
    width = azim_taps.shape[1]
    tile_cols = grid // width
    quad = n_x * n_c
    out_rows = grid // (n_z * quad)
    pulses = n_z * per
    wide = out_rows % LANES == 0
    room = {}
    if wide:
        room = {"compiler_params": pltpu.CompilerParams(vmem_limit_bytes=24 << 20)}

    high = samples // LANES
    tiles = high // n_x
    n128 = np.arange(LANES)
    nh = np.arange(high)
    first = complex_left(*phasor(nh, nh, high, -1.0)).reshape(2 * high, 2, n_x, tiles)
    first = [first[:, :, [x ^ k for k in range(n_x)]].transpose(2, 0, 1, 3) for x in range(n_x)]
    first = table_of(np.stack(first).reshape(n_x, n_x, 2 * high, 2 * tiles))
    turn1 = table_of(np.stack(phasor(nh, n128, samples, -1.0)), F32)
    second = table_of(complex_left(*phasor(n128, n128, LANES, -1.0), 1.0 / math.sqrt(samples)))
    tops = grid // LANES
    shift = grid // n_z
    turn2 = np.stack([np.stack(phasor(n128, n128 + shift * z, grid, 1.0)) for z in range(n_z)])
    turn2 = table_of(turn2, F32)
    c, s = phasor(np.arange(tops), n128, tops, 1.0)
    last = table_of(complex_left(c, s, 1.0 / math.sqrt(grid)))
    low = 16
    tall = grid // low
    nt = np.arange(tall)
    c, s = phasor(nt, nt, tall, 1.0)
    table = table_of(np.concatenate([c, s], axis=1) / math.sqrt(grid))
    turn3 = table_of(np.stack(phasor(np.arange(low), nt, grid, 1.0)), F32)

    piece = pltpu.VMEM((2 * tiles, per * LANES), BF16)
    *pieces, marked = pl.pallas_call(
        functools.partial(split_kernel, n_x, per),
        in_specs=[HELD] * 3,
        out_specs=[VMEM] * (n_x + 1),
        out_shape=[piece] * n_x + [pltpu.VMEM((shard, width + LANES), BF16)],
        scratch_shapes=[
            pltpu.VMEM(raw_echo.shape, BF16),
            pltpu.VMEM(azim_taps.shape, BF16),
            pltpu.SMEM((1, shard), jnp.int32),
            pltpu.VMEM((2, tiles * shard, LANES), F32),
            pltpu.SemaphoreType.DMA((4,)),
        ],
        name="split",
        **room,
    )(*far(raw_echo, azim_taps, tile_col.T))
    parts = []
    for k in range(1, n_x):
        parts.append(traded(pieces[k], "range", k))

    everyone = marked
    for axis, count in (("pulse", n_z), ("sub", n_c)):
        k = count // 2
        while k > 0:
            everyone = jnp.concatenate([everyone, traded(everyone, axis, k)], axis=0)
            k //= 2

    fixed = (turn1, second)
    part1, rest, turn1, second = pl.pallas_call(
        functools.partial(ready_kernel, len(fixed)),
        in_specs=[VMEM] + [HELD] * (1 + len(fixed)),
        out_specs=[VMEM] * (2 + len(fixed)),
        out_shape=[
            pltpu.VMEM((2 * high, per * LANES), F32),
            pltpu.VMEM((max(n_x - 1, 1), 2 * high, 2 * tiles), BF16),
        ]
        + [pltpu.VMEM(f.shape, f.dtype) for f in fixed],
        scratch_shapes=[
            pltpu.VMEM((2 * high, 2 * tiles), BF16),
            pltpu.SemaphoreType.DMA((2 + len(fixed),)),
        ],
        name="ready",
        **room,
    )(*near(pieces[0]), *far(first, *fixed))
    fixed = (last, range_taps, table, turn3)
    turn2, last, range_taps, table, turn3 = pl.pallas_call(
        functools.partial(bring_kernel, len(fixed)),
        in_specs=[HELD] * (1 + len(fixed)),
        out_specs=[VMEM] * (1 + len(fixed)),
        out_shape=[pltpu.VMEM(turn2.shape[1:], F32)]
        + [pltpu.VMEM(f.shape, f.dtype) for f in fixed],
        scratch_shapes=[pltpu.SemaphoreType.DMA((1 + len(fixed),))],
        name="bring",
        **room,
    )(*far(turn2, *fixed))

    band = LANES // n_z
    chunk = pltpu.VMEM((2 * band, per * high), BF16)
    chunks = pl.pallas_call(
        functools.partial(pulse_kernel, n_x, n_z, per),
        in_specs=[VMEM] * (n_x + 3),
        out_specs=[VMEM] * n_z,
        out_shape=[chunk] * n_z,
        name="pulse_transform",
        **room,
    )(*near(*parts, part1, rest, turn1, second))
    moved = [chunks[0]]
    for k in range(1, n_z):
        moved.append(traded(chunks[k], "pulse", k))

    group = 64
    all_pulses = n_c * n_z * shard
    cuts = all_pulses // group
    scratch = [
        pltpu.VMEM((low, 2 * group, 2 * tall), BF16),
        pltpu.VMEM((grid, 2 * group), F32),
    ]
    make = functools.partial(column_kernel, width, tile_cols)
    if cuts == 1:
        cols = pl.pallas_call(
            make,
            in_specs=[VMEM] * 3,
            out_specs=VMEM,
            out_shape=pltpu.VMEM((grid, 2 * group), BF16),
            scratch_shapes=scratch,
            name="column_transform",
            **room,
        )(*near(everyone, table, turn3))
    else:
        cols = pl.pallas_call(
            make,
            grid=(cuts,),
            in_specs=[
                pl.BlockSpec((group, width + LANES), lambda i: (i, 0)),
                pl.BlockSpec((tall, 2 * tall), lambda i: (0, 0)),
                pl.BlockSpec((2, low, tall), lambda i: (0, 0, 0)),
            ],
            out_specs=pl.BlockSpec((grid, 2 * group), lambda i: (0, i)),
            out_shape=jax.ShapeDtypeStruct((grid, 2 * all_pulses), BF16),
            scratch_shapes=scratch,
            name="column_transform",
        )(everyone, table, turn3)

    quads = block_bins // LANES
    paired = n_z == 4 and per == 4 and blocks >= 4 and blocks * quads % 16 == 0 and tops % 32 == 0
    out_lines = [pltpu.VMEM((2 * pulses, grid // n_z), BF16)] * n_z
    if paired:
        head, tail = (0, 2), (1, 3)
        dims = (per, blocks, quads, total_blocks)
        early = pltpu.VMEM((pulses * tops, LANES), F32)
        scratch = [
            pltpu.VMEM((2, total_blocks * pulses // 2, LANES), F32),
            pltpu.VMEM((pulses // 2, LANES, 2 * LANES), BF16),
        ]
        early_rows = pl.pallas_call(
            functools.partial(line_head_kernel, dims),
            in_specs=[VMEM] * 5,
            out_specs=VMEM,
            out_shape=early,
            scratch_shapes=scratch,
            name="line_head",
            **room,
        )(*near(*(moved[k] for k in head), range_taps, turn2, last))
        lines = pl.pallas_call(
            functools.partial(line_tail_kernel, n_z, dims, head, tail),
            in_specs=[VMEM] * 6,
            out_specs=[VMEM] * n_z,
            out_shape=out_lines,
            scratch_shapes=scratch + [early],
            name="line_tail",
            **room,
        )(*near(*(moved[k] for k in tail), range_taps, turn2, last, early_rows))
    else:
        lines = pl.pallas_call(
            functools.partial(line_plain, n_z, per, blocks, quads, total_blocks),
            in_specs=[VMEM] * (n_z + 3),
            out_specs=[VMEM] * n_z,
            out_shape=out_lines,
            scratch_shapes=[
                pltpu.VMEM((2 * pulses * blocks * quads, LANES), F32),
                pltpu.VMEM((2, total_blocks * pulses, LANES), F32),
                pltpu.VMEM((2 * pulses * tops, LANES), F32),
            ],
            name="line_transform",
            **room,
        )(*near(*moved, range_taps, turn2, last))
    moved = [lines[0]]
    for k in range(1, n_z):
        moved.append(traded(lines[k], "pulse", k))
    if wide:
        pieces = pl.pallas_call(
            functools.partial(fold_kernel, n_z, n_c),
            in_specs=[VMEM] * n_z,
            out_specs=[VMEM] * quad,
            out_shape=[pltpu.VMEM((2 * pulses, out_rows), BF16)] * quad,
            scratch_shapes=[pltpu.VMEM((2 * pulses, grid // n_z), BF16)],
            name="fold",
            **room,
        )(*near(*moved))
    else:
        acc = sum(m.astype(F32) for m in moved).astype(BF16)
        mine = my_x * n_c + my_c
        pieces = [
            lax.dynamic_slice_in_dim(acc, (mine ^ k) * out_rows, out_rows, 1)
            for k in range(quad)
        ]
    parts = [pieces[0]]
    for k in range(1, quad):
        parts.append(traded(pieces[k], ("range", "sub"), k))

    wide_x = 256
    depth = 2 * all_pulses
    out_shape = jax.ShapeDtypeStruct((2, out_rows, grid), F32)
    if cuts == 1 and wide:
        return pl.pallas_call(
            functools.partial(image_kernel, (n_z, n_x, n_c, per), wide_x),
            in_specs=[VMEM] * (quad + 1),
            out_specs=HELD,
            out_shape=out_shape,
            scratch_shapes=[
                pltpu.VMEM((2, out_rows, grid), F32),
                pltpu.SemaphoreType.DMA((grid // wide_x,)),
            ],
            name="image",
            **room,
        )(*near(*parts, cols))
    lines = factor([p.astype(F32) for p in parts], n_z, n_x, n_c, per).T
    re = lines[:, :all_pulses].reshape(out_rows, cuts, 1, group)
    im = lines[:, all_pulses:].reshape(out_rows, cuts, 1, group)
    lhs = jnp.stack(
        [jnp.concatenate([re, -im], axis=2), jnp.concatenate([im, re], axis=2)]
    ).reshape(2 * out_rows, depth).astype(BF16)
    return pl.pallas_call(
        image_plain,
        grid=(grid // wide_x,),
        in_specs=[
            pl.BlockSpec(lhs.shape, lambda i: (0, 0)),
            pl.BlockSpec((wide_x, depth), lambda i: (i, 0)),
        ],
        out_specs=pl.BlockSpec((2, out_rows, wide_x), lambda i: (0, 0, i)),
        out_shape=out_shape,
        name="image",
    )(lhs, cols)


def solution(mesh):
    placed = (
        P(None, ("groups", "pulse", "sub"), "range"),
        P("pulse", None, None),
        P(("groups", "pulse", "sub"), None),
        P(("groups", "pulse", "sub"), None),
    )
    return jax.shard_map(
        program,
        mesh=mesh,
        in_specs=placed,
        out_specs=P(None, ("groups", "pulse", "range", "sub"), None),
        check_vma=False,
    )
```
